256 devices in a mesh: dp: 8 (over y, z_lo), owner: 32 (over x, z_hi, core).
Axes of the slice: x: 4, y: 4, z: 8 (z_hi: 4, z_lo: 2; z = z_hi * 2 + z_lo), core: 2. Of those that a mesh axis runs over, the one named last changes fastest.
Arguments:
- partials: bfloat16 [256, 96, 128, 128], P(('dp', 'owner')), may hold values from -1.75 to 1.75
- owners: int32 [96], replicated, may hold values from 0 to 31, as said below
- step_count: int32 [1], replicated, may hold values from 1 to 49
- master: float32 [192, 128, 128], P('owner'), may hold values from -0.3125 to 0.3125
- moment: float32 [192, 128, 128], P('owner'), may hold values from -4 to 4
- second: float32 [192, 128, 128], P('owner'), may hold values from 0.1 to 10
- stat_left: float32 [192, 128, 128], P('owner'), may hold values from -1.5 to 82
- stat_right: float32 [192, 128, 128], P('owner'), may hold values from -1.5 to 82
- basis_left: float32 [192, 128, 128], P('owner'), may hold values from -0.12 to 1.12
- basis_right: float32 [192, 128, 128], P('owner'), may hold values from -0.12 to 1.12
Outputs:
- weights_all: bfloat16 [96, 128, 128], replicated
- direction: float32 [192, 128, 128], P('owner')
- left_new: float32 [192, 128, 128], P('owner')
- right_new: float32 [192, 128, 128], P('owner')
The draws below stay inside these ranges and needn't reach their ends.
Inputs may be any that keep to these rules, and one draw needn't show every extreme that they name: `owners`: each owner index is named by at least one and at most 6 blocks, and some index by exactly 6.
All inputs are finite; a program needn't handle non-finite values.
Results may differ from the reference program's by a relative error of at most 0.0065.
Values may be sent and summed in bfloat16 or wider, within the bound.
A program may use at most 128 MiB of HBM per device.

```python
import math
import jax
import jax.numpy as jnp
from jax import lax

B = 128
OWNER_SLOTS = 6
NS_ITERS = 6
TOTAL_SLOTS = 192
BLOCKS = 96
SOURCES = 256
N_OWNER = 32


def statistic(key, salt):
    key_noise, key_diag = jax.random.split(jax.random.fold_in(key, salt))
    total_slot_count = OWNER_SLOTS * N_OWNER
    jitter = jax.random.uniform(key_noise, (total_slot_count, B, B), jnp.float32, -1.0, 1.0)
    diagonal = jnp.exp(jax.random.uniform(key_diag, (total_slot_count, B), jnp.float32, math.log(4.0), math.log(40.0)))
    symmetric = 0.5 * (jitter + jnp.swapaxes(jitter, 1, 2))
    return symmetric + diagonal[:, :, None] * jnp.eye(B, dtype=jnp.float32)[None, :, :]


def near_identity(key, salt):
    key_noise = jax.random.fold_in(key, salt)
    total_slot_count = OWNER_SLOTS * N_OWNER
    jitter = jax.random.uniform(key_noise, (total_slot_count, B, B), jnp.float32, -0.06, 0.06)
    return jitter + jnp.eye(B, dtype=jnp.float32)[None, :, :]


def draw_stat_left(key, part):
    return statistic(key, 3)


def draw_stat_right(key, part):
    return statistic(key, 5)


def draw_basis_left(key, part):
    return near_identity(key, 7)


def draw_basis_right(key, part):
    return near_identity(key, 9)


def draw_owners(key, part):
    key_order, key_first, key_shuffle = jax.random.split(jax.random.fold_in(key, 11), 3)
    total_slot_count = N_OWNER * OWNER_SLOTS
    owner_scores = jax.random.permutation(key_order, total_slot_count).astype(jnp.int32)
    busiest_owner = jax.random.randint(key_first, (), 0, N_OWNER)
    slot_position = jnp.arange(total_slot_count, dtype=jnp.int32)
    extra_credit = jnp.where(slot_position // OWNER_SLOTS == busiest_owner, 2 * total_slot_count, jnp.where(slot_position % OWNER_SLOTS == 0, total_slot_count, 0))
    owner_scores = owner_scores + extra_credit.astype(jnp.int32)
    chosen = jnp.argsort(-owner_scores)[:OWNER_SLOTS * N_OWNER // 2]
    chosen = jax.random.permutation(key_shuffle, chosen)
    return (chosen // OWNER_SLOTS).astype(jnp.int32)


def strengthened(values, own_key, source, target, shards_of, factor):
    owner, partner = [(jnp.arange(values.shape[position]) // (values.shape[position] // shards_of)).reshape([-1 if axis == position else 1 for axis in range(values.ndim)]) for position in (source, target)]
    chosen = jax.random.permutation(own_key, shards_of)[partner]
    strong = (owner == chosen) | (owner == (partner + shards_of // 2) % shards_of)
    return jnp.where(strong, factor * values, values)


def level_of(key, shape, shards, smallest, largest):
    gain = 1.0
    for axis_at, parts in shards:
        draws = jax.random.uniform(jax.random.fold_in(jax.random.fold_in(key, 6), axis_at), (parts,), jnp.float32, smallest / len(shards), largest / len(shards))
        gain = gain * jnp.repeat(jnp.exp(draws), shape[axis_at] // parts).reshape((-1,) + (1,) * (len(shape) - 1 - axis_at))
    return gain


def gaussian(key, dims, scale, most, cuts=(), held_as=jnp.bfloat16):
    entries = scale * jax.random.normal(key, dims, jnp.float32)
    if cuts:
        entries = entries * level_of(key, dims, cuts, -0.22, 0.18)
    return jnp.clip(entries, -most, most).astype(held_as)


def bell_draw_with(key, extent, spread, most, cuts, heavy, kind=jnp.bfloat16):
    result = spread * jax.random.normal(key, extent, jnp.float32)
    if cuts:
        result = result * level_of(key, extent, cuts, -0.22, 0.18)
    return jnp.clip(strengthened(result, jax.random.fold_in(key, 3), *heavy), -most, most).astype(kind)


def setup_inputs(seed: int = 0) -> dict:
    key_of = jax.random.split(jax.random.key(seed), 11)
    return {
        "partials": bell_draw_with(key_of[0], (SOURCES, BLOCKS, B, B), 0.0625, 1.75, ((0, 256),), (0, 1, 32, 2.75)),
        "owners": draw_owners(jax.random.fold_in(key_of[10], 71), 0),
        "step_count": jax.random.randint(key_of[2], (1,), 1, 50).astype(jnp.int32),
        "master": gaussian(key_of[3], (TOTAL_SLOTS, B, B), 0.02, 0.3125, ((0, 32),), jnp.float32),
        "moment": gaussian(key_of[4], (TOTAL_SLOTS, B, B), 0.3, 4.0, ((0, 32),), jnp.float32),
        "second": jnp.clip(jnp.exp(math.log(10.0) - 4.6051702 * jax.random.uniform(key_of[5], (TOTAL_SLOTS, B, B), jnp.float32) ** level_of(key_of[5], (TOTAL_SLOTS, B, B), ((0, 32),), -0.2, 0.2)), 0.1, 10.0),
        "stat_left": draw_stat_left(jax.random.fold_in(key_of[10], 71), 0),
        "stat_right": draw_stat_right(jax.random.fold_in(key_of[10], 71), 0),
        "basis_left": draw_basis_left(jax.random.fold_in(key_of[10], 71), 0),
        "basis_right": draw_basis_right(jax.random.fold_in(key_of[10], 71), 0),
    }


def product(left, right):
    return jnp.matmul(left, right, precision=lax.Precision.HIGHEST)

def transposed(array):
    return jnp.swapaxes(array, 1, 2)

def refresh(stat, basis):
    power = product(stat, basis)
    magnitude = jnp.sqrt(lax.optimization_barrier(jnp.sum(power * power, axis=(1, 2), keepdims=True)))
    iterate = power / (magnitude + 1e-06)
    for repeat_count in range(NS_ITERS):
        iterate = 1.5 * iterate - 0.5 * product(iterate, product(transposed(iterate), iterate))
    return iterate

def slot_layout(owners, slot_count, total_slot_count):
    block_count = owners.shape[0]
    slot_position = jnp.arange(block_count, dtype=jnp.int32)
    before = (owners[:, None] == owners[None, :]) & (slot_position[:, None] > slot_position[None, :])
    rank_in = lax.optimization_barrier(jnp.sum(before.astype(jnp.int32), axis=1))
    target = owners * slot_count + rank_in
    matches = (target[:, None] == jnp.arange(total_slot_count, dtype=jnp.int32)[None, :]).astype(jnp.int32)
    source = lax.optimization_barrier(jnp.sum(matches * slot_position[:, None], axis=0))
    occupied = lax.optimization_barrier(jnp.sum(matches, axis=0))
    return (target, source, occupied)

def soap_update(gradient, occupied, moment, second, stat_left, stat_right, basis_left, basis_right, step_count):
    elapsed = step_count[0].astype(jnp.float32)
    moment_new = 0.95 * moment + 0.05 * gradient
    rotated = product(transposed(basis_left), product(gradient, basis_right))
    rot_moment = product(transposed(basis_left), product(moment_new, basis_right))
    second_new = 0.95 * second + 0.05 * rotated * rotated
    correction = 1.0 - jnp.power(jnp.float32(0.95), elapsed)
    scaled = rot_moment / correction / (jnp.sqrt(second_new / correction) + 1e-08)
    occupied_mask = (occupied > 0)[:, None, None]
    direction = jnp.where(occupied_mask, product(basis_left, product(scaled, transposed(basis_right))), 0.0)
    left_stat = 0.95 * stat_left + 0.05 * product(gradient, transposed(gradient))
    right_stat = 0.95 * stat_right + 0.05 * product(transposed(gradient), gradient)
    left_new = jnp.where(occupied_mask, refresh(left_stat, basis_left), basis_left)
    right_new = jnp.where(occupied_mask, refresh(right_stat, basis_right), basis_right)
    return (direction, left_new, right_new)

def reference(partials, owners, step_count, master, moment, second, stat_left, stat_right, basis_left, basis_right):
    total_slot_count = OWNER_SLOTS * N_OWNER

    def accumulate(running, piece):
        return (running + piece.astype(jnp.float32), None)
    grad_sum = lax.scan(accumulate, jnp.zeros(partials.shape[1:], jnp.float32), partials)[0]
    target, source, occupied = slot_layout(owners, OWNER_SLOTS, total_slot_count)
    gradient = jnp.take(grad_sum, source, axis=0) * (occupied > 0).astype(jnp.float32)[:, None, None]
    direction, left_new, right_new = soap_update(gradient, occupied, moment, second, stat_left, stat_right, basis_left, basis_right, step_count)
    updated = (master - 0.01 * (direction + 0.1 * master)).astype(jnp.bfloat16)
    weights_all = jnp.take(updated, target, axis=0)
    return (weights_all, direction, left_new, right_new)
```

```python
import functools

import jax
import jax.numpy as jnp
from jax import lax
from jax.experimental import pallas as pl
from jax.experimental.pallas import tpu as pltpu
from jax.sharding import PartitionSpec as P

MESH = pl.DeviceIdType.MESH

NS_ITERS = 6


def product(left, right):
    return jnp.matmul(left, right, precision=lax.Precision.HIGHEST)


def transposed(array):
    return jnp.swapaxes(array, 1, 2)


def refresh(stat, basis):
    power = product(stat, basis)
    magnitude = jnp.sqrt(jnp.sum(power * power, axis=(1, 2), keepdims=True))
    iterate = power / (magnitude + 1e-06)
    for repeat_count in range(NS_ITERS):
        iterate = 1.5 * iterate - 0.5 * product(iterate, product(transposed(iterate), iterate))
    return iterate


def slot_layout(owners, slot_count, total_slot_count):
    block_count = owners.shape[0]
    slot_position = jnp.arange(block_count, dtype=jnp.int32)
    before = (owners[:, None] == owners[None, :]) & (
        slot_position[:, None] > slot_position[None, :]
    )
    rank_in = jnp.sum(before.astype(jnp.int32), axis=1)
    target = owners * slot_count + rank_in
    matches = (target[:, None] == jnp.arange(total_slot_count, dtype=jnp.int32)[None, :]).astype(
        jnp.int32
    )
    source = jnp.sum(matches * slot_position[:, None], axis=0)
    occupied = jnp.sum(matches, axis=0)
    return (target, source, occupied)


def soap_update(
    gradient, occupied, moment, second, stat_left, stat_right, basis_left, basis_right, step_count
):
    elapsed = step_count[0].astype(jnp.float32)
    moment_new = 0.95 * moment + 0.05 * gradient
    rotated = product(transposed(basis_left), product(gradient, basis_right))
    rot_moment = product(transposed(basis_left), product(moment_new, basis_right))
    second_new = 0.95 * second + 0.05 * rotated * rotated
    correction = 1.0 - jnp.power(jnp.float32(0.95), elapsed)
    scaled = rot_moment / correction / (jnp.sqrt(second_new / correction) + 1e-08)
    occupied_mask = (occupied > 0)[:, None, None]
    direction = jnp.where(
        occupied_mask, product(basis_left, product(scaled, transposed(basis_right))), 0.0
    )
    left_stat = 0.95 * stat_left + 0.05 * product(gradient, transposed(gradient))
    right_stat = 0.95 * stat_right + 0.05 * product(transposed(gradient), gradient)
    left_new = jnp.where(occupied_mask, refresh(left_stat, basis_left), basis_left)
    right_new = jnp.where(occupied_mask, refresh(right_stat, basis_right), basis_right)
    return (direction, left_new, right_new)


def gather_kernel(n, group, x_ref, o_ref, send_sem, recv_sem):
    me, peer = group()
    barrier = pltpu.get_barrier_semaphore()
    for k in range(1, n):
        pl.semaphore_signal(barrier, inc=1, device_id=peer(lax.rem(me + k, n)), device_id_type=MESH)
    pl.semaphore_wait(barrier, n - 1)
    copies = []
    for k in range(1, n):
        copy = pltpu.make_async_remote_copy(
            src_ref=x_ref,
            dst_ref=o_ref.at[me],
            send_sem=send_sem.at[k],
            recv_sem=recv_sem.at[k],
            device_id=peer(lax.rem(me + k, n)),
            device_id_type=MESH,
        )
        copy.start()
        copies.append(copy)
    o_ref[me] = x_ref[...]
    for copy in copies:
        copy.wait()


def dp_group():
    me = lax.axis_index("dp")
    owner = lax.axis_index("owner")
    return me, lambda j: (j, owner)


def gather_group(x, n, group, collective_id):
    return pl.pallas_call(
        functools.partial(gather_kernel, n, group),
        out_shape=jax.ShapeDtypeStruct((n,) + x.shape, x.dtype),
        in_specs=[pl.BlockSpec(memory_space=pltpu.VMEM)],
        out_specs=pl.BlockSpec(memory_space=pltpu.VMEM),
        scratch_shapes=[pltpu.SemaphoreType.DMA((n,)), pltpu.SemaphoreType.DMA((n,))],
        compiler_params=pltpu.CompilerParams(collective_id=collective_id, has_side_effects=True),
    )(x)


def body(
    partials,
    owners,
    step_count,
    master,
    moment,
    second,
    stat_left,
    stat_right,
    basis_left,
    basis_right,
):
    owner_count = lax.axis_size("owner")
    slot_count = master.shape[0]
    total_slot_count = slot_count * owner_count
    target, source, occupied = slot_layout(owners, slot_count, total_slot_count)
    first_slot = lax.axis_index("owner") * slot_count
    occupied_mine = lax.dynamic_slice_in_dim(occupied, first_slot, slot_count, 0)
    own_part = partials[0]
    mask_all = (occupied > 0).astype(jnp.float32)[:, None, None]
    placed = jnp.take(own_part, source, axis=0).astype(jnp.float32) * mask_all
    summed = lax.psum_scatter(placed.astype(jnp.bfloat16), "owner", scatter_dimension=0, tiled=True)
    replicas = gather_group(summed, lax.axis_size("dp"), dp_group, 0)
    gradient = jnp.sum(replicas.astype(jnp.float32), axis=0)
    direction, left_new, right_new = soap_update(
        gradient,
        occupied_mine,
        moment,
        second,
        stat_left,
        stat_right,
        basis_left,
        basis_right,
        step_count,
    )
    updated = (master - 0.01 * (direction + 0.1 * master)).astype(jnp.bfloat16)
    every_slot = lax.all_gather(updated, "owner", axis=0, tiled=True)
    weights_all = jnp.take(every_slot, target, axis=0)
    return (weights_all, direction, left_new, right_new)


def solution(mesh):
    placed = (
        P(("dp", "owner"), None, None, None),
        P(),
        P(),
        P("owner", None, None),
        P("owner", None, None),
        P("owner", None, None),
        P("owner", None, None),
        P("owner", None, None),
        P("owner", None, None),
        P("owner", None, None),
    )
    return jax.shard_map(
        body,
        mesh=mesh,
        in_specs=placed,
        out_specs=(P(), P("owner", None, None), P("owner", None, None), P("owner", None, None)),
        check_vma=False,
    )
```

```python
import functools

import jax
import jax.numpy as jnp
from jax import lax
from jax.experimental import pallas as pl
from jax.experimental.pallas import tpu as pltpu
from jax.sharding import PartitionSpec as P

MESH = pl.DeviceIdType.MESH

NS_ITERS = 6


def product(left, right):
    return jnp.matmul(left, right, precision=lax.Precision.HIGHEST)


def transposed(array):
    return jnp.swapaxes(array, 1, 2)


def refresh(stat, basis):
    power = product(stat, basis)
    magnitude = jnp.sqrt(jnp.sum(power * power, axis=(1, 2), keepdims=True))
    iterate = power / (magnitude + 1e-06)
    for repeat_count in range(NS_ITERS):
        iterate = 1.5 * iterate - 0.5 * product(iterate, product(transposed(iterate), iterate))
    return iterate


def slot_layout(owners, slot_count, total_slot_count):
    block_count = owners.shape[0]
    slot_position = jnp.arange(block_count, dtype=jnp.int32)
    before = (owners[:, None] == owners[None, :]) & (
        slot_position[:, None] > slot_position[None, :]
    )
    rank_in = jnp.sum(before.astype(jnp.int32), axis=1)
    target = owners * slot_count + rank_in
    matches = (target[:, None] == jnp.arange(total_slot_count, dtype=jnp.int32)[None, :]).astype(
        jnp.int32
    )
    source = jnp.sum(matches * slot_position[:, None], axis=0)
    occupied = jnp.sum(matches, axis=0)
    return (target, source, occupied)


def soap_update(
    gradient, occupied, moment, second, stat_left, stat_right, basis_left, basis_right, step_count
):
    elapsed = step_count[0].astype(jnp.float32)
    moment_new = 0.95 * moment + 0.05 * gradient
    rotated = product(transposed(basis_left), product(gradient, basis_right))
    rot_moment = product(transposed(basis_left), product(moment_new, basis_right))
    second_new = 0.95 * second + 0.05 * rotated * rotated
    correction = 1.0 - jnp.power(jnp.float32(0.95), elapsed)
    scaled = rot_moment / correction / (jnp.sqrt(second_new / correction) + 1e-08)
    occupied_mask = (occupied > 0)[:, None, None]
    direction = jnp.where(
        occupied_mask, product(basis_left, product(scaled, transposed(basis_right))), 0.0
    )
    left_stat = 0.95 * stat_left + 0.05 * product(gradient, transposed(gradient))
    right_stat = 0.95 * stat_right + 0.05 * product(transposed(gradient), gradient)
    left_new = jnp.where(occupied_mask, refresh(left_stat, basis_left), basis_left)
    right_new = jnp.where(occupied_mask, refresh(right_stat, basis_right), basis_right)
    return (direction, left_new, right_new)


def group_kernel(n, group, spread, x_ref, o_ref, send_sem, recv_sem):
    me, peer = group()
    barrier = pltpu.get_barrier_semaphore()
    for k in range(1, n):
        pl.semaphore_signal(barrier, inc=1, device_id=peer(lax.rem(me + k, n)), device_id_type=MESH)
    pl.semaphore_wait(barrier, n - 1)
    copies = []
    for k in range(1, n):
        other = lax.rem(me + k, n)
        copy = pltpu.make_async_remote_copy(
            src_ref=x_ref.at[other] if spread else x_ref,
            dst_ref=o_ref.at[me],
            send_sem=send_sem.at[k],
            recv_sem=recv_sem.at[k],
            device_id=peer(other),
            device_id_type=MESH,
        )
        copy.start()
        copies.append(copy)
    o_ref[me] = x_ref[me] if spread else x_ref[...]
    for copy in copies:
        copy.wait()


def dp_group():
    me = lax.axis_index("dp")
    owner = lax.axis_index("owner")
    return me, lambda j: (j, owner)


def core_group():
    replica = lax.axis_index("dp")
    owner = lax.axis_index("owner")
    me = lax.rem(owner, 2)
    return me, lambda j: (replica, owner - me + j)


def chip_group():
    replica = lax.axis_index("dp")
    owner = lax.axis_index("owner")
    core = lax.rem(owner, 2)
    return lax.div(owner, 2), lambda j: (replica, j * 2 + core)


GROUPS = {"dp": dp_group, "core": core_group, "chip": chip_group}
CALLS = []


def exchange(x, name, n, spread):
    CALLS.append(name)
    shape = x.shape[1:] if spread else x.shape
    return pl.pallas_call(
        functools.partial(group_kernel, n, GROUPS[name], spread),
        out_shape=jax.ShapeDtypeStruct((n,) + shape, x.dtype),
        in_specs=[pl.BlockSpec(memory_space=pltpu.VMEM)],
        out_specs=pl.BlockSpec(memory_space=pltpu.VMEM),
        scratch_shapes=[pltpu.SemaphoreType.DMA((n,)), pltpu.SemaphoreType.DMA((n,))],
        compiler_params=pltpu.CompilerParams(
            collective_id=len(CALLS) - 1, has_side_effects=True, vmem_limit_bytes=48 * 1024 * 1024
        ),
    )(x)


def reduce_in(x, name, n):
    return jnp.sum(exchange(x, name, n, True).astype(jnp.float32), axis=0)


def all_reduce_blocks(blocks, n_dp, n_chip):
    count, rows, cols = blocks.shape
    per = count // (2 * n_dp)
    half = reduce_in(blocks.reshape(2, count // 2, rows, cols), "core", 2).astype(jnp.bfloat16)
    mine = reduce_in(half.reshape(n_dp, per, rows, cols), "dp", n_dp).astype(jnp.bfloat16)
    piece = reduce_in(mine.reshape(n_chip, per * rows // n_chip, cols), "chip", n_chip)
    return spread_out(piece.astype(jnp.bfloat16), n_dp, n_chip, per, rows, cols)


def spread_out(piece, n_dp, n_chip, per, rows, cols):
    mine = exchange(piece, "chip", n_chip, False).reshape(per, rows, cols)
    half = exchange(mine, "dp", n_dp, False).reshape(n_dp * per, rows, cols)
    return exchange(half, "core", 2, False).reshape(2 * n_dp * per, rows, cols)


def body(
    partials,
    owners,
    step_count,
    master,
    moment,
    second,
    stat_left,
    stat_right,
    basis_left,
    basis_right,
):
    CALLS.clear()
    owner_count = lax.axis_size("owner")
    n_dp = lax.axis_size("dp")
    n_chip = owner_count // 2
    slot_count = master.shape[0]
    total_slot_count = slot_count * owner_count
    target, source, occupied = slot_layout(owners, slot_count, total_slot_count)
    first_slot = lax.axis_index("owner") * slot_count
    occupied_mine = lax.dynamic_slice_in_dim(occupied, first_slot, slot_count, 0)
    source_mine = lax.dynamic_slice_in_dim(source, first_slot, slot_count, 0)
    grad_sum = all_reduce_blocks(partials[0], n_dp, n_chip)
    mask_mine = (occupied_mine > 0).astype(jnp.float32)[:, None, None]
    gradient = jnp.take(grad_sum, source_mine, axis=0).astype(jnp.float32) * mask_mine
    direction, left_new, right_new = soap_update(
        gradient,
        occupied_mine,
        moment,
        second,
        stat_left,
        stat_right,
        basis_left,
        basis_right,
        step_count,
    )
    updated = (master - 0.01 * (direction + 0.1 * master)).astype(jnp.bfloat16)
    block_count = owners.shape[0]
    count, rows, cols = block_count, updated.shape[1], updated.shape[2]
    per = count // (2 * n_dp)
    rank = target - first_slot
    in_mine = (rank >= 0) & (rank < slot_count)
    dense = jnp.where(
        in_mine[:, None, None], jnp.take(updated, jnp.clip(rank, 0, slot_count - 1), axis=0), 0
    ).astype(jnp.bfloat16)
    replica = lax.axis_index("dp")
    chunks = dense.reshape(2, n_dp, per, rows, cols)
    chunks = lax.dynamic_index_in_dim(chunks, replica, axis=1, keepdims=False)
    pair = reduce_in(chunks, "core", 2)
    piece = reduce_in(pair.astype(jnp.bfloat16).reshape(n_chip, per * rows // n_chip, cols), "chip", n_chip)
    weights_all = spread_out(piece.astype(jnp.bfloat16), n_dp, n_chip, per, rows, cols)
    return (weights_all, direction, left_new, right_new)


def solution(mesh):
    placed = (
        P(("dp", "owner"), None, None, None),
        P(),
        P(),
        P("owner", None, None),
        P("owner", None, None),
        P("owner", None, None),
        P("owner", None, None),
        P("owner", None, None),
        P("owner", None, None),
        P("owner", None, None),
    )
    return jax.shard_map(
        body,
        mesh=mesh,
        in_specs=placed,
        out_specs=(P(), P("owner", None, None), P("owner", None, None), P("owner", None, None)),
        check_vma=False,
    )
```

```python
import functools

import jax
import jax.numpy as jnp
from jax import lax
from jax.experimental import pallas as pl
from jax.experimental.pallas import tpu as pltpu
from jax.sharding import PartitionSpec as P

MESH = pl.DeviceIdType.MESH

NS_ITERS = 6


def product(left, right):
    return jnp.matmul(left, right, precision=lax.Precision.HIGHEST)


def transposed(array):
    return jnp.swapaxes(array, 1, 2)


def refresh(stat, basis):
    power = product(stat, basis)
    magnitude = jnp.sqrt(jnp.sum(power * power, axis=(1, 2), keepdims=True))
    iterate = power / (magnitude + 1e-06)
    for repeat_count in range(NS_ITERS):
        iterate = 1.5 * iterate - 0.5 * product(iterate, product(transposed(iterate), iterate))
    return iterate


def slot_layout(owners, slot_count, total_slot_count):
    block_count = owners.shape[0]
    slot_position = jnp.arange(block_count, dtype=jnp.int32)
    before = (owners[:, None] == owners[None, :]) & (
        slot_position[:, None] > slot_position[None, :]
    )
    rank_in = jnp.sum(before.astype(jnp.int32), axis=1)
    target = owners * slot_count + rank_in
    matches = (target[:, None] == jnp.arange(total_slot_count, dtype=jnp.int32)[None, :]).astype(
        jnp.int32
    )
    source = jnp.sum(matches * slot_position[:, None], axis=0)
    occupied = jnp.sum(matches, axis=0)
    return (target, source, occupied)


def soap_update(
    gradient, occupied, moment, second, stat_left, stat_right, basis_left, basis_right, step_count
):
    elapsed = step_count[0].astype(jnp.float32)
    moment_new = 0.95 * moment + 0.05 * gradient
    rotated = product(transposed(basis_left), product(gradient, basis_right))
    rot_moment = product(transposed(basis_left), product(moment_new, basis_right))
    second_new = 0.95 * second + 0.05 * rotated * rotated
    correction = 1.0 - jnp.power(jnp.float32(0.95), elapsed)
    scaled = rot_moment / correction / (jnp.sqrt(second_new / correction) + 1e-08)
    occupied_mask = (occupied > 0)[:, None, None]
    direction = jnp.where(
        occupied_mask, product(basis_left, product(scaled, transposed(basis_right))), 0.0
    )
    left_stat = 0.95 * stat_left + 0.05 * product(gradient, transposed(gradient))
    right_stat = 0.95 * stat_right + 0.05 * product(transposed(gradient), gradient)
    left_new = jnp.where(occupied_mask, refresh(left_stat, basis_left), basis_left)
    right_new = jnp.where(occupied_mask, refresh(right_stat, basis_right), basis_right)
    return (direction, left_new, right_new)


def dp_group():
    me = lax.axis_index("dp")
    owner = lax.axis_index("owner")
    return me, lambda j: (j, owner)


def core_group():
    replica = lax.axis_index("dp")
    owner = lax.axis_index("owner")
    me = lax.rem(owner, 2)
    return me, lambda j: (replica, owner - me + j)


def chip_group():
    replica = lax.axis_index("dp")
    owner = lax.axis_index("owner")
    core = lax.rem(owner, 2)
    return lax.div(owner, 2), lambda j: (replica, j * 2 + core)


def enter(groups):
    barrier = pltpu.get_barrier_semaphore()
    total = 0
    for n, me, peer in groups:
        for k in range(1, n):
            pl.semaphore_signal(barrier, inc=1, device_id=peer(lax.rem(me + k, n)), device_id_type=MESH)
        total += n - 1
    pl.semaphore_wait(barrier, total)


def phase(group, source, dest, send, recv):
    n, me, peer = group
    copies = []
    for k in range(1, n):
        other = lax.rem(me + k, n)
        copy = pltpu.make_async_remote_copy(
            src_ref=source(other),
            dst_ref=dest(me),
            send_sem=send.at[k],
            recv_sem=recv.at[k],
            device_id=peer(other),
            device_id_type=MESH,
        )
        copy.start()
        copies.append(copy)
    return copies


def finish(copies):
    for copy in copies:
        copy.wait()


def sum_slots(buf, out, n, rows, start):
    step = 128 if rows % 128 == 0 else rows

    def one(i, carry):
        at = pl.multiple_of(i * step, step)
        total = buf[0, pl.ds(at, step), :].astype(jnp.float32)
        for j in range(1, n):
            total = total + buf[j, pl.ds(at, step), :].astype(jnp.float32)
        out[pl.ds(start + at, step), :] = total.astype(out.dtype)
        return carry

    lax.fori_loop(0, rows // step, one, 0)


def spread_phases(o_ref, core, dp, chip, piece, send, recv, first):
    n_dp, n_chip = dp[0], chip[0]
    c, r, m = core[1], dp[1], chip[1]
    chunk = n_chip * piece
    half = n_dp * chunk
    base = c * half + r * chunk
    finish(phase(chip, lambda j: o_ref.at[pl.ds(base + m * piece, piece)],
                 lambda me: o_ref.at[pl.ds(base + me * piece, piece)], send.at[first], recv.at[first]))
    finish(phase(dp, lambda j: o_ref.at[pl.ds(c * half + r * chunk, chunk)],
                 lambda me: o_ref.at[pl.ds(c * half + me * chunk, chunk)], send.at[first + 1], recv.at[first + 1]))
    finish(phase(core, lambda j: o_ref.at[pl.ds(c * half, half)],
                 lambda me: o_ref.at[pl.ds(me * half, half)], send.at[first + 2], recv.at[first + 2]))


def groups_of(n_dp, n_chip):
    core_me, core_peer = core_group()
    dp_me, dp_peer = dp_group()
    chip_me, chip_peer = chip_group()
    return (2, core_me, core_peer), (n_dp, dp_me, dp_peer), (n_chip, chip_me, chip_peer)


def grad_kernel(n_dp, n_chip, p_ref, o_ref, buf1, hbuf, buf2, mbuf, buf3, send, recv):
    core, dp, chip = groups_of(n_dp, n_chip)
    enter((core, dp, chip))
    half = p_ref.shape[0] // 2
    chunk = half // n_dp
    piece = chunk // n_chip
    c, r, m = core[1], dp[1], chip[1]
    finish(phase(core, lambda j: p_ref.at[pl.ds(j * half, half)], lambda me: buf1.at[1], send.at[0], recv.at[0]))
    buf1[0] = p_ref[pl.ds(c * half, half), :]
    sum_slots(buf1, hbuf, 2, half, 0)
    buf2[r] = hbuf[pl.ds(r * chunk, chunk), :]
    finish(phase(dp, lambda j: hbuf.at[pl.ds(j * chunk, chunk)], lambda me: buf2.at[me], send.at[1], recv.at[1]))
    sum_slots(buf2, mbuf, n_dp, chunk, 0)
    buf3[m] = mbuf[pl.ds(m * piece, piece), :]
    finish(phase(chip, lambda j: mbuf.at[pl.ds(j * piece, piece)], lambda me: buf3.at[me], send.at[2], recv.at[2]))
    sum_slots(buf3, o_ref, n_chip, piece, c * half + r * chunk + m * piece)
    spread_phases(o_ref, core, dp, chip, piece, send, recv, 3)


def weight_kernel(n_dp, n_chip, x_ref, o_ref, buf1, pbuf, buf3, send, recv):
    core, dp, chip = groups_of(n_dp, n_chip)
    enter((core, dp, chip))
    chunk = x_ref.shape[1]
    piece = chunk // n_chip
    half = n_dp * chunk
    c, r, m = core[1], dp[1], chip[1]
    finish(phase(core, lambda j: x_ref.at[j], lambda me: buf1.at[1], send.at[0], recv.at[0]))
    buf1[0] = x_ref[c]
    sum_slots(buf1, pbuf, 2, chunk, 0)
    buf3[m] = pbuf[pl.ds(m * piece, piece), :]
    finish(phase(chip, lambda j: pbuf.at[pl.ds(j * piece, piece)], lambda me: buf3.at[me], send.at[1], recv.at[1]))
    sum_slots(buf3, o_ref, n_chip, piece, c * half + r * chunk + m * piece)
    spread_phases(o_ref, core, dp, chip, piece, send, recv, 2)


def params(collective_id):
    return pltpu.CompilerParams(
        collective_id=collective_id, has_side_effects=True, vmem_limit_bytes=48 * 1024 * 1024
    )


def all_reduce_blocks(blocks, n_dp, n_chip):
    count, rows, cols = blocks.shape
    flat = blocks.reshape(count * rows, cols)
    half = count * rows // 2
    chunk = half // n_dp
    piece = chunk // n_chip
    vmem = pl.BlockSpec(memory_space=pltpu.VMEM)
    out = pl.pallas_call(
        functools.partial(grad_kernel, n_dp, n_chip),
        out_shape=jax.ShapeDtypeStruct(flat.shape, flat.dtype),
        in_specs=[vmem],
        out_specs=vmem,
        scratch_shapes=[
            pltpu.VMEM((2, half, cols), flat.dtype),
            pltpu.VMEM((half, cols), flat.dtype),
            pltpu.VMEM((n_dp, chunk, cols), flat.dtype),
            pltpu.VMEM((chunk, cols), flat.dtype),
            pltpu.VMEM((n_chip, piece, cols), flat.dtype),
            pltpu.SemaphoreType.DMA((6, n_chip)),
            pltpu.SemaphoreType.DMA((6, n_chip)),
        ],
        compiler_params=params(0),
    )(flat)
    return out.reshape(count, rows, cols)


def gather_blocks(chunks, n_dp, n_chip, count):
    _, chunk, cols = chunks.shape
    piece = chunk // n_chip
    vmem = pl.BlockSpec(memory_space=pltpu.VMEM)
    return pl.pallas_call(
        functools.partial(weight_kernel, n_dp, n_chip),
        out_shape=jax.ShapeDtypeStruct((2 * n_dp * chunk, cols), chunks.dtype),
        in_specs=[vmem],
        out_specs=vmem,
        scratch_shapes=[
            pltpu.VMEM((2, chunk, cols), chunks.dtype),
            pltpu.VMEM((chunk, cols), chunks.dtype),
            pltpu.VMEM((n_chip, piece, cols), chunks.dtype),
            pltpu.SemaphoreType.DMA((5, n_chip)),
            pltpu.SemaphoreType.DMA((5, n_chip)),
        ],
        compiler_params=params(1),
    )(chunks)


def body(
    partials,
    owners,
    step_count,
    master,
    moment,
    second,
    stat_left,
    stat_right,
    basis_left,
    basis_right,
):
    owner_count = lax.axis_size("owner")
    n_dp = lax.axis_size("dp")
    n_chip = owner_count // 2
    slot_count = master.shape[0]
    total_slot_count = slot_count * owner_count
    target, source, occupied = slot_layout(owners, slot_count, total_slot_count)
    first_slot = lax.axis_index("owner") * slot_count
    occupied_mine = lax.dynamic_slice_in_dim(occupied, first_slot, slot_count, 0)
    source_mine = lax.dynamic_slice_in_dim(source, first_slot, slot_count, 0)
    grad_sum = all_reduce_blocks(partials[0], n_dp, n_chip)
    mask_mine = (occupied_mine > 0).astype(jnp.float32)[:, None, None]
    gradient = jnp.take(grad_sum, source_mine, axis=0).astype(jnp.float32) * mask_mine
    direction, left_new, right_new = soap_update(
        gradient,
        occupied_mine,
        moment,
        second,
        stat_left,
        stat_right,
        basis_left,
        basis_right,
        step_count,
    )
    updated = (master - 0.01 * (direction + 0.1 * master)).astype(jnp.bfloat16)
    block_count = owners.shape[0]
    count, rows, cols = block_count, updated.shape[1], updated.shape[2]
    per = count // (2 * n_dp)
    rank = target - first_slot
    in_mine = (rank >= 0) & (rank < slot_count)
    dense = jnp.where(
        in_mine[:, None, None], jnp.take(updated, jnp.clip(rank, 0, slot_count - 1), axis=0), 0
    ).astype(jnp.bfloat16)
    replica = lax.axis_index("dp")
    chunks = dense.reshape(2, n_dp, per * rows, cols)
    chunks = lax.dynamic_index_in_dim(chunks, replica, axis=1, keepdims=False)
    weights_all = gather_blocks(chunks, n_dp, n_chip, count).reshape(count, rows, cols)
    return (weights_all, direction, left_new, right_new)


def solution(mesh):
    placed = (
        P(("dp", "owner"), None, None, None),
        P(),
        P(),
        P("owner", None, None),
        P("owner", None, None),
        P("owner", None, None),
        P("owner", None, None),
        P("owner", None, None),
        P("owner", None, None),
        P("owner", None, None),
    )
    return jax.shard_map(
        body,
        mesh=mesh,
        in_specs=placed,
        out_specs=(P(), P("owner", None, None), P("owner", None, None), P("owner", None, None)),
        check_vma=False,
    )
```

```python
import functools

import jax
import jax.numpy as jnp
from jax import lax
from jax.experimental import pallas as pl
from jax.experimental.pallas import tpu as pltpu
from jax.sharding import PartitionSpec as P

MESH = pl.DeviceIdType.MESH

NS_ITERS = 6


def product(left, right):
    return jnp.matmul(left, right, precision=lax.Precision.HIGHEST)


def transposed(array):
    return jnp.swapaxes(array, 1, 2)


def refresh(stat, basis):
    power = product(stat, basis)
    magnitude = jnp.sqrt(jnp.sum(power * power, axis=(1, 2), keepdims=True))
    iterate = power / (magnitude + 1e-06)
    for repeat_count in range(NS_ITERS):
        iterate = 1.5 * iterate - 0.5 * product(iterate, product(transposed(iterate), iterate))
    return iterate


def slot_layout(owners, slot_count, total_slot_count):
    block_count = owners.shape[0]
    slot_position = jnp.arange(block_count, dtype=jnp.int32)
    before = (owners[:, None] == owners[None, :]) & (
        slot_position[:, None] > slot_position[None, :]
    )
    rank_in = jnp.sum(before.astype(jnp.int32), axis=1)
    target = owners * slot_count + rank_in
    matches = (target[:, None] == jnp.arange(total_slot_count, dtype=jnp.int32)[None, :]).astype(
        jnp.int32
    )
    source = jnp.sum(matches * slot_position[:, None], axis=0)
    occupied = jnp.sum(matches, axis=0)
    return (target, source, occupied)


def soap_update(
    gradient, occupied, moment, second, stat_left, stat_right, basis_left, basis_right, step_count
):
    elapsed = step_count[0].astype(jnp.float32)
    moment_new = 0.95 * moment + 0.05 * gradient
    rotated = product(transposed(basis_left), product(gradient, basis_right))
    rot_moment = product(transposed(basis_left), product(moment_new, basis_right))
    second_new = 0.95 * second + 0.05 * rotated * rotated
    correction = 1.0 - jnp.power(jnp.float32(0.95), elapsed)
    scaled = rot_moment / correction / (jnp.sqrt(second_new / correction) + 1e-08)
    occupied_mask = (occupied > 0)[:, None, None]
    direction = jnp.where(
        occupied_mask, product(basis_left, product(scaled, transposed(basis_right))), 0.0
    )
    left_stat = 0.95 * stat_left + 0.05 * product(gradient, transposed(gradient))
    right_stat = 0.95 * stat_right + 0.05 * product(transposed(gradient), gradient)
    left_new = jnp.where(occupied_mask, refresh(left_stat, basis_left), basis_left)
    right_new = jnp.where(occupied_mask, refresh(right_stat, basis_right), basis_right)
    return (direction, left_new, right_new)


def dp_group():
    me = lax.axis_index("dp")
    owner = lax.axis_index("owner")
    return me, lambda j: (j, owner)


def core_group():
    replica = lax.axis_index("dp")
    owner = lax.axis_index("owner")
    me = lax.rem(owner, 2)
    return me, lambda j: (replica, owner - me + j)


def chip_group():
    replica = lax.axis_index("dp")
    owner = lax.axis_index("owner")
    core = lax.rem(owner, 2)
    return lax.div(owner, 2), lambda j: (replica, j * 2 + core)


def enter(groups):
    barrier = pltpu.get_barrier_semaphore()
    total = 0
    for n, me, peer in groups:
        for k in range(1, n):
            pl.semaphore_signal(barrier, inc=1, device_id=peer(lax.rem(me + k, n)), device_id_type=MESH)
        total += n - 1
    pl.semaphore_wait(barrier, total)


def phase(group, source, dest, send, recv):
    n, me, peer = group
    copies = []
    for k in range(1, n):
        other = lax.rem(me + k, n)
        copy = pltpu.make_async_remote_copy(
            src_ref=source(other),
            dst_ref=dest(me),
            send_sem=send.at[k],
            recv_sem=recv.at[k],
            device_id=peer(other),
            device_id_type=MESH,
        )
        copy.start()
        copies.append(copy)
    return copies


def finish(copies):
    for copy in copies:
        copy.wait()


def sum_slots(buf, out, n, rows, start):
    step = 128 if rows % 128 == 0 else rows

    def one(i, carry):
        at = pl.multiple_of(i * step, step)
        total = buf[0, pl.ds(at, step), :].astype(jnp.float32)
        for j in range(1, n):
            total = total + buf[j, pl.ds(at, step), :].astype(jnp.float32)
        out[pl.ds(start + at, step), :] = total.astype(out.dtype)
        return carry

    lax.fori_loop(0, rows // step, one, 0)


def spread_phases(o_ref, core, dp, chip, piece, send, recv, first):
    n_dp, n_chip = dp[0], chip[0]
    c, r, m = core[1], dp[1], chip[1]
    chunk = n_chip * piece
    half = n_dp * chunk
    base = c * half + r * chunk
    finish(phase(chip, lambda j: o_ref.at[pl.ds(base + m * piece, piece)],
                 lambda me: o_ref.at[pl.ds(base + me * piece, piece)], send.at[first], recv.at[first]))
    finish(phase(dp, lambda j: o_ref.at[pl.ds(c * half + r * chunk, chunk)],
                 lambda me: o_ref.at[pl.ds(c * half + me * chunk, chunk)], send.at[first + 1], recv.at[first + 1]))
    finish(phase(core, lambda j: o_ref.at[pl.ds(c * half, half)],
                 lambda me: o_ref.at[pl.ds(me * half, half)], send.at[first + 2], recv.at[first + 2]))


def groups_of(n_dp, n_chip):
    core_me, core_peer = core_group()
    dp_me, dp_peer = dp_group()
    chip_me, chip_peer = chip_group()
    return (2, core_me, core_peer), (n_dp, dp_me, dp_peer), (n_chip, chip_me, chip_peer)


def grad_kernel(n_dp, n_chip, p_ref, o_ref, buf1, hbuf, buf2, mbuf, buf3, send, recv):
    core, dp, chip = groups_of(n_dp, n_chip)
    enter((core, dp, chip))
    half = p_ref.shape[0] // 2
    chunk = half // n_dp
    piece = chunk // n_chip
    c, r, m = core[1], dp[1], chip[1]
    finish(phase(core, lambda j: p_ref.at[pl.ds(j * half, half)], lambda me: buf1.at[1], send.at[0], recv.at[0]))
    buf1[0] = p_ref[pl.ds(c * half, half), :]
    sum_slots(buf1, hbuf, 2, half, 0)
    buf2[r] = hbuf[pl.ds(r * chunk, chunk), :]
    finish(phase(dp, lambda j: hbuf.at[pl.ds(j * chunk, chunk)], lambda me: buf2.at[me], send.at[1], recv.at[1]))
    sum_slots(buf2, mbuf, n_dp, chunk, 0)
    buf3[m] = mbuf[pl.ds(m * piece, piece), :]
    finish(phase(chip, lambda j: mbuf.at[pl.ds(j * piece, piece)], lambda me: buf3.at[me], send.at[2], recv.at[2]))
    sum_slots(buf3, o_ref, n_chip, piece, c * half + r * chunk + m * piece)
    spread_phases(o_ref, core, dp, chip, piece, send, recv, 3)


def weight_kernel(n_dp, n_chip, x_ref, o_ref, buf1, pbuf, buf3, send, recv):
    core, dp, chip = groups_of(n_dp, n_chip)
    enter((core, dp, chip))
    chunk = x_ref.shape[1]
    piece = chunk // n_chip
    half = n_dp * chunk
    c, r, m = core[1], dp[1], chip[1]
    finish(phase(core, lambda j: x_ref.at[j], lambda me: buf1.at[1], send.at[0], recv.at[0]))
    buf1[0] = x_ref[c]
    sum_slots(buf1, pbuf, 2, chunk, 0)
    buf3[m] = pbuf[pl.ds(m * piece, piece), :]
    finish(phase(chip, lambda j: pbuf.at[pl.ds(j * piece, piece)], lambda me: buf3.at[me], send.at[1], recv.at[1]))
    sum_slots(buf3, o_ref, n_chip, piece, c * half + r * chunk + m * piece)
    spread_phases(o_ref, core, dp, chip, piece, send, recv, 2)


def params(collective_id):
    return pltpu.CompilerParams(
        collective_id=collective_id, has_side_effects=True, vmem_limit_bytes=48 * 1024 * 1024
    )


def all_reduce_blocks(blocks, n_dp, n_chip):
    count, rows, cols = blocks.shape
    flat = blocks.reshape(count * rows, cols)
    half = count * rows // 2
    chunk = half // n_dp
    piece = chunk // n_chip
    vmem = pl.BlockSpec(memory_space=pltpu.VMEM)
    out = pl.pallas_call(
        functools.partial(grad_kernel, n_dp, n_chip),
        out_shape=jax.ShapeDtypeStruct(flat.shape, flat.dtype),
        in_specs=[vmem],
        out_specs=vmem,
        scratch_shapes=[
            pltpu.VMEM((2, half, cols), flat.dtype),
            pltpu.VMEM((half, cols), flat.dtype),
            pltpu.VMEM((n_dp, chunk, cols), flat.dtype),
            pltpu.VMEM((chunk, cols), flat.dtype),
            pltpu.VMEM((n_chip, piece, cols), flat.dtype),
            pltpu.SemaphoreType.DMA((6, n_chip)),
            pltpu.SemaphoreType.DMA((6, n_chip)),
        ],
        compiler_params=params(0),
    )(flat)
    return out.reshape(count, rows, cols)


def gather_blocks(chunks, n_dp, n_chip, count):
    _, chunk, cols = chunks.shape
    piece = chunk // n_chip
    vmem = pl.BlockSpec(memory_space=pltpu.VMEM)
    return pl.pallas_call(
        functools.partial(weight_kernel, n_dp, n_chip),
        out_shape=jax.ShapeDtypeStruct((2 * n_dp * chunk, cols), chunks.dtype),
        in_specs=[vmem],
        out_specs=vmem,
        scratch_shapes=[
            pltpu.VMEM((2, chunk, cols), chunks.dtype),
            pltpu.VMEM((chunk, cols), chunks.dtype),
            pltpu.VMEM((n_chip, piece, cols), chunks.dtype),
            pltpu.SemaphoreType.DMA((5, n_chip)),
            pltpu.SemaphoreType.DMA((5, n_chip)),
        ],
        compiler_params=params(1),
    )(chunks)


def mm(left, right):
    return jnp.dot(left, right, precision=lax.Precision.HIGHEST, preferred_element_type=jnp.float32)


def refresh_one(stat, basis):
    power = mm(stat, basis)
    magnitude = jnp.sqrt(jnp.sum(power * power, keepdims=True))
    iterate = power / (magnitude + 1e-06)
    for repeat_count in range(NS_ITERS):
        iterate = 1.5 * iterate - 0.5 * mm(iterate, mm(iterate.T, iterate))
    return iterate


def soap_kernel(
    scalars, g_ref, m_ref, s_ref, sl_ref, sr_ref, bl_ref, br_ref, w_ref,
    d_out, l_out, r_out, u_out,
):
    slot = pl.program_id(0)
    correction = scalars[0]
    occupied = scalars[1 + slot] > 0
    gradient = g_ref[0]
    basis_left = bl_ref[0]
    basis_right = br_ref[0]
    moment_new = 0.95 * m_ref[0] + 0.05 * gradient
    rotated = mm(basis_left.T, mm(gradient, basis_right))
    rot_moment = mm(basis_left.T, mm(moment_new, basis_right))
    second_new = 0.95 * s_ref[0] + 0.05 * rotated * rotated
    scaled = rot_moment / correction / (jnp.sqrt(second_new / correction) + 1e-08)
    direction = jnp.where(occupied, mm(basis_left, mm(scaled, basis_right.T)), 0.0)
    d_out[0] = direction
    master = w_ref[0]
    u_out[0] = (master - 0.01 * (direction + 0.1 * master)).astype(u_out.dtype)
    left_stat = 0.95 * sl_ref[0] + 0.05 * mm(gradient, gradient.T)
    right_stat = 0.95 * sr_ref[0] + 0.05 * mm(gradient.T, gradient)
    l_out[0] = jnp.where(occupied, refresh_one(left_stat, basis_left), basis_left)
    r_out[0] = jnp.where(occupied, refresh_one(right_stat, basis_right), basis_right)


def soap_slots(gradient, occupied, moment, second, stat_left, stat_right, basis_left, basis_right, master, step_count):
    slots, rows, cols = gradient.shape
    elapsed = step_count[0].astype(jnp.float32)
    correction = 1.0 - jnp.power(jnp.float32(0.95), elapsed)
    scalars = jnp.concatenate([correction[None], occupied.astype(jnp.float32)])
    block = pl.BlockSpec((1, rows, cols), lambda i: (i, 0, 0))
    f32 = jax.ShapeDtypeStruct(gradient.shape, jnp.float32)
    return pl.pallas_call(
        soap_kernel,
        grid=(slots,),
        out_shape=(f32, f32, f32, jax.ShapeDtypeStruct(gradient.shape, jnp.bfloat16)),
        in_specs=[pl.BlockSpec(memory_space=pltpu.SMEM)] + [block] * 8,
        out_specs=(block, block, block, block),
    )(scalars, gradient, moment, second, stat_left, stat_right, basis_left, basis_right, master)


def body(
    partials,
    owners,
    step_count,
    master,
    moment,
    second,
    stat_left,
    stat_right,
    basis_left,
    basis_right,
):
    owner_count = lax.axis_size("owner")
    n_dp = lax.axis_size("dp")
    n_chip = owner_count // 2
    slot_count = master.shape[0]
    total_slot_count = slot_count * owner_count
    target, source, occupied = slot_layout(owners, slot_count, total_slot_count)
    first_slot = lax.axis_index("owner") * slot_count
    occupied_mine = lax.dynamic_slice_in_dim(occupied, first_slot, slot_count, 0)
    source_mine = lax.dynamic_slice_in_dim(source, first_slot, slot_count, 0)
    grad_sum = all_reduce_blocks(partials[0], n_dp, n_chip)
    mask_mine = (occupied_mine > 0).astype(jnp.float32)[:, None, None]
    gradient = jnp.take(grad_sum, source_mine, axis=0).astype(jnp.float32) * mask_mine
    direction, left_new, right_new, updated = soap_slots(
        gradient, occupied_mine, moment, second, stat_left, stat_right, basis_left, basis_right, master, step_count
    )
    block_count = owners.shape[0]
    count, rows, cols = block_count, updated.shape[1], updated.shape[2]
    per = count // (2 * n_dp)
    rank = target - first_slot
    in_mine = (rank >= 0) & (rank < slot_count)
    dense = jnp.where(
        in_mine[:, None, None], jnp.take(updated, jnp.clip(rank, 0, slot_count - 1), axis=0), 0
    ).astype(jnp.bfloat16)
    replica = lax.axis_index("dp")
    chunks = dense.reshape(2, n_dp, per * rows, cols)
    chunks = lax.dynamic_index_in_dim(chunks, replica, axis=1, keepdims=False)
    weights_all = gather_blocks(chunks, n_dp, n_chip, count).reshape(count, rows, cols)
    return (weights_all, direction, left_new, right_new)


def solution(mesh):
    placed = (
        P(("dp", "owner"), None, None, None),
        P(),
        P(),
        P("owner", None, None),
        P("owner", None, None),
        P("owner", None, None),
        P("owner", None, None),
        P("owner", None, None),
        P("owner", None, None),
        P("owner", None, None),
    )
    return jax.shard_map(
        body,
        mesh=mesh,
        in_specs=placed,
        out_specs=(P(), P("owner", None, None), P("owner", None, None), P("owner", None, None)),
        check_vma=False,
    )
```

```python
import functools

import jax
import jax.numpy as jnp
from jax import lax
from jax.experimental import pallas as pl
from jax.experimental.pallas import tpu as pltpu
from jax.sharding import PartitionSpec as P

MESH = pl.DeviceIdType.MESH

NS_ITERS = 6


def product(left, right):
    return jnp.matmul(left, right, precision=lax.Precision.HIGHEST)


def transposed(array):
    return jnp.swapaxes(array, 1, 2)


def refresh(stat, basis):
    power = product(stat, basis)
    magnitude = jnp.sqrt(jnp.sum(power * power, axis=(1, 2), keepdims=True))
    iterate = power / (magnitude + 1e-06)
    for repeat_count in range(NS_ITERS):
        iterate = 1.5 * iterate - 0.5 * product(iterate, product(transposed(iterate), iterate))
    return iterate


def slot_layout(owners, slot_count, total_slot_count):
    block_count = owners.shape[0]
    slot_position = jnp.arange(block_count, dtype=jnp.int32)
    before = (owners[:, None] == owners[None, :]) & (
        slot_position[:, None] > slot_position[None, :]
    )
    rank_in = jnp.sum(before.astype(jnp.int32), axis=1)
    target = owners * slot_count + rank_in
    matches = (target[:, None] == jnp.arange(total_slot_count, dtype=jnp.int32)[None, :]).astype(
        jnp.int32
    )
    source = jnp.sum(matches * slot_position[:, None], axis=0)
    occupied = jnp.sum(matches, axis=0)
    return (target, source, occupied)


def soap_update(
    gradient, occupied, moment, second, stat_left, stat_right, basis_left, basis_right, step_count
):
    elapsed = step_count[0].astype(jnp.float32)
    moment_new = 0.95 * moment + 0.05 * gradient
    rotated = product(transposed(basis_left), product(gradient, basis_right))
    rot_moment = product(transposed(basis_left), product(moment_new, basis_right))
    second_new = 0.95 * second + 0.05 * rotated * rotated
    correction = 1.0 - jnp.power(jnp.float32(0.95), elapsed)
    scaled = rot_moment / correction / (jnp.sqrt(second_new / correction) + 1e-08)
    occupied_mask = (occupied > 0)[:, None, None]
    direction = jnp.where(
        occupied_mask, product(basis_left, product(scaled, transposed(basis_right))), 0.0
    )
    left_stat = 0.95 * stat_left + 0.05 * product(gradient, transposed(gradient))
    right_stat = 0.95 * stat_right + 0.05 * product(transposed(gradient), gradient)
    left_new = jnp.where(occupied_mask, refresh(left_stat, basis_left), basis_left)
    right_new = jnp.where(occupied_mask, refresh(right_stat, basis_right), basis_right)
    return (direction, left_new, right_new)


def dp_group():
    me = lax.axis_index("dp")
    owner = lax.axis_index("owner")
    return me, lambda j: (j, owner)


def core_group():
    replica = lax.axis_index("dp")
    owner = lax.axis_index("owner")
    me = lax.rem(owner, 2)
    return me, lambda j: (replica, owner - me + j)


def chip_group():
    replica = lax.axis_index("dp")
    owner = lax.axis_index("owner")
    core = lax.rem(owner, 2)
    return lax.div(owner, 2), lambda j: (replica, j * 2 + core)


def enter(groups):
    barrier = pltpu.get_barrier_semaphore()
    total = 0
    for n, me, peer in groups:
        for k in range(1, n):
            pl.semaphore_signal(barrier, inc=1, device_id=peer(lax.rem(me + k, n)), device_id_type=MESH)
        total += n - 1
    pl.semaphore_wait(barrier, total)


def phase(group, source, dest, send, recv):
    n, me, peer = group
    copies = []
    for k in range(1, n):
        other = lax.rem(me + k, n)
        copy = pltpu.make_async_remote_copy(
            src_ref=source(other),
            dst_ref=dest(me),
            send_sem=send.at[k],
            recv_sem=recv.at[k],
            device_id=peer(other),
            device_id_type=MESH,
        )
        copy.start()
        copies.append(copy)
    return copies


def finish(copies):
    for copy in copies:
        copy.wait()


def sum_slots(buf, out, n, rows, start):
    step = 128 if rows % 128 == 0 else rows

    def one(i, carry):
        at = pl.multiple_of(i * step, step)
        total = buf[0, pl.ds(at, step), :].astype(jnp.float32)
        for j in range(1, n):
            total = total + buf[j, pl.ds(at, step), :].astype(jnp.float32)
        out[pl.ds(start + at, step), :] = total.astype(out.dtype)
        return carry

    lax.fori_loop(0, rows // step, one, 0)


def spread_phases(o_ref, core, dp, chip, piece, send, recv, first):
    n_dp, n_chip = dp[0], chip[0]
    c, r, m = core[1], dp[1], chip[1]
    chunk = n_chip * piece
    half = n_dp * chunk
    base = c * half + r * chunk
    finish(phase(chip, lambda j: o_ref.at[pl.ds(base + m * piece, piece)],
                 lambda me: o_ref.at[pl.ds(base + me * piece, piece)], send.at[first], recv.at[first]))
    finish(phase(dp, lambda j: o_ref.at[pl.ds(c * half + r * chunk, chunk)],
                 lambda me: o_ref.at[pl.ds(c * half + me * chunk, chunk)], send.at[first + 1], recv.at[first + 1]))
    finish(phase(core, lambda j: o_ref.at[pl.ds(c * half, half)],
                 lambda me: o_ref.at[pl.ds(me * half, half)], send.at[first + 2], recv.at[first + 2]))


def groups_of(n_dp, n_chip):
    core_me, core_peer = core_group()
    dp_me, dp_peer = dp_group()
    chip_me, chip_peer = chip_group()
    return (2, core_me, core_peer), (n_dp, dp_me, dp_peer), (n_chip, chip_me, chip_peer)


def grad_kernel(n_dp, n_chip, p_ref, o_ref, buf1, hbuf, buf2, mbuf, buf3, send, recv):
    core, dp, chip = groups_of(n_dp, n_chip)
    enter((core, dp, chip))
    half = p_ref.shape[0] // 2
    chunk = half // n_dp
    piece = chunk // n_chip
    c, r, m = core[1], dp[1], chip[1]
    finish(phase(core, lambda j: p_ref.at[pl.ds(j * half, half)], lambda me: buf1.at[1], send.at[0], recv.at[0]))
    buf1[0] = p_ref[pl.ds(c * half, half), :]
    sum_slots(buf1, hbuf, 2, half, 0)
    buf2[r] = hbuf[pl.ds(r * chunk, chunk), :]
    finish(phase(dp, lambda j: hbuf.at[pl.ds(j * chunk, chunk)], lambda me: buf2.at[me], send.at[1], recv.at[1]))
    sum_slots(buf2, mbuf, n_dp, chunk, 0)
    buf3[m] = mbuf[pl.ds(m * piece, piece), :]
    finish(phase(chip, lambda j: mbuf.at[pl.ds(j * piece, piece)], lambda me: buf3.at[me], send.at[2], recv.at[2]))
    sum_slots(buf3, o_ref, n_chip, piece, c * half + r * chunk + m * piece)
    spread_phases(o_ref, core, dp, chip, piece, send, recv, 3)


def weight_kernel(n_dp, n_chip, x_ref, o_ref, buf1, pbuf, buf3, send, recv):
    core, dp, chip = groups_of(n_dp, n_chip)
    enter((core, dp, chip))
    chunk = x_ref.shape[1]
    piece = chunk // n_chip
    half = n_dp * chunk
    c, r, m = core[1], dp[1], chip[1]
    finish(phase(core, lambda j: x_ref.at[j], lambda me: buf1.at[1], send.at[0], recv.at[0]))
    buf1[0] = x_ref[c]
    sum_slots(buf1, pbuf, 2, chunk, 0)
    buf3[m] = pbuf[pl.ds(m * piece, piece), :]
    finish(phase(chip, lambda j: pbuf.at[pl.ds(j * piece, piece)], lambda me: buf3.at[me], send.at[1], recv.at[1]))
    sum_slots(buf3, o_ref, n_chip, piece, c * half + r * chunk + m * piece)
    spread_phases(o_ref, core, dp, chip, piece, send, recv, 2)


def params(collective_id):
    return pltpu.CompilerParams(
        collective_id=collective_id, has_side_effects=True, vmem_limit_bytes=48 * 1024 * 1024
    )


def all_reduce_blocks(blocks, n_dp, n_chip):
    count, rows, cols = blocks.shape
    flat = blocks.reshape(count * rows, cols)
    half = count * rows // 2
    chunk = half // n_dp
    piece = chunk // n_chip
    vmem = pl.BlockSpec(memory_space=pltpu.VMEM)
    out = pl.pallas_call(
        functools.partial(grad_kernel, n_dp, n_chip),
        out_shape=jax.ShapeDtypeStruct(flat.shape, flat.dtype),
        in_specs=[vmem],
        out_specs=vmem,
        scratch_shapes=[
            pltpu.VMEM((2, half, cols), flat.dtype),
            pltpu.VMEM((half, cols), flat.dtype),
            pltpu.VMEM((n_dp, chunk, cols), flat.dtype),
            pltpu.VMEM((chunk, cols), flat.dtype),
            pltpu.VMEM((n_chip, piece, cols), flat.dtype),
            pltpu.SemaphoreType.DMA((6, n_chip)),
            pltpu.SemaphoreType.DMA((6, n_chip)),
        ],
        compiler_params=params(0),
    )(flat)
    return out.reshape(count, rows, cols)


def gather_blocks(chunks, n_dp, n_chip, count):
    _, chunk, cols = chunks.shape
    piece = chunk // n_chip
    vmem = pl.BlockSpec(memory_space=pltpu.VMEM)
    return pl.pallas_call(
        functools.partial(weight_kernel, n_dp, n_chip),
        out_shape=jax.ShapeDtypeStruct((2 * n_dp * chunk, cols), chunks.dtype),
        in_specs=[vmem],
        out_specs=vmem,
        scratch_shapes=[
            pltpu.VMEM((2, chunk, cols), chunks.dtype),
            pltpu.VMEM((chunk, cols), chunks.dtype),
            pltpu.VMEM((n_chip, piece, cols), chunks.dtype),
            pltpu.SemaphoreType.DMA((5, n_chip)),
            pltpu.SemaphoreType.DMA((5, n_chip)),
        ],
        compiler_params=params(1),
    )(chunks)


def split(a):
    hi = a.astype(jnp.bfloat16)
    lo = (a - hi.astype(jnp.float32)).astype(jnp.bfloat16)
    return hi, lo

def mm3(left, right):
    lh, ll = split(left)
    rh, rl = split(right)
    dot = functools.partial(jnp.dot, preferred_element_type=jnp.float32)
    return dot(lh, rh) + (dot(lh, rl) + dot(ll, rh))

def soap_kernel(scalars, g_ref, m_ref, s_ref, sl_ref, sr_ref, bl_ref, br_ref, w_ref, d_out, l_out, r_out, u_out):
    slots = g_ref.shape[0]
    correction = scalars[0]
    chains = []
    for i in range(slots):
        occupied = scalars[1 + i] > 0
        gradient = g_ref[i]
        basis_left = bl_ref[i]
        basis_right = br_ref[i]
        moment_new = 0.95 * m_ref[i] + 0.05 * gradient
        rotated = mm3(basis_left.T, mm3(gradient, basis_right))
        rot_moment = mm3(basis_left.T, mm3(moment_new, basis_right))
        second_new = 0.95 * s_ref[i] + 0.05 * rotated * rotated
        scaled = rot_moment / correction / (jnp.sqrt(second_new / correction) + 1e-08)
        direction = jnp.where(occupied, mm3(basis_left, mm3(scaled, basis_right.T)), 0.0)
        d_out[i] = direction
        master = w_ref[i]
        u_out[i] = (master - 0.01 * (direction + 0.1 * master)).astype(u_out.dtype)
        left_stat = 0.95 * sl_ref[i] + 0.05 * mm3(gradient, gradient.T)
        right_stat = 0.95 * sr_ref[i] + 0.05 * mm3(gradient.T, gradient)
        chains.append((left_stat, basis_left, l_out, i, occupied))
        chains.append((right_stat, basis_right, r_out, i, occupied))
    iterates = []
    for stat, basis, out, i, occupied in chains:
        power = mm3(stat, basis)
        magnitude = jnp.sqrt(jnp.sum(power * power, keepdims=True))
        iterates.append(power / (magnitude + 1e-06))
    for repeat_count in range(NS_ITERS):
        grams = [mm3(it.T, it) for it in iterates]
        iterates = [1.5 * it - 0.5 * mm3(it, gram) for it, gram in zip(iterates, grams)]
    for (stat, basis, out, i, occupied), it in zip(chains, iterates):
        out[i] = jnp.where(occupied, it, basis)

def soap_slots(gradient, occupied, moment, second, stat_left, stat_right, basis_left, basis_right, master, step_count):
    elapsed = step_count[0].astype(jnp.float32)
    correction = 1.0 - jnp.power(jnp.float32(0.95), elapsed)
    scalars = jnp.concatenate([correction[None], occupied.astype(jnp.float32)])
    vmem = pl.BlockSpec(memory_space=pltpu.VMEM)
    f32 = jax.ShapeDtypeStruct(gradient.shape, jnp.float32)
    return pl.pallas_call(
        soap_kernel,
        out_shape=(f32, f32, f32, jax.ShapeDtypeStruct(gradient.shape, jnp.bfloat16)),
        in_specs=[pl.BlockSpec(memory_space=pltpu.SMEM)] + [vmem] * 8,
        out_specs=(vmem, vmem, vmem, vmem),
    )(scalars, gradient, moment, second, stat_left, stat_right, basis_left, basis_right, master)


def body(
    partials,
    owners,
    step_count,
    master,
    moment,
    second,
    stat_left,
    stat_right,
    basis_left,
    basis_right,
):
    owner_count = lax.axis_size("owner")
    n_dp = lax.axis_size("dp")
    n_chip = owner_count // 2
    slot_count = master.shape[0]
    total_slot_count = slot_count * owner_count
    target, source, occupied = slot_layout(owners, slot_count, total_slot_count)
    first_slot = lax.axis_index("owner") * slot_count
    occupied_mine = lax.dynamic_slice_in_dim(occupied, first_slot, slot_count, 0)
    source_mine = lax.dynamic_slice_in_dim(source, first_slot, slot_count, 0)
    grad_sum = all_reduce_blocks(partials[0], n_dp, n_chip)
    mask_mine = (occupied_mine > 0).astype(jnp.float32)[:, None, None]
    gradient = jnp.take(grad_sum, source_mine, axis=0).astype(jnp.float32) * mask_mine
    direction, left_new, right_new, updated = soap_slots(
        gradient, occupied_mine, moment, second, stat_left, stat_right, basis_left, basis_right, master, step_count
    )
    block_count = owners.shape[0]
    count, rows, cols = block_count, updated.shape[1], updated.shape[2]
    per = count // (2 * n_dp)
    rank = target - first_slot
    in_mine = (rank >= 0) & (rank < slot_count)
    dense = jnp.where(
        in_mine[:, None, None], jnp.take(updated, jnp.clip(rank, 0, slot_count - 1), axis=0), 0
    ).astype(jnp.bfloat16)
    replica = lax.axis_index("dp")
    chunks = dense.reshape(2, n_dp, per * rows, cols)
    chunks = lax.dynamic_index_in_dim(chunks, replica, axis=1, keepdims=False)
    weights_all = gather_blocks(chunks, n_dp, n_chip, count).reshape(count, rows, cols)
    return (weights_all, direction, left_new, right_new)


def solution(mesh):
    placed = (
        P(("dp", "owner"), None, None, None),
        P(),
        P(),
        P("owner", None, None),
        P("owner", None, None),
        P("owner", None, None),
        P("owner", None, None),
        P("owner", None, None),
        P("owner", None, None),
        P("owner", None, None),
    )
    return jax.shard_map(
        body,
        mesh=mesh,
        in_specs=placed,
        out_specs=(P(), P("owner", None, None), P("owner", None, None), P("owner", None, None)),
        check_vma=False,
    )
```

```python
import functools

import jax
import jax.numpy as jnp
from jax import lax
from jax.experimental import pallas as pl
from jax.experimental.pallas import tpu as pltpu
from jax.sharding import PartitionSpec as P

MESH = pl.DeviceIdType.MESH

NS_ITERS = 6


def product(left, right):
    return jnp.matmul(left, right, precision=lax.Precision.HIGHEST)


def transposed(array):
    return jnp.swapaxes(array, 1, 2)


def refresh(stat, basis):
    power = product(stat, basis)
    magnitude = jnp.sqrt(jnp.sum(power * power, axis=(1, 2), keepdims=True))
    iterate = power / (magnitude + 1e-06)
    for repeat_count in range(NS_ITERS):
        iterate = 1.5 * iterate - 0.5 * product(iterate, product(transposed(iterate), iterate))
    return iterate


def slot_layout(owners, slot_count, total_slot_count):
    block_count = owners.shape[0]
    slot_position = jnp.arange(block_count, dtype=jnp.int32)
    before = (owners[:, None] == owners[None, :]) & (
        slot_position[:, None] > slot_position[None, :]
    )
    rank_in = jnp.sum(before.astype(jnp.int32), axis=1)
    target = owners * slot_count + rank_in
    matches = (target[:, None] == jnp.arange(total_slot_count, dtype=jnp.int32)[None, :]).astype(
        jnp.int32
    )
    source = jnp.sum(matches * slot_position[:, None], axis=0)
    occupied = jnp.sum(matches, axis=0)
    return (target, source, occupied)


def soap_update(
    gradient, occupied, moment, second, stat_left, stat_right, basis_left, basis_right, step_count
):
    elapsed = step_count[0].astype(jnp.float32)
    moment_new = 0.95 * moment + 0.05 * gradient
    rotated = product(transposed(basis_left), product(gradient, basis_right))
    rot_moment = product(transposed(basis_left), product(moment_new, basis_right))
    second_new = 0.95 * second + 0.05 * rotated * rotated
    correction = 1.0 - jnp.power(jnp.float32(0.95), elapsed)
    scaled = rot_moment / correction / (jnp.sqrt(second_new / correction) + 1e-08)
    occupied_mask = (occupied > 0)[:, None, None]
    direction = jnp.where(
        occupied_mask, product(basis_left, product(scaled, transposed(basis_right))), 0.0
    )
    left_stat = 0.95 * stat_left + 0.05 * product(gradient, transposed(gradient))
    right_stat = 0.95 * stat_right + 0.05 * product(transposed(gradient), gradient)
    left_new = jnp.where(occupied_mask, refresh(left_stat, basis_left), basis_left)
    right_new = jnp.where(occupied_mask, refresh(right_stat, basis_right), basis_right)
    return (direction, left_new, right_new)


def dp_group():
    me = lax.axis_index("dp")
    owner = lax.axis_index("owner")
    return me, lambda j: (j, owner)


def core_group():
    replica = lax.axis_index("dp")
    owner = lax.axis_index("owner")
    me = lax.rem(owner, 2)
    return me, lambda j: (replica, owner - me + j)


def chip_group():
    replica = lax.axis_index("dp")
    owner = lax.axis_index("owner")
    core = lax.rem(owner, 2)
    return lax.div(owner, 2), lambda j: (replica, j * 2 + core)


def enter(groups):
    barrier = pltpu.get_barrier_semaphore()
    total = 0
    for n, me, peer in groups:
        for k in range(1, n):
            pl.semaphore_signal(barrier, inc=1, device_id=peer(lax.rem(me + k, n)), device_id_type=MESH)
        total += n - 1
    pl.semaphore_wait(barrier, total)


def phase(group, source, dest, send, recv):
    n, me, peer = group
    copies = []
    for k in range(1, n):
        other = lax.rem(me + k, n)
        copy = pltpu.make_async_remote_copy(
            src_ref=source(other),
            dst_ref=dest(me),
            send_sem=send.at[k],
            recv_sem=recv.at[k],
            device_id=peer(other),
            device_id_type=MESH,
        )
        copy.start()
        copies.append(copy)
    return copies


def finish(copies):
    for copy in copies:
        copy.wait()


def sum_slots(buf, out, n, rows, start):
    step = 128 if rows % 128 == 0 else rows

    def one(i, carry):
        at = pl.multiple_of(i * step, step)
        total = buf[0, pl.ds(at, step), :].astype(jnp.float32)
        for j in range(1, n):
            total = total + buf[j, pl.ds(at, step), :].astype(jnp.float32)
        out[pl.ds(start + at, step), :] = total.astype(out.dtype)
        return carry

    lax.fori_loop(0, rows // step, one, 0)


def spread_phases(o_ref, core, dp, chip, piece, send, recv, first):
    n_dp, n_chip = dp[0], chip[0]
    c, r, m = core[1], dp[1], chip[1]
    chunk = n_chip * piece
    half = n_dp * chunk
    base = c * half + r * chunk
    finish(phase(chip, lambda j: o_ref.at[pl.ds(base + m * piece, piece)],
                 lambda me: o_ref.at[pl.ds(base + me * piece, piece)], send.at[first], recv.at[first]))
    finish(phase(dp, lambda j: o_ref.at[pl.ds(c * half + r * chunk, chunk)],
                 lambda me: o_ref.at[pl.ds(c * half + me * chunk, chunk)], send.at[first + 1], recv.at[first + 1]))
    finish(phase(core, lambda j: o_ref.at[pl.ds(c * half, half)],
                 lambda me: o_ref.at[pl.ds(me * half, half)], send.at[first + 2], recv.at[first + 2]))


def groups_of(n_dp, n_chip):
    core_me, core_peer = core_group()
    dp_me, dp_peer = dp_group()
    chip_me, chip_peer = chip_group()
    return (2, core_me, core_peer), (n_dp, dp_me, dp_peer), (n_chip, chip_me, chip_peer)


def grad_kernel(n_dp, n_chip, sel, p_ref, o_ref, buf1, hbuf, buf2, mbuf, buf3, held, cube, stage, got, send, recv):
    core, dp, chip = groups_of(n_dp, n_chip)
    enter((core, dp, chip))
    half = p_ref.shape[0] // 2
    chunk = half // n_dp
    piece = chunk // n_chip
    rows = o_ref.shape[0] // sel.shape[1]
    c, r, m = core[1], dp[1], chip[1]
    finish(phase(core, lambda j: p_ref.at[pl.ds(j * half, half)], lambda me: buf1.at[1], send.at[0], recv.at[0]))
    buf1[0] = p_ref[pl.ds(c * half, half), :]
    sum_slots(buf1, hbuf, 2, half, 0)
    buf2[r] = hbuf[pl.ds(r * chunk, chunk), :]
    finish(phase(dp, lambda j: hbuf.at[pl.ds(j * chunk, chunk)], lambda me: buf2.at[me], send.at[1], recv.at[1]))
    sum_slots(buf2, mbuf, n_dp, chunk, 0)
    buf3[m] = mbuf[pl.ds(m * piece, piece), :]
    finish(phase(chip, lambda j: mbuf.at[pl.ds(j * piece, piece)], lambda me: buf3.at[me], send.at[2], recv.at[2]))
    sum_slots(buf3, held, n_chip, piece, r * chunk + m * piece)
    finish(phase(chip, lambda j: held.at[pl.ds(r * chunk + m * piece, piece)],
                 lambda me: held.at[pl.ds(r * chunk + me * piece, piece)], send.at[3], recv.at[3]))
    finish(phase(dp, lambda j: held.at[pl.ds(r * chunk, chunk)],
                 lambda me: held.at[pl.ds(me * chunk, chunk)], send.at[4], recv.at[4]))
    blocks = half // rows

    def to_blocks(i, carry):
        cube[i] = held[pl.ds(pl.multiple_of(i * rows, rows), rows), :]
        return carry

    lax.fori_loop(0, blocks, to_blocks, 0)
    for who, out in ((1, stage), (0, o_ref)):
        for k in range(sel.shape[1]):
            block = sel[who, k] - c * blocks
            inside = (block >= 0) & (block < blocks)
            value = cube[jnp.clip(block, 0, blocks - 1)]
            out[pl.ds(k * rows, rows), :] = jnp.where(inside, value, jnp.zeros_like(value))
    finish(phase(core, lambda j: stage, lambda me: got, send.at[5], recv.at[5]))
    o_ref[...] = o_ref[...] + got[...]


def weight_kernel(n_dp, n_chip, x_ref, o_ref, buf1, pbuf, buf3, send, recv):
    core, dp, chip = groups_of(n_dp, n_chip)
    enter((core, dp, chip))
    chunk = x_ref.shape[1]
    piece = chunk // n_chip
    half = n_dp * chunk
    c, r, m = core[1], dp[1], chip[1]
    finish(phase(core, lambda j: x_ref.at[j], lambda me: buf1.at[1], send.at[0], recv.at[0]))
    buf1[0] = x_ref[c]
    sum_slots(buf1, pbuf, 2, chunk, 0)
    buf3[m] = pbuf[pl.ds(m * piece, piece), :]
    finish(phase(chip, lambda j: pbuf.at[pl.ds(j * piece, piece)], lambda me: buf3.at[me], send.at[1], recv.at[1]))
    sum_slots(buf3, o_ref, n_chip, piece, c * half + r * chunk + m * piece)
    spread_phases(o_ref, core, dp, chip, piece, send, recv, 2)


def params(collective_id):
    return pltpu.CompilerParams(
        collective_id=collective_id, has_side_effects=True, vmem_limit_bytes=48 * 1024 * 1024
    )


def owned_gradient(blocks, sel, n_dp, n_chip):
    count, rows, cols = blocks.shape
    slots = sel.shape[1]
    flat = blocks.reshape(count * rows, cols)
    half = count * rows // 2
    chunk = half // n_dp
    piece = chunk // n_chip
    vmem = pl.BlockSpec(memory_space=pltpu.VMEM)
    out = pl.pallas_call(
        functools.partial(grad_kernel, n_dp, n_chip),
        out_shape=jax.ShapeDtypeStruct((slots * rows, cols), flat.dtype),
        in_specs=[pl.BlockSpec(memory_space=pltpu.SMEM), vmem],
        out_specs=vmem,
        scratch_shapes=[
            pltpu.VMEM((2, half, cols), flat.dtype),
            pltpu.VMEM((half, cols), flat.dtype),
            pltpu.VMEM((n_dp, chunk, cols), flat.dtype),
            pltpu.VMEM((chunk, cols), flat.dtype),
            pltpu.VMEM((n_chip, piece, cols), flat.dtype),
            pltpu.VMEM((half, cols), flat.dtype),
            pltpu.VMEM((half // rows, rows, cols), flat.dtype),
            pltpu.VMEM((slots * rows, cols), flat.dtype),
            pltpu.VMEM((slots * rows, cols), flat.dtype),
            pltpu.SemaphoreType.DMA((6, n_chip)),
            pltpu.SemaphoreType.DMA((6, n_chip)),
        ],
        compiler_params=params(0),
    )(sel, flat)
    return out.reshape(slots, rows, cols)


def gather_blocks(chunks, n_dp, n_chip, count):
    _, chunk, cols = chunks.shape
    piece = chunk // n_chip
    vmem = pl.BlockSpec(memory_space=pltpu.VMEM)
    return pl.pallas_call(
        functools.partial(weight_kernel, n_dp, n_chip),
        out_shape=jax.ShapeDtypeStruct((2 * n_dp * chunk, cols), chunks.dtype),
        in_specs=[vmem],
        out_specs=vmem,
        scratch_shapes=[
            pltpu.VMEM((2, chunk, cols), chunks.dtype),
            pltpu.VMEM((chunk, cols), chunks.dtype),
            pltpu.VMEM((n_chip, piece, cols), chunks.dtype),
            pltpu.SemaphoreType.DMA((5, n_chip)),
            pltpu.SemaphoreType.DMA((5, n_chip)),
        ],
        compiler_params=params(1),
    )(chunks)


def split(a):
    hi = a.astype(jnp.bfloat16)
    lo = (a - hi.astype(jnp.float32)).astype(jnp.bfloat16)
    return hi, lo

def mm3(left, right):
    lh, ll = split(left)
    rh, rl = split(right)
    dot = functools.partial(jnp.dot, preferred_element_type=jnp.float32)
    return dot(lh, rh) + (dot(lh, rl) + dot(ll, rh))

def soap_kernel(scalars, g_ref, m_ref, s_ref, sl_ref, sr_ref, bl_ref, br_ref, w_ref, d_out, l_out, r_out, u_out):
    slots = g_ref.shape[0]
    correction = scalars[0]
    chains = []
    for i in range(slots):
        occupied = scalars[1 + i] > 0
        gradient = g_ref[i]
        basis_left = bl_ref[i]
        basis_right = br_ref[i]
        moment_new = 0.95 * m_ref[i] + 0.05 * gradient
        rotated = mm3(basis_left.T, mm3(gradient, basis_right))
        rot_moment = mm3(basis_left.T, mm3(moment_new, basis_right))
        second_new = 0.95 * s_ref[i] + 0.05 * rotated * rotated
        scaled = rot_moment / correction / (jnp.sqrt(second_new / correction) + 1e-08)
        direction = jnp.where(occupied, mm3(basis_left, mm3(scaled, basis_right.T)), 0.0)
        d_out[i] = direction
        master = w_ref[i]
        u_out[i] = (master - 0.01 * (direction + 0.1 * master)).astype(u_out.dtype)
        left_stat = 0.95 * sl_ref[i] + 0.05 * mm3(gradient, gradient.T)
        right_stat = 0.95 * sr_ref[i] + 0.05 * mm3(gradient.T, gradient)
        chains.append((left_stat, basis_left, l_out, i, occupied))
        chains.append((right_stat, basis_right, r_out, i, occupied))
    iterates = []
    for stat, basis, out, i, occupied in chains:
        power = mm3(stat, basis)
        magnitude = jnp.sqrt(jnp.sum(power * power, keepdims=True))
        iterates.append(power / (magnitude + 1e-06))
    for repeat_count in range(NS_ITERS):
        grams = [mm3(it.T, it) for it in iterates]
        iterates = [1.5 * it - 0.5 * mm3(it, gram) for it, gram in zip(iterates, grams)]
    for (stat, basis, out, i, occupied), it in zip(chains, iterates):
        out[i] = jnp.where(occupied, it, basis)

def soap_slots(gradient, occupied, moment, second, stat_left, stat_right, basis_left, basis_right, master, step_count):
    elapsed = step_count[0].astype(jnp.float32)
    correction = 1.0 - jnp.power(jnp.float32(0.95), elapsed)
    scalars = jnp.concatenate([correction[None], occupied.astype(jnp.float32)])
    vmem = pl.BlockSpec(memory_space=pltpu.VMEM)
    f32 = jax.ShapeDtypeStruct(gradient.shape, jnp.float32)
    return pl.pallas_call(
        soap_kernel,
        out_shape=(f32, f32, f32, jax.ShapeDtypeStruct(gradient.shape, jnp.bfloat16)),
        in_specs=[pl.BlockSpec(memory_space=pltpu.SMEM)] + [vmem] * 8,
        out_specs=(vmem, vmem, vmem, vmem),
    )(scalars, gradient, moment, second, stat_left, stat_right, basis_left, basis_right, master)


def body(
    partials,
    owners,
    step_count,
    master,
    moment,
    second,
    stat_left,
    stat_right,
    basis_left,
    basis_right,
):
    owner_count = lax.axis_size("owner")
    n_dp = lax.axis_size("dp")
    n_chip = owner_count // 2
    slot_count = master.shape[0]
    total_slot_count = slot_count * owner_count
    target, source, occupied = slot_layout(owners, slot_count, total_slot_count)
    first_slot = lax.axis_index("owner") * slot_count
    occupied_mine = lax.dynamic_slice_in_dim(occupied, first_slot, slot_count, 0)
    source_mine = lax.dynamic_slice_in_dim(source, first_slot, slot_count, 0)
    partner_slot = (lax.axis_index("owner") ^ 1) * slot_count
    source_partner = lax.dynamic_slice_in_dim(source, partner_slot, slot_count, 0)
    sel = jnp.stack([source_mine, source_partner]).astype(jnp.int32)
    mask_mine = (occupied_mine > 0).astype(jnp.float32)[:, None, None]
    gradient = owned_gradient(partials[0], sel, n_dp, n_chip).astype(jnp.float32) * mask_mine
    direction, left_new, right_new, updated = soap_slots(
        gradient, occupied_mine, moment, second, stat_left, stat_right, basis_left, basis_right, master, step_count
    )
    block_count = owners.shape[0]
    count, rows, cols = block_count, updated.shape[1], updated.shape[2]
    per = count // (2 * n_dp)
    rank = target - first_slot
    in_mine = (rank >= 0) & (rank < slot_count)
    dense = jnp.where(
        in_mine[:, None, None], jnp.take(updated, jnp.clip(rank, 0, slot_count - 1), axis=0), 0
    ).astype(jnp.bfloat16)
    replica = lax.axis_index("dp")
    chunks = dense.reshape(2, n_dp, per * rows, cols)
    chunks = lax.dynamic_index_in_dim(chunks, replica, axis=1, keepdims=False)
    weights_all = gather_blocks(chunks, n_dp, n_chip, count).reshape(count, rows, cols)
    return (weights_all, direction, left_new, right_new)


def solution(mesh):
    placed = (
        P(("dp", "owner"), None, None, None),
        P(),
        P(),
        P("owner", None, None),
        P("owner", None, None),
        P("owner", None, None),
        P("owner", None, None),
        P("owner", None, None),
        P("owner", None, None),
        P("owner", None, None),
    )
    return jax.shard_map(
        body,
        mesh=mesh,
        in_specs=placed,
        out_specs=(P(), P("owner", None, None), P("owner", None, None), P("owner", None, None)),
        check_vma=False,
    )
```

```python
import functools

import jax
import jax.numpy as jnp
from jax import lax
from jax.experimental import pallas as pl
from jax.experimental.pallas import tpu as pltpu
from jax.sharding import PartitionSpec as P

MESH = pl.DeviceIdType.MESH

NS_ITERS = 6


def product(left, right):
    return jnp.matmul(left, right, precision=lax.Precision.HIGHEST)


def transposed(array):
    return jnp.swapaxes(array, 1, 2)


def refresh(stat, basis):
    power = product(stat, basis)
    magnitude = jnp.sqrt(jnp.sum(power * power, axis=(1, 2), keepdims=True))
    iterate = power / (magnitude + 1e-06)
    for repeat_count in range(NS_ITERS):
        iterate = 1.5 * iterate - 0.5 * product(iterate, product(transposed(iterate), iterate))
    return iterate


def slot_layout(owners, slot_count, total_slot_count):
    block_count = owners.shape[0]
    slot_position = jnp.arange(block_count, dtype=jnp.int32)
    before = (owners[:, None] == owners[None, :]) & (
        slot_position[:, None] > slot_position[None, :]
    )
    rank_in = jnp.sum(before.astype(jnp.int32), axis=1)
    target = owners * slot_count + rank_in
    matches = (target[:, None] == jnp.arange(total_slot_count, dtype=jnp.int32)[None, :]).astype(
        jnp.int32
    )
    source = jnp.sum(matches * slot_position[:, None], axis=0)
    occupied = jnp.sum(matches, axis=0)
    return (target, source, occupied)


def soap_update(
    gradient, occupied, moment, second, stat_left, stat_right, basis_left, basis_right, step_count
):
    elapsed = step_count[0].astype(jnp.float32)
    moment_new = 0.95 * moment + 0.05 * gradient
    rotated = product(transposed(basis_left), product(gradient, basis_right))
    rot_moment = product(transposed(basis_left), product(moment_new, basis_right))
    second_new = 0.95 * second + 0.05 * rotated * rotated
    correction = 1.0 - jnp.power(jnp.float32(0.95), elapsed)
    scaled = rot_moment / correction / (jnp.sqrt(second_new / correction) + 1e-08)
    occupied_mask = (occupied > 0)[:, None, None]
    direction = jnp.where(
        occupied_mask, product(basis_left, product(scaled, transposed(basis_right))), 0.0
    )
    left_stat = 0.95 * stat_left + 0.05 * product(gradient, transposed(gradient))
    right_stat = 0.95 * stat_right + 0.05 * product(transposed(gradient), gradient)
    left_new = jnp.where(occupied_mask, refresh(left_stat, basis_left), basis_left)
    right_new = jnp.where(occupied_mask, refresh(right_stat, basis_right), basis_right)
    return (direction, left_new, right_new)


def dp_group():
    me = lax.axis_index("dp")
    owner = lax.axis_index("owner")
    return me, lambda j: (j, owner)


def core_group():
    replica = lax.axis_index("dp")
    owner = lax.axis_index("owner")
    me = lax.rem(owner, 2)
    return me, lambda j: (replica, owner - me + j)


def chip_group():
    replica = lax.axis_index("dp")
    owner = lax.axis_index("owner")
    core = lax.rem(owner, 2)
    return lax.div(owner, 2), lambda j: (replica, j * 2 + core)


def enter(groups):
    barrier = pltpu.get_barrier_semaphore()
    total = 0
    for n, me, peer in groups:
        for k in range(1, n):
            pl.semaphore_signal(barrier, inc=1, device_id=peer(lax.rem(me + k, n)), device_id_type=MESH)
        total += n - 1
    pl.semaphore_wait(barrier, total)


def phase(group, source, dest, send, recv):
    n, me, peer = group
    copies = []
    for k in range(1, n):
        other = lax.rem(me + k, n)
        copy = pltpu.make_async_remote_copy(
            src_ref=source(other),
            dst_ref=dest(me),
            send_sem=send.at[k],
            recv_sem=recv.at[k],
            device_id=peer(other),
            device_id_type=MESH,
        )
        copy.start()
        copies.append(copy)
    return copies


def finish(copies):
    for copy in copies:
        copy.wait()


def sum_slots(buf, out, n, rows, start):
    step = 128 if rows % 128 == 0 else rows

    def one(i, carry):
        at = pl.multiple_of(i * step, step)
        total = buf[0, pl.ds(at, step), :].astype(jnp.float32)
        for j in range(1, n):
            total = total + buf[j, pl.ds(at, step), :].astype(jnp.float32)
        out[pl.ds(start + at, step), :] = total.astype(out.dtype)
        return carry

    lax.fori_loop(0, rows // step, one, 0)


def spread_phases(o_ref, core, dp, chip, piece, send, recv, first, during):
    n_dp, n_chip = dp[0], chip[0]
    c, r, m = core[1], dp[1], chip[1]
    chunk = n_chip * piece
    half = n_dp * chunk
    base = c * half + r * chunk
    finish(phase(chip, lambda j: o_ref.at[pl.ds(base + m * piece, piece)],
                 lambda me: o_ref.at[pl.ds(base + me * piece, piece)], send.at[first], recv.at[first]))
    copies = phase(dp, lambda j: o_ref.at[pl.ds(c * half + r * chunk, chunk)],
                   lambda me: o_ref.at[pl.ds(c * half + me * chunk, chunk)], send.at[first + 1], recv.at[first + 1])
    during()
    finish(copies)
    finish(phase(core, lambda j: o_ref.at[pl.ds(c * half, half)],
                 lambda me: o_ref.at[pl.ds(me * half, half)], send.at[first + 2], recv.at[first + 2]))


def groups_of(n_dp, n_chip):
    core_me, core_peer = core_group()
    dp_me, dp_peer = dp_group()
    chip_me, chip_peer = chip_group()
    return (2, core_me, core_peer), (n_dp, dp_me, dp_peer), (n_chip, chip_me, chip_peer)


def grad_kernel(n_dp, n_chip, sel, p_ref, o_ref, buf1, hbuf, buf2, mbuf, buf3, held, cube, stage, got, send, recv):
    core, dp, chip = groups_of(n_dp, n_chip)
    enter((core, dp, chip))
    half = p_ref.shape[0] // 2
    chunk = half // n_dp
    piece = chunk // n_chip
    rows = o_ref.shape[0] // sel.shape[1]
    c, r, m = core[1], dp[1], chip[1]
    finish(phase(core, lambda j: p_ref.at[pl.ds(j * half, half)], lambda me: buf1.at[1], send.at[0], recv.at[0]))
    buf1[0] = p_ref[pl.ds(c * half, half), :]
    sum_slots(buf1, hbuf, 2, half, 0)
    buf2[r] = hbuf[pl.ds(r * chunk, chunk), :]
    finish(phase(dp, lambda j: hbuf.at[pl.ds(j * chunk, chunk)], lambda me: buf2.at[me], send.at[1], recv.at[1]))
    sum_slots(buf2, mbuf, n_dp, chunk, 0)
    buf3[m] = mbuf[pl.ds(m * piece, piece), :]
    finish(phase(chip, lambda j: mbuf.at[pl.ds(j * piece, piece)], lambda me: buf3.at[me], send.at[2], recv.at[2]))
    sum_slots(buf3, held, n_chip, piece, r * chunk + m * piece)
    finish(phase(chip, lambda j: held.at[pl.ds(r * chunk + m * piece, piece)],
                 lambda me: held.at[pl.ds(r * chunk + me * piece, piece)], send.at[3], recv.at[3]))
    finish(phase(dp, lambda j: held.at[pl.ds(r * chunk, chunk)],
                 lambda me: held.at[pl.ds(me * chunk, chunk)], send.at[4], recv.at[4]))
    blocks = half // rows

    def to_blocks(i, carry):
        cube[i] = held[pl.ds(pl.multiple_of(i * rows, rows), rows), :]
        return carry

    lax.fori_loop(0, blocks, to_blocks, 0)
    for who, out in ((1, stage), (0, o_ref)):
        for k in range(sel.shape[1]):
            block = sel[who, k] - c * blocks
            inside = (block >= 0) & (block < blocks)
            value = cube[jnp.clip(block, 0, blocks - 1)]
            out[pl.ds(k * rows, rows), :] = jnp.where(inside, value, jnp.zeros_like(value))
    finish(phase(core, lambda j: stage, lambda me: got, send.at[5], recv.at[5]))
    o_ref[...] = o_ref[...] + got[...]


def refresh_slots(scalars, g_ref, sl_ref, sr_ref, bl_ref, br_ref, l_out, r_out):
    chains = []
    for i in range(g_ref.shape[0]):
        occupied = scalars[1 + i] > 0
        gradient = g_ref[i]
        left_stat = 0.95 * sl_ref[i] + 0.05 * mm3(gradient, gradient.T)
        right_stat = 0.95 * sr_ref[i] + 0.05 * mm3(gradient.T, gradient)
        chains.append((left_stat, bl_ref[i], l_out, i, occupied))
        chains.append((right_stat, br_ref[i], r_out, i, occupied))
    iterates = []
    for stat, basis, out, i, occupied in chains:
        power = mm3(stat, basis)
        magnitude = jnp.sqrt(jnp.sum(power * power, keepdims=True))
        iterates.append(power / (magnitude + 1e-06))
    for repeat_count in range(NS_ITERS):
        grams = [mm3(it.T, it) for it in iterates]
        iterates = [1.5 * it - 0.5 * mm3(it, gram) for it, gram in zip(iterates, grams)]
    for (stat, basis, out, i, occupied), it in zip(chains, iterates):
        out[i] = jnp.where(occupied, it, basis)


def weight_kernel(
    n_dp, n_chip, scalars, x_ref, g_ref, sl_ref, sr_ref, bl_ref, br_ref,
    o_ref, l_out, r_out, buf1, pbuf, buf3, send, recv,
):
    core, dp, chip = groups_of(n_dp, n_chip)
    enter((core, dp, chip))
    chunk = x_ref.shape[1]
    piece = chunk // n_chip
    half = n_dp * chunk
    c, r, m = core[1], dp[1], chip[1]
    finish(phase(core, lambda j: x_ref.at[j], lambda me: buf1.at[1], send.at[0], recv.at[0]))
    buf1[0] = x_ref[c]
    sum_slots(buf1, pbuf, 2, chunk, 0)
    buf3[m] = pbuf[pl.ds(m * piece, piece), :]
    finish(phase(chip, lambda j: pbuf.at[pl.ds(j * piece, piece)], lambda me: buf3.at[me], send.at[1], recv.at[1]))
    sum_slots(buf3, o_ref, n_chip, piece, c * half + r * chunk + m * piece)

    def during():
        refresh_slots(scalars, g_ref, sl_ref, sr_ref, bl_ref, br_ref, l_out, r_out)

    spread_phases(o_ref, core, dp, chip, piece, send, recv, 2, during)


def params(collective_id):
    return pltpu.CompilerParams(
        collective_id=collective_id, has_side_effects=True, vmem_limit_bytes=48 * 1024 * 1024
    )


def owned_gradient(blocks, sel, n_dp, n_chip):
    count, rows, cols = blocks.shape
    slots = sel.shape[1]
    flat = blocks.reshape(count * rows, cols)
    half = count * rows // 2
    chunk = half // n_dp
    piece = chunk // n_chip
    vmem = pl.BlockSpec(memory_space=pltpu.VMEM)
    out = pl.pallas_call(
        functools.partial(grad_kernel, n_dp, n_chip),
        out_shape=jax.ShapeDtypeStruct((slots * rows, cols), flat.dtype),
        in_specs=[pl.BlockSpec(memory_space=pltpu.SMEM), vmem],
        out_specs=vmem,
        scratch_shapes=[
            pltpu.VMEM((2, half, cols), flat.dtype),
            pltpu.VMEM((half, cols), flat.dtype),
            pltpu.VMEM((n_dp, chunk, cols), flat.dtype),
            pltpu.VMEM((chunk, cols), flat.dtype),
            pltpu.VMEM((n_chip, piece, cols), flat.dtype),
            pltpu.VMEM((half, cols), flat.dtype),
            pltpu.VMEM((half // rows, rows, cols), flat.dtype),
            pltpu.VMEM((slots * rows, cols), flat.dtype),
            pltpu.VMEM((slots * rows, cols), flat.dtype),
            pltpu.SemaphoreType.DMA((6, n_chip)),
            pltpu.SemaphoreType.DMA((6, n_chip)),
        ],
        compiler_params=params(0),
    )(sel, flat)
    return out.reshape(slots, rows, cols)


def gather_blocks(chunks, n_dp, n_chip, scalars, gradient, stat_left, stat_right, basis_left, basis_right):
    _, chunk, cols = chunks.shape
    piece = chunk // n_chip
    vmem = pl.BlockSpec(memory_space=pltpu.VMEM)
    f32 = jax.ShapeDtypeStruct(gradient.shape, jnp.float32)
    return pl.pallas_call(
        functools.partial(weight_kernel, n_dp, n_chip),
        out_shape=(jax.ShapeDtypeStruct((2 * n_dp * chunk, cols), chunks.dtype), f32, f32),
        in_specs=[pl.BlockSpec(memory_space=pltpu.SMEM)] + [vmem] * 6,
        out_specs=(vmem, vmem, vmem),
        scratch_shapes=[
            pltpu.VMEM((2, chunk, cols), chunks.dtype),
            pltpu.VMEM((chunk, cols), chunks.dtype),
            pltpu.VMEM((n_chip, piece, cols), chunks.dtype),
            pltpu.SemaphoreType.DMA((5, n_chip)),
            pltpu.SemaphoreType.DMA((5, n_chip)),
        ],
        compiler_params=params(1),
    )(scalars, chunks, gradient, stat_left, stat_right, basis_left, basis_right)


def split(a):
    hi = a.astype(jnp.bfloat16)
    lo = (a - hi.astype(jnp.float32)).astype(jnp.bfloat16)
    return hi, lo

def mm3(left, right):
    lh, ll = split(left)
    rh, rl = split(right)
    dot = functools.partial(jnp.dot, preferred_element_type=jnp.float32)
    return dot(lh, rh) + (dot(lh, rl) + dot(ll, rh))

def soap_kernel(scalars, g_ref, m_ref, s_ref, bl_ref, br_ref, w_ref, d_out, u_out):
    slots = g_ref.shape[0]
    correction = scalars[0]
    for i in range(slots):
        occupied = scalars[1 + i] > 0
        gradient = g_ref[i]
        basis_left = bl_ref[i]
        basis_right = br_ref[i]
        moment_new = 0.95 * m_ref[i] + 0.05 * gradient
        rotated = mm3(basis_left.T, mm3(gradient, basis_right))
        rot_moment = mm3(basis_left.T, mm3(moment_new, basis_right))
        second_new = 0.95 * s_ref[i] + 0.05 * rotated * rotated
        scaled = rot_moment / correction / (jnp.sqrt(second_new / correction) + 1e-08)
        direction = jnp.where(occupied, mm3(basis_left, mm3(scaled, basis_right.T)), 0.0)
        d_out[i] = direction
        master = w_ref[i]
        u_out[i] = (master - 0.01 * (direction + 0.1 * master)).astype(u_out.dtype)


def soap_scalars(occupied, step_count):
    elapsed = step_count[0].astype(jnp.float32)
    correction = 1.0 - jnp.power(jnp.float32(0.95), elapsed)
    return jnp.concatenate([correction[None], occupied.astype(jnp.float32)])


def soap_slots(scalars, gradient, moment, second, basis_left, basis_right, master):
    vmem = pl.BlockSpec(memory_space=pltpu.VMEM)
    f32 = jax.ShapeDtypeStruct(gradient.shape, jnp.float32)
    return pl.pallas_call(
        soap_kernel,
        out_shape=(f32, jax.ShapeDtypeStruct(gradient.shape, jnp.bfloat16)),
        in_specs=[pl.BlockSpec(memory_space=pltpu.SMEM)] + [vmem] * 6,
        out_specs=(vmem, vmem),
    )(scalars, gradient, moment, second, basis_left, basis_right, master)


def body(
    partials,
    owners,
    step_count,
    master,
    moment,
    second,
    stat_left,
    stat_right,
    basis_left,
    basis_right,
):
    owner_count = lax.axis_size("owner")
    n_dp = lax.axis_size("dp")
    n_chip = owner_count // 2
    slot_count = master.shape[0]
    total_slot_count = slot_count * owner_count
    target, source, occupied = slot_layout(owners, slot_count, total_slot_count)
    first_slot = lax.axis_index("owner") * slot_count
    occupied_mine = lax.dynamic_slice_in_dim(occupied, first_slot, slot_count, 0)
    source_mine = lax.dynamic_slice_in_dim(source, first_slot, slot_count, 0)
    partner_slot = (lax.axis_index("owner") ^ 1) * slot_count
    source_partner = lax.dynamic_slice_in_dim(source, partner_slot, slot_count, 0)
    sel = jnp.stack([source_mine, source_partner]).astype(jnp.int32)
    mask_mine = (occupied_mine > 0).astype(jnp.float32)[:, None, None]
    gradient = owned_gradient(partials[0], sel, n_dp, n_chip).astype(jnp.float32) * mask_mine
    scalars = soap_scalars(occupied_mine, step_count)
    direction, updated = soap_slots(scalars, gradient, moment, second, basis_left, basis_right, master)
    block_count = owners.shape[0]
    count, rows, cols = block_count, updated.shape[1], updated.shape[2]
    per = count // (2 * n_dp)
    rank = target - first_slot
    in_mine = (rank >= 0) & (rank < slot_count)
    dense = jnp.where(
        in_mine[:, None, None], jnp.take(updated, jnp.clip(rank, 0, slot_count - 1), axis=0), 0
    ).astype(jnp.bfloat16)
    replica = lax.axis_index("dp")
    chunks = dense.reshape(2, n_dp, per * rows, cols)
    chunks = lax.dynamic_index_in_dim(chunks, replica, axis=1, keepdims=False)
    weights_flat, left_new, right_new = gather_blocks(
        chunks, n_dp, n_chip, scalars, gradient, stat_left, stat_right, basis_left, basis_right
    )
    weights_all = weights_flat.reshape(count, rows, cols)
    return (weights_all, direction, left_new, right_new)


def solution(mesh):
    placed = (
        P(("dp", "owner"), None, None, None),
        P(),
        P(),
        P("owner", None, None),
        P("owner", None, None),
        P("owner", None, None),
        P("owner", None, None),
        P("owner", None, None),
        P("owner", None, None),
        P("owner", None, None),
    )
    return jax.shard_map(
        body,
        mesh=mesh,
        in_specs=placed,
        out_specs=(P(), P("owner", None, None), P("owner", None, None), P("owner", None, None)),
        check_vma=False,
    )
```

```python
import functools

import jax
import jax.numpy as jnp
from jax import lax
from jax.experimental import pallas as pl
from jax.experimental.pallas import tpu as pltpu
from jax.sharding import PartitionSpec as P

MESH = pl.DeviceIdType.MESH

NS_ITERS = 6


def product(left, right):
    return jnp.matmul(left, right, precision=lax.Precision.HIGHEST)


def transposed(array):
    return jnp.swapaxes(array, 1, 2)


def refresh(stat, basis):
    power = product(stat, basis)
    magnitude = jnp.sqrt(jnp.sum(power * power, axis=(1, 2), keepdims=True))
    iterate = power / (magnitude + 1e-06)
    for repeat_count in range(NS_ITERS):
        iterate = 1.5 * iterate - 0.5 * product(iterate, product(transposed(iterate), iterate))
    return iterate


def slot_layout(owners, slot_count, total_slot_count):
    block_count = owners.shape[0]
    slot_position = jnp.arange(block_count, dtype=jnp.int32)
    before = (owners[:, None] == owners[None, :]) & (
        slot_position[:, None] > slot_position[None, :]
    )
    rank_in = jnp.sum(before.astype(jnp.int32), axis=1)
    target = owners * slot_count + rank_in
    matches = (target[:, None] == jnp.arange(total_slot_count, dtype=jnp.int32)[None, :]).astype(
        jnp.int32
    )
    source = jnp.sum(matches * slot_position[:, None], axis=0)
    occupied = jnp.sum(matches, axis=0)
    return (target, source, occupied)


def soap_update(
    gradient, occupied, moment, second, stat_left, stat_right, basis_left, basis_right, step_count
):
    elapsed = step_count[0].astype(jnp.float32)
    moment_new = 0.95 * moment + 0.05 * gradient
    rotated = product(transposed(basis_left), product(gradient, basis_right))
    rot_moment = product(transposed(basis_left), product(moment_new, basis_right))
    second_new = 0.95 * second + 0.05 * rotated * rotated
    correction = 1.0 - jnp.power(jnp.float32(0.95), elapsed)
    scaled = rot_moment / correction / (jnp.sqrt(second_new / correction) + 1e-08)
    occupied_mask = (occupied > 0)[:, None, None]
    direction = jnp.where(
        occupied_mask, product(basis_left, product(scaled, transposed(basis_right))), 0.0
    )
    left_stat = 0.95 * stat_left + 0.05 * product(gradient, transposed(gradient))
    right_stat = 0.95 * stat_right + 0.05 * product(transposed(gradient), gradient)
    left_new = jnp.where(occupied_mask, refresh(left_stat, basis_left), basis_left)
    right_new = jnp.where(occupied_mask, refresh(right_stat, basis_right), basis_right)
    return (direction, left_new, right_new)


def dp_group():
    me = lax.axis_index("dp")
    owner = lax.axis_index("owner")
    return me, lambda j: (j, owner)


def core_group():
    replica = lax.axis_index("dp")
    owner = lax.axis_index("owner")
    me = lax.rem(owner, 2)
    return me, lambda j: (replica, owner - me + j)


def chip_group():
    replica = lax.axis_index("dp")
    owner = lax.axis_index("owner")
    core = lax.rem(owner, 2)
    return lax.div(owner, 2), lambda j: (replica, j * 2 + core)


def enter(groups):
    barrier = pltpu.get_barrier_semaphore()
    total = 0
    for n, me, peer in groups:
        for k in range(1, n):
            pl.semaphore_signal(barrier, inc=1, device_id=peer(lax.rem(me + k, n)), device_id_type=MESH)
        total += n - 1
    pl.semaphore_wait(barrier, total)


def phase(group, source, dest, send, recv):
    n, me, peer = group
    copies = []
    for k in range(1, n):
        other = lax.rem(me + k, n)
        copy = pltpu.make_async_remote_copy(
            src_ref=source(other),
            dst_ref=dest(me),
            send_sem=send.at[k],
            recv_sem=recv.at[k],
            device_id=peer(other),
            device_id_type=MESH,
        )
        copy.start()
        copies.append(copy)
    return copies


def finish(copies):
    for copy in copies:
        copy.wait()


def sum_slots(buf, out, n, rows, start):
    step = 128 if rows % 128 == 0 else rows

    def one(i, carry):
        at = pl.multiple_of(i * step, step)
        total = buf[0, pl.ds(at, step), :].astype(jnp.float32)
        for j in range(1, n):
            total = total + buf[j, pl.ds(at, step), :].astype(jnp.float32)
        out[pl.ds(start + at, step), :] = total.astype(out.dtype)
        return carry

    lax.fori_loop(0, rows // step, one, 0)


def spread_phases(o_ref, core, dp, chip, piece, send, recv, first):
    n_dp, n_chip = dp[0], chip[0]
    c, r, m = core[1], dp[1], chip[1]
    chunk = n_chip * piece
    half = n_dp * chunk
    base = c * half + r * chunk
    finish(phase(chip, lambda j: o_ref.at[pl.ds(base + m * piece, piece)],
                 lambda me: o_ref.at[pl.ds(base + me * piece, piece)], send.at[first], recv.at[first]))
    finish(phase(dp, lambda j: o_ref.at[pl.ds(c * half + r * chunk, chunk)],
                 lambda me: o_ref.at[pl.ds(c * half + me * chunk, chunk)], send.at[first + 1], recv.at[first + 1]))
    finish(phase(core, lambda j: o_ref.at[pl.ds(c * half, half)],
                 lambda me: o_ref.at[pl.ds(me * half, half)], send.at[first + 2], recv.at[first + 2]))


def groups_of(n_dp, n_chip):
    core_me, core_peer = core_group()
    dp_me, dp_peer = dp_group()
    chip_me, chip_peer = chip_group()
    return (2, core_me, core_peer), (n_dp, dp_me, dp_peer), (n_chip, chip_me, chip_peer)


def grad_kernel(n_dp, n_chip, sel, p_ref, o_ref, buf1, hbuf, buf2, mbuf, buf3, pair, cube, pay, buf5, send, recv):
    core, dp, chip = groups_of(n_dp, n_chip)
    enter((core, dp, chip))
    half = p_ref.shape[0] // 2
    chunk = half // n_dp
    piece = chunk // n_chip
    rows = cube.shape[1]
    slots = sel.shape[1]
    per = chunk // rows
    share = slots * rows // n_dp
    c, r, m = core[1], dp[1], chip[1]
    finish(phase(core, lambda j: p_ref.at[pl.ds(j * half, half)], lambda me: buf1.at[1], send.at[0], recv.at[0]))
    buf1[0] = p_ref[pl.ds(c * half, half), :]
    sum_slots(buf1, hbuf, 2, half, 0)
    buf2[r] = hbuf[pl.ds(r * chunk, chunk), :]
    finish(phase(dp, lambda j: hbuf.at[pl.ds(j * chunk, chunk)], lambda me: buf2.at[me], send.at[1], recv.at[1]))
    sum_slots(buf2, mbuf, n_dp, chunk, 0)
    buf3[m] = mbuf[pl.ds(m * piece, piece), :]
    finish(phase(chip, lambda j: mbuf.at[pl.ds(j * piece, piece)], lambda me: buf3.at[me], send.at[2], recv.at[2]))
    mine = pair.at[c]
    sum_slots(buf3, mine, n_chip, piece, m * piece)
    finish(phase(chip, lambda j: mine.at[pl.ds(m * piece, piece)],
                 lambda me: mine.at[pl.ds(me * piece, piece)], send.at[3], recv.at[3]))
    finish(phase(core, lambda j: mine, lambda me: pair.at[me], send.at[4], recv.at[4]))
    for h in range(2):
        for i in range(per):
            cube[h * per + i] = pair[h, pl.ds(i * rows, rows), :]
    blocks = half // rows
    for k in range(slots):
        block = sel[0, k]
        side = block // blocks
        within = block - side * blocks
        inside = (within // per) == r
        value = cube[side * per + lax.rem(within, per)]
        pay[pl.ds(k * rows, rows), :] = jnp.where(inside, value, jnp.zeros_like(value))
    buf5[r] = pay[pl.ds(r * share, share), :]
    finish(phase(dp, lambda j: pay.at[pl.ds(j * share, share)], lambda me: buf5.at[me], send.at[5], recv.at[5]))
    sum_slots(buf5, o_ref, n_dp, share, r * share)
    finish(phase(dp, lambda j: o_ref.at[pl.ds(r * share, share)],
                 lambda me: o_ref.at[pl.ds(me * share, share)], send.at[6], recv.at[6]))


def weight_kernel(n_dp, n_chip, x_ref, o_ref, buf1, pbuf, buf3, send, recv):
    core, dp, chip = groups_of(n_dp, n_chip)
    enter((core, dp, chip))
    chunk = x_ref.shape[1]
    piece = chunk // n_chip
    half = n_dp * chunk
    c, r, m = core[1], dp[1], chip[1]
    finish(phase(core, lambda j: x_ref.at[j], lambda me: buf1.at[1], send.at[0], recv.at[0]))
    buf1[0] = x_ref[c]
    sum_slots(buf1, pbuf, 2, chunk, 0)
    buf3[m] = pbuf[pl.ds(m * piece, piece), :]
    finish(phase(chip, lambda j: pbuf.at[pl.ds(j * piece, piece)], lambda me: buf3.at[me], send.at[1], recv.at[1]))
    sum_slots(buf3, o_ref, n_chip, piece, c * half + r * chunk + m * piece)
    spread_phases(o_ref, core, dp, chip, piece, send, recv, 2)


def params(collective_id):
    return pltpu.CompilerParams(
        collective_id=collective_id, has_side_effects=True, vmem_limit_bytes=48 * 1024 * 1024
    )


def owned_gradient(blocks, sel, n_dp, n_chip):
    count, rows, cols = blocks.shape
    slots = sel.shape[1]
    flat = blocks.reshape(count * rows, cols)
    half = count * rows // 2
    chunk = half // n_dp
    piece = chunk // n_chip
    vmem = pl.BlockSpec(memory_space=pltpu.VMEM)
    out = pl.pallas_call(
        functools.partial(grad_kernel, n_dp, n_chip),
        out_shape=jax.ShapeDtypeStruct((slots * rows, cols), flat.dtype),
        in_specs=[pl.BlockSpec(memory_space=pltpu.SMEM), vmem],
        out_specs=vmem,
        scratch_shapes=[
            pltpu.VMEM((2, half, cols), flat.dtype),
            pltpu.VMEM((half, cols), flat.dtype),
            pltpu.VMEM((n_dp, chunk, cols), flat.dtype),
            pltpu.VMEM((chunk, cols), flat.dtype),
            pltpu.VMEM((n_chip, piece, cols), flat.dtype),
            pltpu.VMEM((2, chunk, cols), flat.dtype),
            pltpu.VMEM((2 * chunk // rows, rows, cols), flat.dtype),
            pltpu.VMEM((slots * rows, cols), flat.dtype),
            pltpu.VMEM((n_dp, slots * rows // n_dp, cols), flat.dtype),
            pltpu.SemaphoreType.DMA((7, n_chip)),
            pltpu.SemaphoreType.DMA((7, n_chip)),
        ],
        compiler_params=params(0),
    )(sel, flat)
    return out.reshape(slots, rows, cols)


def gather_blocks(chunks, n_dp, n_chip, count):
    _, chunk, cols = chunks.shape
    piece = chunk // n_chip
    vmem = pl.BlockSpec(memory_space=pltpu.VMEM)
    return pl.pallas_call(
        functools.partial(weight_kernel, n_dp, n_chip),
        out_shape=jax.ShapeDtypeStruct((2 * n_dp * chunk, cols), chunks.dtype),
        in_specs=[vmem],
        out_specs=vmem,
        scratch_shapes=[
            pltpu.VMEM((2, chunk, cols), chunks.dtype),
            pltpu.VMEM((chunk, cols), chunks.dtype),
            pltpu.VMEM((n_chip, piece, cols), chunks.dtype),
            pltpu.SemaphoreType.DMA((5, n_chip)),
            pltpu.SemaphoreType.DMA((5, n_chip)),
        ],
        compiler_params=params(1),
    )(chunks)


def split(a):
    hi = a.astype(jnp.bfloat16)
    lo = (a - hi.astype(jnp.float32)).astype(jnp.bfloat16)
    return hi, lo

def mm3(left, right):
    lh, ll = split(left)
    rh, rl = split(right)
    dot = functools.partial(jnp.dot, preferred_element_type=jnp.float32)
    return dot(lh, rh) + (dot(lh, rl) + dot(ll, rh))

def soap_kernel(scalars, g_ref, m_ref, s_ref, sl_ref, sr_ref, bl_ref, br_ref, w_ref, d_out, l_out, r_out, u_out):
    slots = g_ref.shape[0]
    correction = scalars[0]
    chains = []
    for i in range(slots):
        occupied = scalars[1 + i] > 0
        gradient = g_ref[i]
        basis_left = bl_ref[i]
        basis_right = br_ref[i]
        moment_new = 0.95 * m_ref[i] + 0.05 * gradient
        rotated = mm3(basis_left.T, mm3(gradient, basis_right))
        rot_moment = mm3(basis_left.T, mm3(moment_new, basis_right))
        second_new = 0.95 * s_ref[i] + 0.05 * rotated * rotated
        scaled = rot_moment / correction / (jnp.sqrt(second_new / correction) + 1e-08)
        direction = jnp.where(occupied, mm3(basis_left, mm3(scaled, basis_right.T)), 0.0)
        d_out[i] = direction
        master = w_ref[i]
        u_out[i] = (master - 0.01 * (direction + 0.1 * master)).astype(u_out.dtype)
        left_stat = 0.95 * sl_ref[i] + 0.05 * mm3(gradient, gradient.T)
        right_stat = 0.95 * sr_ref[i] + 0.05 * mm3(gradient.T, gradient)
        chains.append((left_stat, basis_left, l_out, i, occupied))
        chains.append((right_stat, basis_right, r_out, i, occupied))
    iterates = []
    for stat, basis, out, i, occupied in chains:
        power = mm3(stat, basis)
        magnitude = jnp.sqrt(jnp.sum(power * power, keepdims=True))
        iterates.append(power / (magnitude + 1e-06))
    for repeat_count in range(NS_ITERS):
        grams = [mm3(it.T, it) for it in iterates]
        iterates = [1.5 * it - 0.5 * mm3(it, gram) for it, gram in zip(iterates, grams)]
    for (stat, basis, out, i, occupied), it in zip(chains, iterates):
        out[i] = jnp.where(occupied, it, basis)

def soap_slots(gradient, occupied, moment, second, stat_left, stat_right, basis_left, basis_right, master, step_count):
    elapsed = step_count[0].astype(jnp.float32)
    correction = 1.0 - jnp.power(jnp.float32(0.95), elapsed)
    scalars = jnp.concatenate([correction[None], occupied.astype(jnp.float32)])
    vmem = pl.BlockSpec(memory_space=pltpu.VMEM)
    f32 = jax.ShapeDtypeStruct(gradient.shape, jnp.float32)
    return pl.pallas_call(
        soap_kernel,
        out_shape=(f32, f32, f32, jax.ShapeDtypeStruct(gradient.shape, jnp.bfloat16)),
        in_specs=[pl.BlockSpec(memory_space=pltpu.SMEM)] + [vmem] * 8,
        out_specs=(vmem, vmem, vmem, vmem),
    )(scalars, gradient, moment, second, stat_left, stat_right, basis_left, basis_right, master)


def body(
    partials,
    owners,
    step_count,
    master,
    moment,
    second,
    stat_left,
    stat_right,
    basis_left,
    basis_right,
):
    owner_count = lax.axis_size("owner")
    n_dp = lax.axis_size("dp")
    n_chip = owner_count // 2
    slot_count = master.shape[0]
    total_slot_count = slot_count * owner_count
    target, source, occupied = slot_layout(owners, slot_count, total_slot_count)
    first_slot = lax.axis_index("owner") * slot_count
    occupied_mine = lax.dynamic_slice_in_dim(occupied, first_slot, slot_count, 0)
    source_mine = lax.dynamic_slice_in_dim(source, first_slot, slot_count, 0)
    sel = source_mine[None, :].astype(jnp.int32)
    mask_mine = (occupied_mine > 0).astype(jnp.float32)[:, None, None]
    gradient = owned_gradient(partials[0], sel, n_dp, n_chip).astype(jnp.float32) * mask_mine
    direction, left_new, right_new, updated = soap_slots(
        gradient, occupied_mine, moment, second, stat_left, stat_right, basis_left, basis_right, master, step_count
    )
    block_count = owners.shape[0]
    count, rows, cols = block_count, updated.shape[1], updated.shape[2]
    per = count // (2 * n_dp)
    rank = target - first_slot
    in_mine = (rank >= 0) & (rank < slot_count)
    dense = jnp.where(
        in_mine[:, None, None], jnp.take(updated, jnp.clip(rank, 0, slot_count - 1), axis=0), 0
    ).astype(jnp.bfloat16)
    replica = lax.axis_index("dp")
    chunks = dense.reshape(2, n_dp, per * rows, cols)
    chunks = lax.dynamic_index_in_dim(chunks, replica, axis=1, keepdims=False)
    weights_all = gather_blocks(chunks, n_dp, n_chip, count).reshape(count, rows, cols)
    return (weights_all, direction, left_new, right_new)


def solution(mesh):
    placed = (
        P(("dp", "owner"), None, None, None),
        P(),
        P(),
        P("owner", None, None),
        P("owner", None, None),
        P("owner", None, None),
        P("owner", None, None),
        P("owner", None, None),
        P("owner", None, None),
        P("owner", None, None),
    )
    return jax.shard_map(
        body,
        mesh=mesh,
        in_specs=placed,
        out_specs=(P(), P("owner", None, None), P("owner", None, None), P("owner", None, None)),
        check_vma=False,
    )
```

```python
import functools

import jax
import jax.numpy as jnp
from jax import lax
from jax.experimental import pallas as pl
from jax.experimental.pallas import tpu as pltpu
from jax.sharding import PartitionSpec as P

MESH = pl.DeviceIdType.MESH

NS_ITERS = 6


def product(left, right):
    return jnp.matmul(left, right, precision=lax.Precision.HIGHEST)


def transposed(array):
    return jnp.swapaxes(array, 1, 2)


def refresh(stat, basis):
    power = product(stat, basis)
    magnitude = jnp.sqrt(jnp.sum(power * power, axis=(1, 2), keepdims=True))
    iterate = power / (magnitude + 1e-06)
    for repeat_count in range(NS_ITERS):
        iterate = 1.5 * iterate - 0.5 * product(iterate, product(transposed(iterate), iterate))
    return iterate


def slot_layout(owners, slot_count, total_slot_count):
    block_count = owners.shape[0]
    slot_position = jnp.arange(block_count, dtype=jnp.int32)
    before = (owners[:, None] == owners[None, :]) & (
        slot_position[:, None] > slot_position[None, :]
    )
    rank_in = jnp.sum(before.astype(jnp.int32), axis=1)
    target = owners * slot_count + rank_in
    matches = (target[:, None] == jnp.arange(total_slot_count, dtype=jnp.int32)[None, :]).astype(
        jnp.int32
    )
    source = jnp.sum(matches * slot_position[:, None], axis=0)
    occupied = jnp.sum(matches, axis=0)
    return (target, source, occupied)


def soap_update(
    gradient, occupied, moment, second, stat_left, stat_right, basis_left, basis_right, step_count
):
    elapsed = step_count[0].astype(jnp.float32)
    moment_new = 0.95 * moment + 0.05 * gradient
    rotated = product(transposed(basis_left), product(gradient, basis_right))
    rot_moment = product(transposed(basis_left), product(moment_new, basis_right))
    second_new = 0.95 * second + 0.05 * rotated * rotated
    correction = 1.0 - jnp.power(jnp.float32(0.95), elapsed)
    scaled = rot_moment / correction / (jnp.sqrt(second_new / correction) + 1e-08)
    occupied_mask = (occupied > 0)[:, None, None]
    direction = jnp.where(
        occupied_mask, product(basis_left, product(scaled, transposed(basis_right))), 0.0
    )
    left_stat = 0.95 * stat_left + 0.05 * product(gradient, transposed(gradient))
    right_stat = 0.95 * stat_right + 0.05 * product(transposed(gradient), gradient)
    left_new = jnp.where(occupied_mask, refresh(left_stat, basis_left), basis_left)
    right_new = jnp.where(occupied_mask, refresh(right_stat, basis_right), basis_right)
    return (direction, left_new, right_new)


def dp_group():
    me = lax.axis_index("dp")
    owner = lax.axis_index("owner")
    return me, lambda j: (j, owner)


def core_group():
    replica = lax.axis_index("dp")
    owner = lax.axis_index("owner")
    me = lax.rem(owner, 2)
    return me, lambda j: (replica, owner - me + j)


def chip_group():
    replica = lax.axis_index("dp")
    owner = lax.axis_index("owner")
    core = lax.rem(owner, 2)
    return lax.div(owner, 2), lambda j: (replica, j * 2 + core)


def enter(groups):
    barrier = pltpu.get_barrier_semaphore()
    total = 0
    for n, me, peer in groups:
        for k in range(1, n):
            pl.semaphore_signal(barrier, inc=1, device_id=peer(lax.rem(me + k, n)), device_id_type=MESH)
        total += n - 1
    pl.semaphore_wait(barrier, total)


def phase(group, source, dest, send, recv):
    n, me, peer = group
    copies = []
    for k in range(1, n):
        other = lax.rem(me + k, n)
        copy = pltpu.make_async_remote_copy(
            src_ref=source(other),
            dst_ref=dest(me),
            send_sem=send.at[k],
            recv_sem=recv.at[k],
            device_id=peer(other),
            device_id_type=MESH,
        )
        copy.start()
        copies.append(copy)
    return copies


def finish(copies):
    for copy in copies:
        copy.wait()


def sum_slots(buf, out, n, rows, start):
    step = 128 if rows % 128 == 0 else rows

    def one(i, carry):
        at = pl.multiple_of(i * step, step)
        total = buf[0, pl.ds(at, step), :].astype(jnp.float32)
        for j in range(1, n):
            total = total + buf[j, pl.ds(at, step), :].astype(jnp.float32)
        out[pl.ds(start + at, step), :] = total.astype(out.dtype)
        return carry

    lax.fori_loop(0, rows // step, one, 0)


def spread_phases(o_ref, core, dp, chip, piece, send, recv, first):
    n_dp, n_chip = dp[0], chip[0]
    c, r, m = core[1], dp[1], chip[1]
    chunk = n_chip * piece
    half = n_dp * chunk
    base = c * half + r * chunk
    finish(phase(chip, lambda j: o_ref.at[pl.ds(base + m * piece, piece)],
                 lambda me: o_ref.at[pl.ds(base + me * piece, piece)], send.at[first], recv.at[first]))
    copies = phase(dp, lambda j: o_ref.at[pl.ds(c * half + r * chunk, chunk)],
                   lambda me: o_ref.at[pl.ds(c * half + me * chunk, chunk)], send.at[first + 1], recv.at[first + 1])
    partner = core[2](1 - c)
    onward = []
    for k in range(n_dp):
        if k > 0:
            copies[k - 1].wait_recv()
        rows = o_ref.at[pl.ds(c * half + lax.rem(r - k + n_dp, n_dp) * chunk, chunk)]
        copy = pltpu.make_async_remote_copy(
            src_ref=rows,
            dst_ref=rows,
            send_sem=send.at[first + 2, k],
            recv_sem=recv.at[first + 2, k],
            device_id=partner,
            device_id_type=MESH,
        )
        copy.start()
        onward.append(copy)
    for copy in copies:
        copy.wait_send()
    finish(onward)


def groups_of(n_dp, n_chip):
    core_me, core_peer = core_group()
    dp_me, dp_peer = dp_group()
    chip_me, chip_peer = chip_group()
    return (2, core_me, core_peer), (n_dp, dp_me, dp_peer), (n_chip, chip_me, chip_peer)


def grad_kernel(n_dp, n_chip, sel, p_ref, o_ref, buf1, hbuf, buf2, mbuf, buf3, pair, cube, pay, buf5, send, recv):
    core, dp, chip = groups_of(n_dp, n_chip)
    enter((core, dp, chip))
    half = p_ref.shape[0] // 2
    chunk = half // n_dp
    piece = chunk // n_chip
    rows = cube.shape[1]
    slots = sel.shape[1]
    per = chunk // rows
    share = slots * rows // n_dp
    c, r, m = core[1], dp[1], chip[1]
    finish(phase(core, lambda j: p_ref.at[pl.ds(j * half, half)], lambda me: buf1.at[1], send.at[0], recv.at[0]))
    buf1[0] = p_ref[pl.ds(c * half, half), :]
    sum_slots(buf1, hbuf, 2, half, 0)
    buf2[r] = hbuf[pl.ds(r * chunk, chunk), :]
    finish(phase(dp, lambda j: hbuf.at[pl.ds(j * chunk, chunk)], lambda me: buf2.at[me], send.at[1], recv.at[1]))
    sum_slots(buf2, mbuf, n_dp, chunk, 0)
    buf3[m] = mbuf[pl.ds(m * piece, piece), :]
    finish(phase(chip, lambda j: mbuf.at[pl.ds(j * piece, piece)], lambda me: buf3.at[me], send.at[2], recv.at[2]))
    mine = pair.at[c]
    sum_slots(buf3, mine, n_chip, piece, m * piece)
    finish(phase(chip, lambda j: mine.at[pl.ds(m * piece, piece)],
                 lambda me: mine.at[pl.ds(me * piece, piece)], send.at[3], recv.at[3]))
    finish(phase(core, lambda j: mine, lambda me: pair.at[me], send.at[4], recv.at[4]))
    for h in range(2):
        for i in range(per):
            cube[h * per + i] = pair[h, pl.ds(i * rows, rows), :]
    blocks = half // rows
    for k in range(slots):
        block = sel[0, k]
        side = block // blocks
        within = block - side * blocks
        inside = (within // per) == r
        value = cube[side * per + lax.rem(within, per)]
        pay[pl.ds(k * rows, rows), :] = jnp.where(inside, value, jnp.zeros_like(value))
    buf5[r] = pay[pl.ds(r * share, share), :]
    finish(phase(dp, lambda j: pay.at[pl.ds(j * share, share)], lambda me: buf5.at[me], send.at[5], recv.at[5]))
    sum_slots(buf5, o_ref, n_dp, share, r * share)
    finish(phase(dp, lambda j: o_ref.at[pl.ds(r * share, share)],
                 lambda me: o_ref.at[pl.ds(me * share, share)], send.at[6], recv.at[6]))


def weight_kernel(n_dp, n_chip, x_ref, o_ref, buf1, pbuf, buf3, send, recv):
    core, dp, chip = groups_of(n_dp, n_chip)
    enter((core, dp, chip))
    chunk = x_ref.shape[1]
    piece = chunk // n_chip
    half = n_dp * chunk
    c, r, m = core[1], dp[1], chip[1]
    finish(phase(core, lambda j: x_ref.at[j], lambda me: buf1.at[1], send.at[0], recv.at[0]))
    buf1[0] = x_ref[c]
    sum_slots(buf1, pbuf, 2, chunk, 0)
    buf3[m] = pbuf[pl.ds(m * piece, piece), :]
    finish(phase(chip, lambda j: pbuf.at[pl.ds(j * piece, piece)], lambda me: buf3.at[me], send.at[1], recv.at[1]))
    sum_slots(buf3, o_ref, n_chip, piece, c * half + r * chunk + m * piece)
    spread_phases(o_ref, core, dp, chip, piece, send, recv, 2)


def params(collective_id):
    return pltpu.CompilerParams(
        collective_id=collective_id, has_side_effects=True, vmem_limit_bytes=48 * 1024 * 1024
    )


def owned_gradient(blocks, sel, n_dp, n_chip):
    count, rows, cols = blocks.shape
    slots = sel.shape[1]
    flat = blocks.reshape(count * rows, cols)
    half = count * rows // 2
    chunk = half // n_dp
    piece = chunk // n_chip
    vmem = pl.BlockSpec(memory_space=pltpu.VMEM)
    out = pl.pallas_call(
        functools.partial(grad_kernel, n_dp, n_chip),
        out_shape=jax.ShapeDtypeStruct((slots * rows, cols), flat.dtype),
        in_specs=[pl.BlockSpec(memory_space=pltpu.SMEM), vmem],
        out_specs=vmem,
        scratch_shapes=[
            pltpu.VMEM((2, half, cols), flat.dtype),
            pltpu.VMEM((half, cols), flat.dtype),
            pltpu.VMEM((n_dp, chunk, cols), flat.dtype),
            pltpu.VMEM((chunk, cols), flat.dtype),
            pltpu.VMEM((n_chip, piece, cols), flat.dtype),
            pltpu.VMEM((2, chunk, cols), flat.dtype),
            pltpu.VMEM((2 * chunk // rows, rows, cols), flat.dtype),
            pltpu.VMEM((slots * rows, cols), flat.dtype),
            pltpu.VMEM((n_dp, slots * rows // n_dp, cols), flat.dtype),
            pltpu.SemaphoreType.DMA((7, n_chip)),
            pltpu.SemaphoreType.DMA((7, n_chip)),
        ],
        compiler_params=params(0),
    )(sel, flat)
    return out.reshape(slots, rows, cols)


def gather_blocks(chunks, n_dp, n_chip, count):
    _, chunk, cols = chunks.shape
    piece = chunk // n_chip
    vmem = pl.BlockSpec(memory_space=pltpu.VMEM)
    return pl.pallas_call(
        functools.partial(weight_kernel, n_dp, n_chip),
        out_shape=jax.ShapeDtypeStruct((2 * n_dp * chunk, cols), chunks.dtype),
        in_specs=[vmem],
        out_specs=vmem,
        scratch_shapes=[
            pltpu.VMEM((2, chunk, cols), chunks.dtype),
            pltpu.VMEM((chunk, cols), chunks.dtype),
            pltpu.VMEM((n_chip, piece, cols), chunks.dtype),
            pltpu.SemaphoreType.DMA((5, n_chip)),
            pltpu.SemaphoreType.DMA((5, n_chip)),
        ],
        compiler_params=params(1),
    )(chunks)


def split(a):
    hi = a.astype(jnp.bfloat16)
    lo = (a - hi.astype(jnp.float32)).astype(jnp.bfloat16)
    return hi, lo

def mm3(left, right):
    lh, ll = split(left)
    rh, rl = split(right)
    dot = functools.partial(jnp.dot, preferred_element_type=jnp.float32)
    return dot(lh, rh) + (dot(lh, rl) + dot(ll, rh))

def soap_kernel(scalars, g_ref, m_ref, s_ref, sl_ref, sr_ref, bl_ref, br_ref, w_ref, d_out, l_out, r_out, u_out):
    slots = g_ref.shape[0]
    correction = scalars[0]
    chains = []
    for i in range(slots):
        occupied = scalars[1 + i] > 0
        gradient = g_ref[i]
        basis_left = bl_ref[i]
        basis_right = br_ref[i]
        moment_new = 0.95 * m_ref[i] + 0.05 * gradient
        rotated = mm3(basis_left.T, mm3(gradient, basis_right))
        rot_moment = mm3(basis_left.T, mm3(moment_new, basis_right))
        second_new = 0.95 * s_ref[i] + 0.05 * rotated * rotated
        scaled = rot_moment / correction / (jnp.sqrt(second_new / correction) + 1e-08)
        direction = jnp.where(occupied, mm3(basis_left, mm3(scaled, basis_right.T)), 0.0)
        d_out[i] = direction
        master = w_ref[i]
        u_out[i] = (master - 0.01 * (direction + 0.1 * master)).astype(u_out.dtype)
        left_stat = 0.95 * sl_ref[i] + 0.05 * mm3(gradient, gradient.T)
        right_stat = 0.95 * sr_ref[i] + 0.05 * mm3(gradient.T, gradient)
        chains.append((left_stat, basis_left, l_out, i, occupied))
        chains.append((right_stat, basis_right, r_out, i, occupied))
    iterates = []
    for stat, basis, out, i, occupied in chains:
        power = mm3(stat, basis)
        magnitude = jnp.sqrt(jnp.sum(power * power, keepdims=True))
        iterates.append(power / (magnitude + 1e-06))
    for repeat_count in range(NS_ITERS):
        grams = [mm3(it.T, it) for it in iterates]
        iterates = [1.5 * it - 0.5 * mm3(it, gram) for it, gram in zip(iterates, grams)]
    for (stat, basis, out, i, occupied), it in zip(chains, iterates):
        out[i] = jnp.where(occupied, it, basis)

def soap_slots(gradient, occupied, moment, second, stat_left, stat_right, basis_left, basis_right, master, step_count):
    elapsed = step_count[0].astype(jnp.float32)
    correction = 1.0 - jnp.power(jnp.float32(0.95), elapsed)
    scalars = jnp.concatenate([correction[None], occupied.astype(jnp.float32)])
    vmem = pl.BlockSpec(memory_space=pltpu.VMEM)
    f32 = jax.ShapeDtypeStruct(gradient.shape, jnp.float32)
    return pl.pallas_call(
        soap_kernel,
        out_shape=(f32, f32, f32, jax.ShapeDtypeStruct(gradient.shape, jnp.bfloat16)),
        in_specs=[pl.BlockSpec(memory_space=pltpu.SMEM)] + [vmem] * 8,
        out_specs=(vmem, vmem, vmem, vmem),
    )(scalars, gradient, moment, second, stat_left, stat_right, basis_left, basis_right, master)


def body(
    partials,
    owners,
    step_count,
    master,
    moment,
    second,
    stat_left,
    stat_right,
    basis_left,
    basis_right,
):
    owner_count = lax.axis_size("owner")
    n_dp = lax.axis_size("dp")
    n_chip = owner_count // 2
    slot_count = master.shape[0]
    total_slot_count = slot_count * owner_count
    target, source, occupied = slot_layout(owners, slot_count, total_slot_count)
    first_slot = lax.axis_index("owner") * slot_count
    occupied_mine = lax.dynamic_slice_in_dim(occupied, first_slot, slot_count, 0)
    source_mine = lax.dynamic_slice_in_dim(source, first_slot, slot_count, 0)
    sel = source_mine[None, :].astype(jnp.int32)
    mask_mine = (occupied_mine > 0).astype(jnp.float32)[:, None, None]
    gradient = owned_gradient(partials[0], sel, n_dp, n_chip).astype(jnp.float32) * mask_mine
    direction, left_new, right_new, updated = soap_slots(
        gradient, occupied_mine, moment, second, stat_left, stat_right, basis_left, basis_right, master, step_count
    )
    block_count = owners.shape[0]
    count, rows, cols = block_count, updated.shape[1], updated.shape[2]
    per = count // (2 * n_dp)
    rank = target - first_slot
    in_mine = (rank >= 0) & (rank < slot_count)
    dense = jnp.where(
        in_mine[:, None, None], jnp.take(updated, jnp.clip(rank, 0, slot_count - 1), axis=0), 0
    ).astype(jnp.bfloat16)
    replica = lax.axis_index("dp")
    chunks = dense.reshape(2, n_dp, per * rows, cols)
    chunks = lax.dynamic_index_in_dim(chunks, replica, axis=1, keepdims=False)
    weights_all = gather_blocks(chunks, n_dp, n_chip, count).reshape(count, rows, cols)
    return (weights_all, direction, left_new, right_new)


def solution(mesh):
    placed = (
        P(("dp", "owner"), None, None, None),
        P(),
        P(),
        P("owner", None, None),
        P("owner", None, None),
        P("owner", None, None),
        P("owner", None, None),
        P("owner", None, None),
        P("owner", None, None),
        P("owner", None, None),
    )
    return jax.shard_map(
        body,
        mesh=mesh,
        in_specs=placed,
        out_specs=(P(), P("owner", None, None), P("owner", None, None), P("owner", None, None)),
        check_vma=False,
    )
```

```python
import functools

import jax
import jax.numpy as jnp
from jax import lax
from jax.experimental import pallas as pl
from jax.experimental.pallas import tpu as pltpu
from jax.sharding import PartitionSpec as P

MESH = pl.DeviceIdType.MESH

NS_ITERS = 6


def product(left, right):
    return jnp.matmul(left, right, precision=lax.Precision.HIGHEST)


def transposed(array):
    return jnp.swapaxes(array, 1, 2)


def refresh(stat, basis):
    power = product(stat, basis)
    magnitude = jnp.sqrt(jnp.sum(power * power, axis=(1, 2), keepdims=True))
    iterate = power / (magnitude + 1e-06)
    for repeat_count in range(NS_ITERS):
        iterate = 1.5 * iterate - 0.5 * product(iterate, product(transposed(iterate), iterate))
    return iterate


def slot_layout(owners, slot_count, total_slot_count):
    block_count = owners.shape[0]
    slot_position = jnp.arange(block_count, dtype=jnp.int32)
    before = (owners[:, None] == owners[None, :]) & (
        slot_position[:, None] > slot_position[None, :]
    )
    rank_in = jnp.sum(before.astype(jnp.int32), axis=1)
    target = owners * slot_count + rank_in
    matches = (target[:, None] == jnp.arange(total_slot_count, dtype=jnp.int32)[None, :]).astype(
        jnp.int32
    )
    source = jnp.sum(matches * slot_position[:, None], axis=0)
    occupied = jnp.sum(matches, axis=0)
    return (target, source, occupied)


def soap_update(
    gradient, occupied, moment, second, stat_left, stat_right, basis_left, basis_right, step_count
):
    elapsed = step_count[0].astype(jnp.float32)
    moment_new = 0.95 * moment + 0.05 * gradient
    rotated = product(transposed(basis_left), product(gradient, basis_right))
    rot_moment = product(transposed(basis_left), product(moment_new, basis_right))
    second_new = 0.95 * second + 0.05 * rotated * rotated
    correction = 1.0 - jnp.power(jnp.float32(0.95), elapsed)
    scaled = rot_moment / correction / (jnp.sqrt(second_new / correction) + 1e-08)
    occupied_mask = (occupied > 0)[:, None, None]
    direction = jnp.where(
        occupied_mask, product(basis_left, product(scaled, transposed(basis_right))), 0.0
    )
    left_stat = 0.95 * stat_left + 0.05 * product(gradient, transposed(gradient))
    right_stat = 0.95 * stat_right + 0.05 * product(transposed(gradient), gradient)
    left_new = jnp.where(occupied_mask, refresh(left_stat, basis_left), basis_left)
    right_new = jnp.where(occupied_mask, refresh(right_stat, basis_right), basis_right)
    return (direction, left_new, right_new)


def dp_group():
    me = lax.axis_index("dp")
    owner = lax.axis_index("owner")
    return me, lambda j: (j, owner)


def core_group():
    replica = lax.axis_index("dp")
    owner = lax.axis_index("owner")
    me = lax.rem(owner, 2)
    return me, lambda j: (replica, owner - me + j)


def chip_group():
    replica = lax.axis_index("dp")
    owner = lax.axis_index("owner")
    core = lax.rem(owner, 2)
    return lax.div(owner, 2), lambda j: (replica, j * 2 + core)


def enter(groups):
    barrier = pltpu.get_barrier_semaphore()
    total = 0
    for n, me, peer in groups:
        for k in range(1, n):
            pl.semaphore_signal(barrier, inc=1, device_id=peer(lax.rem(me + k, n)), device_id_type=MESH)
        total += n - 1
    pl.semaphore_wait(barrier, total)


def phase(group, source, dest, send, recv):
    n, me, peer = group
    copies = []
    for k in range(1, n):
        other = lax.rem(me + k, n)
        copy = pltpu.make_async_remote_copy(
            src_ref=source(other),
            dst_ref=dest(me),
            send_sem=send.at[k],
            recv_sem=recv.at[k],
            device_id=peer(other),
            device_id_type=MESH,
        )
        copy.start()
        copies.append(copy)
    return copies


def finish(copies):
    for copy in copies:
        copy.wait()


def sum_slots(buf, out, n, rows, start):
    step = 128 if rows % 128 == 0 else rows

    def one(i, carry):
        at = pl.multiple_of(i * step, step)
        total = buf[0, pl.ds(at, step), :].astype(jnp.float32)
        for j in range(1, n):
            total = total + buf[j, pl.ds(at, step), :].astype(jnp.float32)
        out[pl.ds(start + at, step), :] = total.astype(out.dtype)
        return carry

    lax.fori_loop(0, rows // step, one, 0)


def spread_phases(o_ref, core, dp, chip, piece, send, recv, first):
    n_dp, n_chip = dp[0], chip[0]
    c, r, m = core[1], dp[1], chip[1]
    chunk = n_chip * piece
    half = n_dp * chunk
    base = c * half + r * chunk
    finish(phase(chip, lambda j: o_ref.at[pl.ds(base + m * piece, piece)],
                 lambda me: o_ref.at[pl.ds(base + me * piece, piece)], send.at[first], recv.at[first]))
    copies = phase(dp, lambda j: o_ref.at[pl.ds(c * half + r * chunk, chunk)],
                   lambda me: o_ref.at[pl.ds(c * half + me * chunk, chunk)], send.at[first + 1], recv.at[first + 1])
    partner = core[2](1 - c)
    onward = []
    for k in range(n_dp):
        if k > 0:
            copies[k - 1].wait_recv()
        rows = o_ref.at[pl.ds(c * half + lax.rem(r - k + n_dp, n_dp) * chunk, chunk)]
        copy = pltpu.make_async_remote_copy(
            src_ref=rows,
            dst_ref=rows,
            send_sem=send.at[first + 2, k],
            recv_sem=recv.at[first + 2, k],
            device_id=partner,
            device_id_type=MESH,
        )
        copy.start()
        onward.append(copy)
    for copy in copies:
        copy.wait_send()
    finish(onward)


def groups_of(n_dp, n_chip):
    core_me, core_peer = core_group()
    dp_me, dp_peer = dp_group()
    chip_me, chip_peer = chip_group()
    return (2, core_me, core_peer), (n_dp, dp_me, dp_peer), (n_chip, chip_me, chip_peer)


def grad_kernel(n_dp, n_chip, sel, p_ref, o_ref, buf1, hbuf, buf2, mbuf, buf3, pair, cube, pay, buf5, send, recv):
    core, dp, chip = groups_of(n_dp, n_chip)
    enter((core, dp, chip))
    half = p_ref.shape[0] // 2
    chunk = half // n_dp
    piece = chunk // n_chip
    rows = cube.shape[1]
    slots = sel.shape[1]
    per = chunk // rows
    share = slots * rows // n_dp
    c, r, m = core[1], dp[1], chip[1]
    partner = core[2](1 - c)
    order = [lax.rem(r + k, n_dp) for k in range(n_dp)]
    halves = []
    for k in range(n_dp):
        copy = pltpu.make_async_remote_copy(
            src_ref=p_ref.at[pl.ds((1 - c) * half + order[k] * chunk, chunk)],
            dst_ref=buf1.at[pl.ds(order[k] * chunk, chunk)],
            send_sem=send.at[0, k],
            recv_sem=recv.at[0, k],
            device_id=partner,
            device_id_type=MESH,
        )
        copy.start()
        halves.append(copy)
    onward = []
    for k in range(n_dp):
        j = order[k]
        halves[k].wait_recv()
        out, start = (buf2.at[r], 0) if k == 0 else (hbuf, j * chunk)

        def add(i, carry, j=j, out=out, start=start):
            at = pl.multiple_of(i * 128, 128)
            own = p_ref[pl.ds(c * half + j * chunk + at, 128), :].astype(jnp.float32)
            got = buf1[pl.ds(j * chunk + at, 128), :].astype(jnp.float32)
            out[pl.ds(start + at, 128), :] = (own + got).astype(out.dtype)
            return carry

        lax.fori_loop(0, chunk // 128, add, 0)
        if k > 0:
            copy = pltpu.make_async_remote_copy(
                src_ref=hbuf.at[pl.ds(j * chunk, chunk)],
                dst_ref=buf2.at[r],
                send_sem=send.at[1, k],
                recv_sem=recv.at[1, k],
                device_id=dp[2](j),
                device_id_type=MESH,
            )
            copy.start()
            onward.append(copy)
    for copy in halves:
        copy.wait_send()
    finish(onward)
    sum_slots(buf2, mbuf, n_dp, chunk, 0)
    buf3[m] = mbuf[pl.ds(m * piece, piece), :]
    finish(phase(chip, lambda j: mbuf.at[pl.ds(j * piece, piece)], lambda me: buf3.at[me], send.at[2], recv.at[2]))
    mine = pair.at[c]
    sum_slots(buf3, mine, n_chip, piece, m * piece)
    finish(phase(chip, lambda j: mine.at[pl.ds(m * piece, piece)],
                 lambda me: mine.at[pl.ds(me * piece, piece)], send.at[3], recv.at[3]))
    finish(phase(core, lambda j: mine, lambda me: pair.at[me], send.at[4], recv.at[4]))
    for h in range(2):
        for i in range(per):
            cube[h * per + i] = pair[h, pl.ds(i * rows, rows), :]
    blocks = half // rows
    for k in range(slots):
        block = sel[0, k]
        side = block // blocks
        within = block - side * blocks
        inside = (within // per) == r
        value = cube[side * per + lax.rem(within, per)]
        pay[pl.ds(k * rows, rows), :] = jnp.where(inside, value, jnp.zeros_like(value))
    buf5[r] = pay[pl.ds(r * share, share), :]
    finish(phase(dp, lambda j: pay.at[pl.ds(j * share, share)], lambda me: buf5.at[me], send.at[5], recv.at[5]))
    sum_slots(buf5, o_ref, n_dp, share, r * share)
    finish(phase(dp, lambda j: o_ref.at[pl.ds(r * share, share)],
                 lambda me: o_ref.at[pl.ds(me * share, share)], send.at[6], recv.at[6]))


def weight_kernel(n_dp, n_chip, x_ref, o_ref, buf1, pbuf, buf3, send, recv):
    core, dp, chip = groups_of(n_dp, n_chip)
    enter((core, dp, chip))
    chunk = x_ref.shape[1]
    piece = chunk // n_chip
    half = n_dp * chunk
    c, r, m = core[1], dp[1], chip[1]
    finish(phase(core, lambda j: x_ref.at[j], lambda me: buf1.at[1], send.at[0], recv.at[0]))
    buf1[0] = x_ref[c]
    sum_slots(buf1, pbuf, 2, chunk, 0)
    buf3[m] = pbuf[pl.ds(m * piece, piece), :]
    finish(phase(chip, lambda j: pbuf.at[pl.ds(j * piece, piece)], lambda me: buf3.at[me], send.at[1], recv.at[1]))
    sum_slots(buf3, o_ref, n_chip, piece, c * half + r * chunk + m * piece)
    spread_phases(o_ref, core, dp, chip, piece, send, recv, 2)


def params(collective_id):
    return pltpu.CompilerParams(
        collective_id=collective_id, has_side_effects=True, vmem_limit_bytes=48 * 1024 * 1024
    )


def owned_gradient(blocks, sel, n_dp, n_chip):
    count, rows, cols = blocks.shape
    slots = sel.shape[1]
    flat = blocks.reshape(count * rows, cols)
    half = count * rows // 2
    chunk = half // n_dp
    piece = chunk // n_chip
    vmem = pl.BlockSpec(memory_space=pltpu.VMEM)
    out = pl.pallas_call(
        functools.partial(grad_kernel, n_dp, n_chip),
        out_shape=jax.ShapeDtypeStruct((slots * rows, cols), flat.dtype),
        in_specs=[pl.BlockSpec(memory_space=pltpu.SMEM), vmem],
        out_specs=vmem,
        scratch_shapes=[
            pltpu.VMEM((half, cols), flat.dtype),
            pltpu.VMEM((half, cols), flat.dtype),
            pltpu.VMEM((n_dp, chunk, cols), flat.dtype),
            pltpu.VMEM((chunk, cols), flat.dtype),
            pltpu.VMEM((n_chip, piece, cols), flat.dtype),
            pltpu.VMEM((2, chunk, cols), flat.dtype),
            pltpu.VMEM((2 * chunk // rows, rows, cols), flat.dtype),
            pltpu.VMEM((slots * rows, cols), flat.dtype),
            pltpu.VMEM((n_dp, slots * rows // n_dp, cols), flat.dtype),
            pltpu.SemaphoreType.DMA((7, n_chip)),
            pltpu.SemaphoreType.DMA((7, n_chip)),
        ],
        compiler_params=params(0),
    )(sel, flat)
    return out.reshape(slots, rows, cols)


def gather_blocks(chunks, n_dp, n_chip, count):
    _, chunk, cols = chunks.shape
    piece = chunk // n_chip
    vmem = pl.BlockSpec(memory_space=pltpu.VMEM)
    return pl.pallas_call(
        functools.partial(weight_kernel, n_dp, n_chip),
        out_shape=jax.ShapeDtypeStruct((2 * n_dp * chunk, cols), chunks.dtype),
        in_specs=[vmem],
        out_specs=vmem,
        scratch_shapes=[
            pltpu.VMEM((2, chunk, cols), chunks.dtype),
            pltpu.VMEM((chunk, cols), chunks.dtype),
            pltpu.VMEM((n_chip, piece, cols), chunks.dtype),
            pltpu.SemaphoreType.DMA((5, n_chip)),
            pltpu.SemaphoreType.DMA((5, n_chip)),
        ],
        compiler_params=params(1),
    )(chunks)


def split(a):
    hi = a.astype(jnp.bfloat16)
    lo = (a - hi.astype(jnp.float32)).astype(jnp.bfloat16)
    return hi, lo

def mm3(left, right):
    lh, ll = split(left)
    rh, rl = split(right)
    dot = functools.partial(jnp.dot, preferred_element_type=jnp.float32)
    return dot(lh, rh) + (dot(lh, rl) + dot(ll, rh))

def soap_kernel(scalars, g_ref, m_ref, s_ref, sl_ref, sr_ref, bl_ref, br_ref, w_ref, d_out, l_out, r_out, u_out):
    slots = g_ref.shape[0]
    correction = scalars[0]
    chains = []
    for i in range(slots):
        occupied = scalars[1 + i] > 0
        gradient = g_ref[i]
        basis_left = bl_ref[i]
        basis_right = br_ref[i]
        moment_new = 0.95 * m_ref[i] + 0.05 * gradient
        rotated = mm3(basis_left.T, mm3(gradient, basis_right))
        rot_moment = mm3(basis_left.T, mm3(moment_new, basis_right))
        second_new = 0.95 * s_ref[i] + 0.05 * rotated * rotated
        scaled = rot_moment / correction / (jnp.sqrt(second_new / correction) + 1e-08)
        direction = jnp.where(occupied, mm3(basis_left, mm3(scaled, basis_right.T)), 0.0)
        d_out[i] = direction
        master = w_ref[i]
        u_out[i] = (master - 0.01 * (direction + 0.1 * master)).astype(u_out.dtype)
        left_stat = 0.95 * sl_ref[i] + 0.05 * mm3(gradient, gradient.T)
        right_stat = 0.95 * sr_ref[i] + 0.05 * mm3(gradient.T, gradient)
        chains.append((left_stat, basis_left, l_out, i, occupied))
        chains.append((right_stat, basis_right, r_out, i, occupied))
    iterates = []
    for stat, basis, out, i, occupied in chains:
        power = mm3(stat, basis)
        magnitude = jnp.sqrt(jnp.sum(power * power, keepdims=True))
        iterates.append(power / (magnitude + 1e-06))
    for repeat_count in range(NS_ITERS):
        grams = [mm3(it.T, it) for it in iterates]
        iterates = [1.5 * it - 0.5 * mm3(it, gram) for it, gram in zip(iterates, grams)]
    for (stat, basis, out, i, occupied), it in zip(chains, iterates):
        out[i] = jnp.where(occupied, it, basis)

def soap_slots(gradient, occupied, moment, second, stat_left, stat_right, basis_left, basis_right, master, step_count):
    elapsed = step_count[0].astype(jnp.float32)
    correction = 1.0 - jnp.power(jnp.float32(0.95), elapsed)
    scalars = jnp.concatenate([correction[None], occupied.astype(jnp.float32)])
    vmem = pl.BlockSpec(memory_space=pltpu.VMEM)
    f32 = jax.ShapeDtypeStruct(gradient.shape, jnp.float32)
    return pl.pallas_call(
        soap_kernel,
        out_shape=(f32, f32, f32, jax.ShapeDtypeStruct(gradient.shape, jnp.bfloat16)),
        in_specs=[pl.BlockSpec(memory_space=pltpu.SMEM)] + [vmem] * 8,
        out_specs=(vmem, vmem, vmem, vmem),
    )(scalars, gradient, moment, second, stat_left, stat_right, basis_left, basis_right, master)


def body(
    partials,
    owners,
    step_count,
    master,
    moment,
    second,
    stat_left,
    stat_right,
    basis_left,
    basis_right,
):
    owner_count = lax.axis_size("owner")
    n_dp = lax.axis_size("dp")
    n_chip = owner_count // 2
    slot_count = master.shape[0]
    total_slot_count = slot_count * owner_count
    target, source, occupied = slot_layout(owners, slot_count, total_slot_count)
    first_slot = lax.axis_index("owner") * slot_count
    occupied_mine = lax.dynamic_slice_in_dim(occupied, first_slot, slot_count, 0)
    source_mine = lax.dynamic_slice_in_dim(source, first_slot, slot_count, 0)
    sel = source_mine[None, :].astype(jnp.int32)
    mask_mine = (occupied_mine > 0).astype(jnp.float32)[:, None, None]
    gradient = owned_gradient(partials[0], sel, n_dp, n_chip).astype(jnp.float32) * mask_mine
    direction, left_new, right_new, updated = soap_slots(
        gradient, occupied_mine, moment, second, stat_left, stat_right, basis_left, basis_right, master, step_count
    )
    block_count = owners.shape[0]
    count, rows, cols = block_count, updated.shape[1], updated.shape[2]
    per = count // (2 * n_dp)
    rank = target - first_slot
    in_mine = (rank >= 0) & (rank < slot_count)
    dense = jnp.where(
        in_mine[:, None, None], jnp.take(updated, jnp.clip(rank, 0, slot_count - 1), axis=0), 0
    ).astype(jnp.bfloat16)
    replica = lax.axis_index("dp")
    chunks = dense.reshape(2, n_dp, per * rows, cols)
    chunks = lax.dynamic_index_in_dim(chunks, replica, axis=1, keepdims=False)
    weights_all = gather_blocks(chunks, n_dp, n_chip, count).reshape(count, rows, cols)
    return (weights_all, direction, left_new, right_new)


def solution(mesh):
    placed = (
        P(("dp", "owner"), None, None, None),
        P(),
        P(),
        P("owner", None, None),
        P("owner", None, None),
        P("owner", None, None),
        P("owner", None, None),
        P("owner", None, None),
        P("owner", None, None),
        P("owner", None, None),
    )
    return jax.shard_map(
        body,
        mesh=mesh,
        in_specs=placed,
        out_specs=(P(), P("owner", None, None), P("owner", None, None), P("owner", None, None)),
        check_vma=False,
    )
```

```python
import functools

import jax
import jax.numpy as jnp
from jax import lax
from jax.experimental import pallas as pl
from jax.experimental.pallas import tpu as pltpu
from jax.sharding import PartitionSpec as P

MESH = pl.DeviceIdType.MESH

NS_ITERS = 6


def product(left, right):
    return jnp.matmul(left, right, precision=lax.Precision.HIGHEST)


def transposed(array):
    return jnp.swapaxes(array, 1, 2)


def refresh(stat, basis):
    power = product(stat, basis)
    magnitude = jnp.sqrt(jnp.sum(power * power, axis=(1, 2), keepdims=True))
    iterate = power / (magnitude + 1e-06)
    for repeat_count in range(NS_ITERS):
        iterate = 1.5 * iterate - 0.5 * product(iterate, product(transposed(iterate), iterate))
    return iterate


def slot_layout(owners, slot_count, total_slot_count):
    block_count = owners.shape[0]
    slot_position = jnp.arange(block_count, dtype=jnp.int32)
    before = (owners[:, None] == owners[None, :]) & (
        slot_position[:, None] > slot_position[None, :]
    )
    rank_in = jnp.sum(before.astype(jnp.int32), axis=1)
    target = owners * slot_count + rank_in
    matches = (target[:, None] == jnp.arange(total_slot_count, dtype=jnp.int32)[None, :]).astype(
        jnp.int32
    )
    source = jnp.sum(matches * slot_position[:, None], axis=0)
    occupied = jnp.sum(matches, axis=0)
    return (target, source, occupied)


def soap_update(
    gradient, occupied, moment, second, stat_left, stat_right, basis_left, basis_right, step_count
):
    elapsed = step_count[0].astype(jnp.float32)
    moment_new = 0.95 * moment + 0.05 * gradient
    rotated = product(transposed(basis_left), product(gradient, basis_right))
    rot_moment = product(transposed(basis_left), product(moment_new, basis_right))
    second_new = 0.95 * second + 0.05 * rotated * rotated
    correction = 1.0 - jnp.power(jnp.float32(0.95), elapsed)
    scaled = rot_moment / correction / (jnp.sqrt(second_new / correction) + 1e-08)
    occupied_mask = (occupied > 0)[:, None, None]
    direction = jnp.where(
        occupied_mask, product(basis_left, product(scaled, transposed(basis_right))), 0.0
    )
    left_stat = 0.95 * stat_left + 0.05 * product(gradient, transposed(gradient))
    right_stat = 0.95 * stat_right + 0.05 * product(transposed(gradient), gradient)
    left_new = jnp.where(occupied_mask, refresh(left_stat, basis_left), basis_left)
    right_new = jnp.where(occupied_mask, refresh(right_stat, basis_right), basis_right)
    return (direction, left_new, right_new)


def dp_group():
    me = lax.axis_index("dp")
    owner = lax.axis_index("owner")
    return me, lambda j: (j, owner)


def core_group():
    replica = lax.axis_index("dp")
    owner = lax.axis_index("owner")
    me = lax.rem(owner, 2)
    return me, lambda j: (replica, owner - me + j)


def chip_group():
    replica = lax.axis_index("dp")
    owner = lax.axis_index("owner")
    core = lax.rem(owner, 2)
    return lax.div(owner, 2), lambda j: (replica, j * 2 + core)


def enter(groups):
    barrier = pltpu.get_barrier_semaphore()
    total = 0
    for n, me, peer in groups:
        for k in range(1, n):
            pl.semaphore_signal(barrier, inc=1, device_id=peer(lax.rem(me + k, n)), device_id_type=MESH)
        total += n - 1
    pl.semaphore_wait(barrier, total)


def phase(group, source, dest, send, recv):
    n, me, peer = group
    copies = []
    for k in range(1, n):
        other = lax.rem(me + k, n)
        copy = pltpu.make_async_remote_copy(
            src_ref=source(other),
            dst_ref=dest(me),
            send_sem=send.at[k],
            recv_sem=recv.at[k],
            device_id=peer(other),
            device_id_type=MESH,
        )
        copy.start()
        copies.append(copy)
    return copies


def finish(copies):
    for copy in copies:
        copy.wait()


def sum_slots(buf, out, n, rows, start):
    step = 128 if rows % 128 == 0 else rows

    def one(i, carry):
        at = pl.multiple_of(i * step, step)
        total = buf[0, pl.ds(at, step), :].astype(jnp.float32)
        for j in range(1, n):
            total = total + buf[j, pl.ds(at, step), :].astype(jnp.float32)
        out[pl.ds(start + at, step), :] = total.astype(out.dtype)
        return carry

    lax.fori_loop(0, rows // step, one, 0)


def spread_phases(o_ref, core, dp, chip, piece, send, recv, first):
    n_dp, n_chip = dp[0], chip[0]
    c, r, m = core[1], dp[1], chip[1]
    chunk = n_chip * piece
    half = n_dp * chunk
    base = c * half + r * chunk
    finish(phase(chip, lambda j: o_ref.at[pl.ds(base + m * piece, piece)],
                 lambda me: o_ref.at[pl.ds(base + me * piece, piece)], send.at[first], recv.at[first]))
    copies = phase(dp, lambda j: o_ref.at[pl.ds(c * half + r * chunk, chunk)],
                   lambda me: o_ref.at[pl.ds(c * half + me * chunk, chunk)], send.at[first + 1], recv.at[first + 1])
    partner = core[2](1 - c)
    onward = []
    for k in range(n_dp):
        if k > 0:
            copies[k - 1].wait_recv()
        rows = o_ref.at[pl.ds(c * half + lax.rem(r - k + n_dp, n_dp) * chunk, chunk)]
        copy = pltpu.make_async_remote_copy(
            src_ref=rows,
            dst_ref=rows,
            send_sem=send.at[first + 2, k],
            recv_sem=recv.at[first + 2, k],
            device_id=partner,
            device_id_type=MESH,
        )
        copy.start()
        onward.append(copy)
    for copy in copies:
        copy.wait_send()
    finish(onward)


def groups_of(n_dp, n_chip):
    core_me, core_peer = core_group()
    dp_me, dp_peer = dp_group()
    chip_me, chip_peer = chip_group()
    return (2, core_me, core_peer), (n_dp, dp_me, dp_peer), (n_chip, chip_me, chip_peer)


def grad_kernel(n_dp, n_chip, sel, p_ref, o_ref, buf1, hbuf, buf2, mbuf, buf3, pair, cube, pay, buf5, send, recv):
    core, dp, chip = groups_of(n_dp, n_chip)
    enter((core, dp, chip))
    half = p_ref.shape[0] // 2
    chunk = half // n_dp
    piece = chunk // n_chip
    rows = cube.shape[1]
    slots = sel.shape[1]
    per = chunk // rows
    share = slots * rows // n_dp
    c, r, m = core[1], dp[1], chip[1]
    partner = core[2](1 - c)
    order = [lax.rem(r + k, n_dp) for k in range(n_dp)]
    halves = []
    for k in range(n_dp):
        copy = pltpu.make_async_remote_copy(
            src_ref=p_ref.at[pl.ds((1 - c) * half + order[k] * chunk, chunk)],
            dst_ref=buf1.at[pl.ds(order[k] * chunk, chunk)],
            send_sem=send.at[0, k],
            recv_sem=recv.at[0, k],
            device_id=partner,
            device_id_type=MESH,
        )
        copy.start()
        halves.append(copy)
    onward = []
    for k in range(n_dp):
        j = order[k]
        halves[k].wait_recv()
        out, start = (buf2.at[r], 0) if k == 0 else (hbuf, j * chunk)

        def add(i, carry, j=j, out=out, start=start):
            at = pl.multiple_of(i * 128, 128)
            own = p_ref[pl.ds(c * half + j * chunk + at, 128), :].astype(jnp.float32)
            got = buf1[pl.ds(j * chunk + at, 128), :].astype(jnp.float32)
            out[pl.ds(start + at, 128), :] = (own + got).astype(out.dtype)
            return carry

        lax.fori_loop(0, chunk // 128, add, 0)
        if k > 0:
            copy = pltpu.make_async_remote_copy(
                src_ref=hbuf.at[pl.ds(j * chunk, chunk)],
                dst_ref=buf2.at[r],
                send_sem=send.at[1, k],
                recv_sem=recv.at[1, k],
                device_id=dp[2](j),
                device_id_type=MESH,
            )
            copy.start()
            onward.append(copy)
    for copy in halves:
        copy.wait_send()
    finish(onward)
    sum_slots(buf2, mbuf, n_dp, chunk, 0)
    buf3[m] = mbuf[pl.ds(m * piece, piece), :]
    finish(phase(chip, lambda j: mbuf.at[pl.ds(j * piece, piece)], lambda me: buf3.at[me], send.at[2], recv.at[2]))
    mine = pair.at[c]
    sum_slots(buf3, mine, n_chip, piece, m * piece)
    finish(phase(chip, lambda j: mine.at[pl.ds(m * piece, piece)],
                 lambda me: mine.at[pl.ds(me * piece, piece)], send.at[3], recv.at[3]))
    finish(phase(core, lambda j: mine, lambda me: pair.at[me], send.at[4], recv.at[4]))
    for h in range(2):
        for i in range(per):
            cube[h * per + i] = pair[h, pl.ds(i * rows, rows), :]
    blocks = half // rows
    for k in range(slots):
        block = sel[0, k]
        side = block // blocks
        within = block - side * blocks
        inside = (within // per) == r
        value = cube[side * per + lax.rem(within, per)]
        pay[pl.ds(k * rows, rows), :] = jnp.where(inside, value, jnp.zeros_like(value))
    buf5[r] = pay[pl.ds(r * share, share), :]
    finish(phase(dp, lambda j: pay.at[pl.ds(j * share, share)], lambda me: buf5.at[me], send.at[5], recv.at[5]))
    sum_slots(buf5, o_ref, n_dp, share, r * share)
    finish(phase(dp, lambda j: o_ref.at[pl.ds(r * share, share)],
                 lambda me: o_ref.at[pl.ds(me * share, share)], send.at[6], recv.at[6]))


def weight_kernel(n_dp, n_chip, x_ref, o_ref, buf1, pbuf, buf3, send, recv):
    core, dp, chip = groups_of(n_dp, n_chip)
    enter((core, dp, chip))
    chunk = x_ref.shape[1]
    piece = chunk // n_chip
    half = n_dp * chunk
    c, r, m = core[1], dp[1], chip[1]
    finish(phase(core, lambda j: x_ref.at[j], lambda me: buf1.at[1], send.at[0], recv.at[0]))
    buf1[0] = x_ref[c]
    sum_slots(buf1, pbuf, 2, chunk, 0)
    buf3[m] = pbuf[pl.ds(m * piece, piece), :]
    finish(phase(chip, lambda j: pbuf.at[pl.ds(j * piece, piece)], lambda me: buf3.at[me], send.at[1], recv.at[1]))
    sum_slots(buf3, o_ref, n_chip, piece, c * half + r * chunk + m * piece)
    spread_phases(o_ref, core, dp, chip, piece, send, recv, 2)


def params(collective_id):
    return pltpu.CompilerParams(
        collective_id=collective_id, has_side_effects=True, vmem_limit_bytes=48 * 1024 * 1024
    )


def owned_gradient(blocks, sel, n_dp, n_chip):
    count, rows, cols = blocks.shape
    slots = sel.shape[1]
    flat = blocks.reshape(count * rows, cols)
    half = count * rows // 2
    chunk = half // n_dp
    piece = chunk // n_chip
    vmem = pl.BlockSpec(memory_space=pltpu.VMEM)
    out = pl.pallas_call(
        functools.partial(grad_kernel, n_dp, n_chip),
        out_shape=jax.ShapeDtypeStruct((slots * rows, cols), flat.dtype),
        in_specs=[pl.BlockSpec(memory_space=pltpu.SMEM), vmem],
        out_specs=vmem,
        scratch_shapes=[
            pltpu.VMEM((half, cols), flat.dtype),
            pltpu.VMEM((half, cols), flat.dtype),
            pltpu.VMEM((n_dp, chunk, cols), flat.dtype),
            pltpu.VMEM((chunk, cols), flat.dtype),
            pltpu.VMEM((n_chip, piece, cols), flat.dtype),
            pltpu.VMEM((2, chunk, cols), flat.dtype),
            pltpu.VMEM((2 * chunk // rows, rows, cols), flat.dtype),
            pltpu.VMEM((slots * rows, cols), flat.dtype),
            pltpu.VMEM((n_dp, slots * rows // n_dp, cols), flat.dtype),
            pltpu.SemaphoreType.DMA((7, n_chip)),
            pltpu.SemaphoreType.DMA((7, n_chip)),
        ],
        compiler_params=params(0),
    )(sel, flat)
    return out.reshape(slots, rows, cols)


def gather_blocks(chunks, n_dp, n_chip, count):
    _, chunk, cols = chunks.shape
    piece = chunk // n_chip
    vmem = pl.BlockSpec(memory_space=pltpu.VMEM)
    return pl.pallas_call(
        functools.partial(weight_kernel, n_dp, n_chip),
        out_shape=jax.ShapeDtypeStruct((2 * n_dp * chunk, cols), chunks.dtype),
        in_specs=[vmem],
        out_specs=vmem,
        scratch_shapes=[
            pltpu.VMEM((2, chunk, cols), chunks.dtype),
            pltpu.VMEM((chunk, cols), chunks.dtype),
            pltpu.VMEM((n_chip, piece, cols), chunks.dtype),
            pltpu.SemaphoreType.DMA((5, n_chip)),
            pltpu.SemaphoreType.DMA((5, n_chip)),
        ],
        compiler_params=params(1),
    )(chunks)


def split(a):
    hi = a.astype(jnp.bfloat16)
    lo = (a - hi.astype(jnp.float32)).astype(jnp.bfloat16)
    return hi, lo

def mm3(left, right):
    lh, ll = split(left)
    rh, rl = split(right)
    dot = functools.partial(jnp.dot, preferred_element_type=jnp.float32)
    return dot(lh, rh) + (dot(lh, rl) + dot(ll, rh))

def soap_kernel(scalars, pick, g_ref, m_ref, s_ref, sl_ref, sr_ref, bl_ref, br_ref, w_ref, d_out, l_out, r_out, c_out, u_buf):
    slots = g_ref.shape[0]
    correction = scalars[0]
    chains = []
    for i in range(slots):
        occupied = scalars[1 + i] > 0
        gradient = g_ref[i]
        basis_left = bl_ref[i]
        basis_right = br_ref[i]
        moment_new = 0.95 * m_ref[i] + 0.05 * gradient
        rotated = mm3(basis_left.T, mm3(gradient, basis_right))
        rot_moment = mm3(basis_left.T, mm3(moment_new, basis_right))
        second_new = 0.95 * s_ref[i] + 0.05 * rotated * rotated
        scaled = rot_moment / correction / (jnp.sqrt(second_new / correction) + 1e-08)
        direction = jnp.where(occupied, mm3(basis_left, mm3(scaled, basis_right.T)), 0.0)
        d_out[i] = direction
        master = w_ref[i]
        u_buf[i] = (master - 0.01 * (direction + 0.1 * master)).astype(u_buf.dtype)
        left_stat = 0.95 * sl_ref[i] + 0.05 * mm3(gradient, gradient.T)
        right_stat = 0.95 * sr_ref[i] + 0.05 * mm3(gradient.T, gradient)
        chains.append((left_stat, basis_left, l_out, i, occupied))
        chains.append((right_stat, basis_right, r_out, i, occupied))
    iterates = []
    for stat, basis, out, i, occupied in chains:
        power = mm3(stat, basis)
        magnitude = jnp.sqrt(jnp.sum(power * power, keepdims=True))
        iterates.append(power / (magnitude + 1e-06))
    for repeat_count in range(NS_ITERS):
        grams = [mm3(it.T, it) for it in iterates]
        iterates = [1.5 * it - 0.5 * mm3(it, gram) for it, gram in zip(iterates, grams)]
    for (stat, basis, out, i, occupied), it in zip(chains, iterates):
        out[i] = jnp.where(occupied, it, basis)
    halves, rows = c_out.shape[0], g_ref.shape[1]
    for h in range(halves):
        for k in range(c_out.shape[1] // rows):
            index = pick[h * (c_out.shape[1] // rows) + k]
            value = u_buf[jnp.maximum(index, 0)]
            c_out[h, pl.ds(k * rows, rows), :] = jnp.where(index >= 0, value, jnp.zeros_like(value))


def soap_slots(gradient, occupied, pick, moment, second, stat_left, stat_right, basis_left, basis_right, master, step_count):
    slots, rows, cols = gradient.shape
    elapsed = step_count[0].astype(jnp.float32)
    correction = 1.0 - jnp.power(jnp.float32(0.95), elapsed)
    scalars = jnp.concatenate([correction[None], occupied.astype(jnp.float32)])
    vmem = pl.BlockSpec(memory_space=pltpu.VMEM)
    smem = pl.BlockSpec(memory_space=pltpu.SMEM)
    f32 = jax.ShapeDtypeStruct(gradient.shape, jnp.float32)
    chunks = jax.ShapeDtypeStruct((2, pick.shape[0] // 2 * rows, cols), jnp.bfloat16)
    return pl.pallas_call(
        soap_kernel,
        out_shape=(f32, f32, f32, chunks),
        in_specs=[smem, smem] + [vmem] * 8,
        out_specs=(vmem, vmem, vmem, vmem),
        scratch_shapes=[pltpu.VMEM(gradient.shape, jnp.bfloat16)],
    )(scalars, pick, gradient, moment, second, stat_left, stat_right, basis_left, basis_right, master)


def body(
    partials,
    owners,
    step_count,
    master,
    moment,
    second,
    stat_left,
    stat_right,
    basis_left,
    basis_right,
):
    owner_count = lax.axis_size("owner")
    n_dp = lax.axis_size("dp")
    n_chip = owner_count // 2
    slot_count = master.shape[0]
    total_slot_count = slot_count * owner_count
    target, source, occupied = slot_layout(owners, slot_count, total_slot_count)
    first_slot = lax.axis_index("owner") * slot_count
    occupied_mine = lax.dynamic_slice_in_dim(occupied, first_slot, slot_count, 0)
    source_mine = lax.dynamic_slice_in_dim(source, first_slot, slot_count, 0)
    sel = source_mine[None, :].astype(jnp.int32)
    mask_mine = (occupied_mine > 0).astype(jnp.float32)[:, None, None]
    gradient = owned_gradient(partials[0], sel, n_dp, n_chip).astype(jnp.float32) * mask_mine
    block_count = owners.shape[0]
    count, rows, cols = block_count, master.shape[1], master.shape[2]
    per = count // (2 * n_dp)
    replica = lax.axis_index("dp")
    mine = (jnp.arange(2)[:, None] * (count // 2) + replica * per + jnp.arange(per)[None, :]).reshape(-1)
    rank = jnp.take(target, mine) - first_slot
    pick = jnp.where((rank >= 0) & (rank < slot_count), rank, -1).astype(jnp.int32)
    direction, left_new, right_new, chunks = soap_slots(
        gradient, occupied_mine, pick, moment, second, stat_left, stat_right, basis_left, basis_right, master, step_count
    )
    weights_all = gather_blocks(chunks, n_dp, n_chip, count).reshape(count, rows, cols)
    return (weights_all, direction, left_new, right_new)


def solution(mesh):
    placed = (
        P(("dp", "owner"), None, None, None),
        P(),
        P(),
        P("owner", None, None),
        P("owner", None, None),
        P("owner", None, None),
        P("owner", None, None),
        P("owner", None, None),
        P("owner", None, None),
        P("owner", None, None),
    )
    return jax.shard_map(
        body,
        mesh=mesh,
        in_specs=placed,
        out_specs=(P(), P("owner", None, None), P("owner", None, None), P("owner", None, None)),
        check_vma=False,
    )
```

```python
import functools

import jax
import jax.numpy as jnp
from jax import lax
from jax.experimental import pallas as pl
from jax.experimental.pallas import tpu as pltpu
from jax.sharding import PartitionSpec as P

MESH = pl.DeviceIdType.MESH

NS_ITERS = 6


def product(left, right):
    return jnp.matmul(left, right, precision=lax.Precision.HIGHEST)


def transposed(array):
    return jnp.swapaxes(array, 1, 2)


def refresh(stat, basis):
    power = product(stat, basis)
    magnitude = jnp.sqrt(jnp.sum(power * power, axis=(1, 2), keepdims=True))
    iterate = power / (magnitude + 1e-06)
    for repeat_count in range(NS_ITERS):
        iterate = 1.5 * iterate - 0.5 * product(iterate, product(transposed(iterate), iterate))
    return iterate


def slot_layout(owners, slot_count, total_slot_count):
    block_count = owners.shape[0]
    slot_position = jnp.arange(block_count, dtype=jnp.int32)
    before = (owners[:, None] == owners[None, :]) & (
        slot_position[:, None] > slot_position[None, :]
    )
    rank_in = jnp.sum(before.astype(jnp.int32), axis=1)
    target = owners * slot_count + rank_in
    matches = (target[:, None] == jnp.arange(total_slot_count, dtype=jnp.int32)[None, :]).astype(
        jnp.int32
    )
    source = jnp.sum(matches * slot_position[:, None], axis=0)
    occupied = jnp.sum(matches, axis=0)
    return (target, source, occupied)


def soap_update(
    gradient, occupied, moment, second, stat_left, stat_right, basis_left, basis_right, step_count
):
    elapsed = step_count[0].astype(jnp.float32)
    moment_new = 0.95 * moment + 0.05 * gradient
    rotated = product(transposed(basis_left), product(gradient, basis_right))
    rot_moment = product(transposed(basis_left), product(moment_new, basis_right))
    second_new = 0.95 * second + 0.05 * rotated * rotated
    correction = 1.0 - jnp.power(jnp.float32(0.95), elapsed)
    scaled = rot_moment / correction / (jnp.sqrt(second_new / correction) + 1e-08)
    occupied_mask = (occupied > 0)[:, None, None]
    direction = jnp.where(
        occupied_mask, product(basis_left, product(scaled, transposed(basis_right))), 0.0
    )
    left_stat = 0.95 * stat_left + 0.05 * product(gradient, transposed(gradient))
    right_stat = 0.95 * stat_right + 0.05 * product(transposed(gradient), gradient)
    left_new = jnp.where(occupied_mask, refresh(left_stat, basis_left), basis_left)
    right_new = jnp.where(occupied_mask, refresh(right_stat, basis_right), basis_right)
    return (direction, left_new, right_new)


def dp_group():
    me = lax.axis_index("dp")
    owner = lax.axis_index("owner")
    return me, lambda j: (j, owner)


def core_group():
    replica = lax.axis_index("dp")
    owner = lax.axis_index("owner")
    me = lax.rem(owner, 2)
    return me, lambda j: (replica, owner - me + j)


def chip_group():
    replica = lax.axis_index("dp")
    owner = lax.axis_index("owner")
    core = lax.rem(owner, 2)
    return lax.div(owner, 2), lambda j: (replica, j * 2 + core)


def enter(groups):
    barrier = pltpu.get_barrier_semaphore()
    total = 0
    for n, me, peer in groups:
        for k in range(1, n):
            pl.semaphore_signal(barrier, inc=1, device_id=peer(lax.rem(me + k, n)), device_id_type=MESH)
        total += n - 1
    pl.semaphore_wait(barrier, total)


def phase(group, source, dest, send, recv):
    n, me, peer = group
    copies = []
    for k in range(1, n):
        other = lax.rem(me + k, n)
        copy = pltpu.make_async_remote_copy(
            src_ref=source(other),
            dst_ref=dest(me),
            send_sem=send.at[k],
            recv_sem=recv.at[k],
            device_id=peer(other),
            device_id_type=MESH,
        )
        copy.start()
        copies.append(copy)
    return copies


def finish(copies):
    for copy in copies:
        copy.wait()


def sum_slots(buf, out, n, rows, start):
    step = 128 if rows % 128 == 0 else rows

    def one(i, carry):
        at = pl.multiple_of(i * step, step)
        total = buf[0, pl.ds(at, step), :].astype(jnp.float32)
        for j in range(1, n):
            total = total + buf[j, pl.ds(at, step), :].astype(jnp.float32)
        out[pl.ds(start + at, step), :] = total.astype(out.dtype)
        return carry

    lax.fori_loop(0, rows // step, one, 0)


def spread_phases(o_ref, core, dp, chip, piece, send, recv, first):
    n_dp, n_chip = dp[0], chip[0]
    c, r, m = core[1], dp[1], chip[1]
    chunk = n_chip * piece
    half = n_dp * chunk
    base = c * half + r * chunk
    finish(phase(chip, lambda j: o_ref.at[pl.ds(base + m * piece, piece)],
                 lambda me: o_ref.at[pl.ds(base + me * piece, piece)], send.at[first], recv.at[first]))
    copies = phase(dp, lambda j: o_ref.at[pl.ds(c * half + r * chunk, chunk)],
                   lambda me: o_ref.at[pl.ds(c * half + me * chunk, chunk)], send.at[first + 1], recv.at[first + 1])
    partner = core[2](1 - c)
    onward = []
    for k in range(n_dp):
        if k > 0:
            copies[k - 1].wait_recv()
        rows = o_ref.at[pl.ds(c * half + lax.rem(r - k + n_dp, n_dp) * chunk, chunk)]
        copy = pltpu.make_async_remote_copy(
            src_ref=rows,
            dst_ref=rows,
            send_sem=send.at[first + 2, k],
            recv_sem=recv.at[first + 2, k],
            device_id=partner,
            device_id_type=MESH,
        )
        copy.start()
        onward.append(copy)
    for copy in copies:
        copy.wait_send()
    finish(onward)


def groups_of(n_dp, n_chip):
    core_me, core_peer = core_group()
    dp_me, dp_peer = dp_group()
    chip_me, chip_peer = chip_group()
    return (2, core_me, core_peer), (n_dp, dp_me, dp_peer), (n_chip, chip_me, chip_peer)


def grad_kernel(n_dp, n_chip, sel, p_ref, o_ref, buf1, hbuf, buf2, mbuf, buf3, pair, cube, pay, buf5, own_buf, send, recv, local):
    core, dp, chip = groups_of(n_dp, n_chip)
    enter((core, dp, chip))
    half = p_ref.shape[0] // 2
    chunk = half // n_dp
    piece = chunk // n_chip
    rows = cube.shape[1]
    slots = sel.shape[1]
    per = chunk // rows
    share = slots * rows // n_dp
    c, r, m = core[1], dp[1], chip[1]
    partner = core[2](1 - c)
    order = [lax.rem(r + k, n_dp) for k in range(n_dp)]
    halves = []
    for k in range(n_dp):
        copy = pltpu.make_async_remote_copy(
            src_ref=p_ref.at[pl.ds((1 - c) * half + order[k] * chunk, chunk)],
            dst_ref=buf1.at[pl.ds(order[k] * chunk, chunk)],
            send_sem=send.at[0, k],
            recv_sem=recv.at[0, k],
            device_id=partner,
            device_id_type=MESH,
        )
        copy.start()
        halves.append(copy)
    loads = []
    for k in range(n_dp):
        rows_at = pl.ds(c * half + order[k] * chunk, chunk)
        load = pltpu.make_async_copy(p_ref.at[rows_at], own_buf.at[pl.ds(order[k] * chunk, chunk)], local.at[k])
        load.start()
        loads.append(load)
    onward = []
    for k in range(n_dp):
        j = order[k]
        halves[k].wait_recv()
        loads[k].wait()
        out, start = (buf2.at[r], 0) if k == 0 else (hbuf, j * chunk)

        def add(i, carry, j=j, out=out, start=start):
            at = pl.multiple_of(i * 128, 128)
            own = own_buf[pl.ds(j * chunk + at, 128), :].astype(jnp.float32)
            got = buf1[pl.ds(j * chunk + at, 128), :].astype(jnp.float32)
            out[pl.ds(start + at, 128), :] = (own + got).astype(out.dtype)
            return carry

        lax.fori_loop(0, chunk // 128, add, 0)
        if k > 0:
            copy = pltpu.make_async_remote_copy(
                src_ref=hbuf.at[pl.ds(j * chunk, chunk)],
                dst_ref=buf2.at[r],
                send_sem=send.at[1, k],
                recv_sem=recv.at[1, k],
                device_id=dp[2](j),
                device_id_type=MESH,
            )
            copy.start()
            onward.append(copy)
    for copy in halves:
        copy.wait_send()
    finish(onward)
    sum_slots(buf2, mbuf, n_dp, chunk, 0)
    buf3[m] = mbuf[pl.ds(m * piece, piece), :]
    finish(phase(chip, lambda j: mbuf.at[pl.ds(j * piece, piece)], lambda me: buf3.at[me], send.at[2], recv.at[2]))
    mine = pair.at[c]
    sum_slots(buf3, mine, n_chip, piece, m * piece)
    finish(phase(chip, lambda j: mine.at[pl.ds(m * piece, piece)],
                 lambda me: mine.at[pl.ds(me * piece, piece)], send.at[3], recv.at[3]))
    finish(phase(core, lambda j: mine, lambda me: pair.at[me], send.at[4], recv.at[4]))
    for h in range(2):
        for i in range(per):
            cube[h * per + i] = pair[h, pl.ds(i * rows, rows), :]
    blocks = half // rows
    for k in range(slots):
        block = sel[0, k]
        side = block // blocks
        within = block - side * blocks
        inside = (within // per) == r
        value = cube[side * per + lax.rem(within, per)]
        pay[pl.ds(k * rows, rows), :] = jnp.where(inside, value, jnp.zeros_like(value))
    buf5[r] = pay[pl.ds(r * share, share), :]
    finish(phase(dp, lambda j: pay.at[pl.ds(j * share, share)], lambda me: buf5.at[me], send.at[5], recv.at[5]))
    sum_slots(buf5, o_ref, n_dp, share, r * share)
    finish(phase(dp, lambda j: o_ref.at[pl.ds(r * share, share)],
                 lambda me: o_ref.at[pl.ds(me * share, share)], send.at[6], recv.at[6]))


def weight_kernel(n_dp, n_chip, x_ref, o_ref, buf1, pbuf, buf3, send, recv):
    core, dp, chip = groups_of(n_dp, n_chip)
    enter((core, dp, chip))
    chunk = x_ref.shape[1]
    piece = chunk // n_chip
    half = n_dp * chunk
    c, r, m = core[1], dp[1], chip[1]
    finish(phase(core, lambda j: x_ref.at[j], lambda me: buf1.at[1], send.at[0], recv.at[0]))
    buf1[0] = x_ref[c]
    sum_slots(buf1, pbuf, 2, chunk, 0)
    buf3[m] = pbuf[pl.ds(m * piece, piece), :]
    finish(phase(chip, lambda j: pbuf.at[pl.ds(j * piece, piece)], lambda me: buf3.at[me], send.at[1], recv.at[1]))
    sum_slots(buf3, o_ref, n_chip, piece, c * half + r * chunk + m * piece)
    spread_phases(o_ref, core, dp, chip, piece, send, recv, 2)


def params(collective_id):
    return pltpu.CompilerParams(
        collective_id=collective_id, has_side_effects=True, vmem_limit_bytes=48 * 1024 * 1024
    )


def owned_gradient(blocks, sel, n_dp, n_chip):
    count, rows, cols = blocks.shape
    slots = sel.shape[1]
    flat = blocks.reshape(count * rows, cols)
    half = count * rows // 2
    chunk = half // n_dp
    piece = chunk // n_chip
    vmem = pl.BlockSpec(memory_space=pltpu.VMEM)
    out = pl.pallas_call(
        functools.partial(grad_kernel, n_dp, n_chip),
        out_shape=jax.ShapeDtypeStruct((slots * rows, cols), flat.dtype),
        in_specs=[pl.BlockSpec(memory_space=pltpu.SMEM), pl.BlockSpec(memory_space=pl.ANY)],
        out_specs=vmem,
        scratch_shapes=[
            pltpu.VMEM((half, cols), flat.dtype),
            pltpu.VMEM((half, cols), flat.dtype),
            pltpu.VMEM((n_dp, chunk, cols), flat.dtype),
            pltpu.VMEM((chunk, cols), flat.dtype),
            pltpu.VMEM((n_chip, piece, cols), flat.dtype),
            pltpu.VMEM((2, chunk, cols), flat.dtype),
            pltpu.VMEM((2 * chunk // rows, rows, cols), flat.dtype),
            pltpu.VMEM((slots * rows, cols), flat.dtype),
            pltpu.VMEM((n_dp, slots * rows // n_dp, cols), flat.dtype),
            pltpu.VMEM((half, cols), flat.dtype),
            pltpu.SemaphoreType.DMA((7, n_chip)),
            pltpu.SemaphoreType.DMA((7, n_chip)),
            pltpu.SemaphoreType.DMA((n_dp,)),
        ],
        compiler_params=params(0),
    )(sel, flat)
    return out.reshape(slots, rows, cols)


def gather_blocks(chunks, n_dp, n_chip, count):
    _, chunk, cols = chunks.shape
    piece = chunk // n_chip
    vmem = pl.BlockSpec(memory_space=pltpu.VMEM)
    return pl.pallas_call(
        functools.partial(weight_kernel, n_dp, n_chip),
        out_shape=jax.ShapeDtypeStruct((2 * n_dp * chunk, cols), chunks.dtype),
        in_specs=[vmem],
        out_specs=vmem,
        scratch_shapes=[
            pltpu.VMEM((2, chunk, cols), chunks.dtype),
            pltpu.VMEM((chunk, cols), chunks.dtype),
            pltpu.VMEM((n_chip, piece, cols), chunks.dtype),
            pltpu.SemaphoreType.DMA((5, n_chip)),
            pltpu.SemaphoreType.DMA((5, n_chip)),
        ],
        compiler_params=params(1),
    )(chunks)


def split(a):
    hi = a.astype(jnp.bfloat16)
    lo = (a - hi.astype(jnp.float32)).astype(jnp.bfloat16)
    return hi, lo

def mm3(left, right):
    lh, ll = split(left)
    rh, rl = split(right)
    dot = functools.partial(jnp.dot, preferred_element_type=jnp.float32)
    return dot(lh, rh) + (dot(lh, rl) + dot(ll, rh))

def soap_kernel(scalars, pick, g_ref, m_ref, s_ref, sl_ref, sr_ref, bl_ref, br_ref, w_ref, d_out, l_out, r_out, c_out, u_buf):
    slots = g_ref.shape[0]
    correction = scalars[0]
    chains = []
    for i in range(slots):
        occupied = scalars[1 + i] > 0
        gradient = g_ref[i]
        basis_left = bl_ref[i]
        basis_right = br_ref[i]
        moment_new = 0.95 * m_ref[i] + 0.05 * gradient
        rotated = mm3(basis_left.T, mm3(gradient, basis_right))
        rot_moment = mm3(basis_left.T, mm3(moment_new, basis_right))
        second_new = 0.95 * s_ref[i] + 0.05 * rotated * rotated
        scaled = rot_moment / correction / (jnp.sqrt(second_new / correction) + 1e-08)
        direction = jnp.where(occupied, mm3(basis_left, mm3(scaled, basis_right.T)), 0.0)
        d_out[i] = direction
        master = w_ref[i]
        u_buf[i] = (master - 0.01 * (direction + 0.1 * master)).astype(u_buf.dtype)
        left_stat = 0.95 * sl_ref[i] + 0.05 * mm3(gradient, gradient.T)
        right_stat = 0.95 * sr_ref[i] + 0.05 * mm3(gradient.T, gradient)
        chains.append((left_stat, basis_left, l_out, i, occupied))
        chains.append((right_stat, basis_right, r_out, i, occupied))
    iterates = []
    for stat, basis, out, i, occupied in chains:
        power = mm3(stat, basis)
        magnitude = jnp.sqrt(jnp.sum(power * power, keepdims=True))
        iterates.append(power / (magnitude + 1e-06))
    for repeat_count in range(NS_ITERS):
        grams = [mm3(it.T, it) for it in iterates]
        iterates = [1.5 * it - 0.5 * mm3(it, gram) for it, gram in zip(iterates, grams)]
    for (stat, basis, out, i, occupied), it in zip(chains, iterates):
        out[i] = jnp.where(occupied, it, basis)
    halves, rows = c_out.shape[0], g_ref.shape[1]
    for h in range(halves):
        for k in range(c_out.shape[1] // rows):
            index = pick[h * (c_out.shape[1] // rows) + k]
            value = u_buf[jnp.maximum(index, 0)]
            c_out[h, pl.ds(k * rows, rows), :] = jnp.where(index >= 0, value, jnp.zeros_like(value))


def soap_slots(gradient, occupied, pick, moment, second, stat_left, stat_right, basis_left, basis_right, master, step_count):
    slots, rows, cols = gradient.shape
    elapsed = step_count[0].astype(jnp.float32)
    correction = 1.0 - jnp.power(jnp.float32(0.95), elapsed)
    scalars = jnp.concatenate([correction[None], occupied.astype(jnp.float32)])
    vmem = pl.BlockSpec(memory_space=pltpu.VMEM)
    smem = pl.BlockSpec(memory_space=pltpu.SMEM)
    f32 = jax.ShapeDtypeStruct(gradient.shape, jnp.float32)
    chunks = jax.ShapeDtypeStruct((2, pick.shape[0] // 2 * rows, cols), jnp.bfloat16)
    return pl.pallas_call(
        soap_kernel,
        out_shape=(f32, f32, f32, chunks),
        in_specs=[smem, smem] + [vmem] * 8,
        out_specs=(vmem, vmem, vmem, vmem),
        scratch_shapes=[pltpu.VMEM(gradient.shape, jnp.bfloat16)],
    )(scalars, pick, gradient, moment, second, stat_left, stat_right, basis_left, basis_right, master)


def body(
    partials,
    owners,
    step_count,
    master,
    moment,
    second,
    stat_left,
    stat_right,
    basis_left,
    basis_right,
):
    owner_count = lax.axis_size("owner")
    n_dp = lax.axis_size("dp")
    n_chip = owner_count // 2
    slot_count = master.shape[0]
    total_slot_count = slot_count * owner_count
    target, source, occupied = slot_layout(owners, slot_count, total_slot_count)
    first_slot = lax.axis_index("owner") * slot_count
    occupied_mine = lax.dynamic_slice_in_dim(occupied, first_slot, slot_count, 0)
    source_mine = lax.dynamic_slice_in_dim(source, first_slot, slot_count, 0)
    sel = source_mine[None, :].astype(jnp.int32)
    mask_mine = (occupied_mine > 0).astype(jnp.float32)[:, None, None]
    gradient = owned_gradient(partials[0], sel, n_dp, n_chip).astype(jnp.float32) * mask_mine
    block_count = owners.shape[0]
    count, rows, cols = block_count, master.shape[1], master.shape[2]
    per = count // (2 * n_dp)
    replica = lax.axis_index("dp")
    mine = (jnp.arange(2)[:, None] * (count // 2) + replica * per + jnp.arange(per)[None, :]).reshape(-1)
    rank = jnp.take(target, mine) - first_slot
    pick = jnp.where((rank >= 0) & (rank < slot_count), rank, -1).astype(jnp.int32)
    direction, left_new, right_new, chunks = soap_slots(
        gradient, occupied_mine, pick, moment, second, stat_left, stat_right, basis_left, basis_right, master, step_count
    )
    weights_all = gather_blocks(chunks, n_dp, n_chip, count).reshape(count, rows, cols)
    return (weights_all, direction, left_new, right_new)


def solution(mesh):
    placed = (
        P(("dp", "owner"), None, None, None),
        P(),
        P(),
        P("owner", None, None),
        P("owner", None, None),
        P("owner", None, None),
        P("owner", None, None),
        P("owner", None, None),
        P("owner", None, None),
        P("owner", None, None),
    )
    return jax.shard_map(
        body,
        mesh=mesh,
        in_specs=placed,
        out_specs=(P(), P("owner", None, None), P("owner", None, None), P("owner", None, None)),
        check_vma=False,
    )
```

```python
import functools

import jax
import jax.numpy as jnp
from jax import lax
from jax.experimental import pallas as pl
from jax.experimental.pallas import tpu as pltpu
from jax.sharding import PartitionSpec as P

MESH = pl.DeviceIdType.MESH

NS_ITERS = 6


def product(left, right):
    return jnp.matmul(left, right, precision=lax.Precision.HIGHEST)


def transposed(array):
    return jnp.swapaxes(array, 1, 2)


def refresh(stat, basis):
    power = product(stat, basis)
    magnitude = jnp.sqrt(jnp.sum(power * power, axis=(1, 2), keepdims=True))
    iterate = power / (magnitude + 1e-06)
    for repeat_count in range(NS_ITERS):
        iterate = 1.5 * iterate - 0.5 * product(iterate, product(transposed(iterate), iterate))
    return iterate


def slot_layout(owners, slot_count, total_slot_count):
    block_count = owners.shape[0]
    slot_position = jnp.arange(block_count, dtype=jnp.int32)
    before = (owners[:, None] == owners[None, :]) & (
        slot_position[:, None] > slot_position[None, :]
    )
    rank_in = jnp.sum(before.astype(jnp.int32), axis=1)
    target = owners * slot_count + rank_in
    matches = (target[:, None] == jnp.arange(total_slot_count, dtype=jnp.int32)[None, :]).astype(
        jnp.int32
    )
    source = jnp.sum(matches * slot_position[:, None], axis=0)
    occupied = jnp.sum(matches, axis=0)
    return (target, source, occupied)


def soap_update(
    gradient, occupied, moment, second, stat_left, stat_right, basis_left, basis_right, step_count
):
    elapsed = step_count[0].astype(jnp.float32)
    moment_new = 0.95 * moment + 0.05 * gradient
    rotated = product(transposed(basis_left), product(gradient, basis_right))
    rot_moment = product(transposed(basis_left), product(moment_new, basis_right))
    second_new = 0.95 * second + 0.05 * rotated * rotated
    correction = 1.0 - jnp.power(jnp.float32(0.95), elapsed)
    scaled = rot_moment / correction / (jnp.sqrt(second_new / correction) + 1e-08)
    occupied_mask = (occupied > 0)[:, None, None]
    direction = jnp.where(
        occupied_mask, product(basis_left, product(scaled, transposed(basis_right))), 0.0
    )
    left_stat = 0.95 * stat_left + 0.05 * product(gradient, transposed(gradient))
    right_stat = 0.95 * stat_right + 0.05 * product(transposed(gradient), gradient)
    left_new = jnp.where(occupied_mask, refresh(left_stat, basis_left), basis_left)
    right_new = jnp.where(occupied_mask, refresh(right_stat, basis_right), basis_right)
    return (direction, left_new, right_new)


def dp_group():
    me = lax.axis_index("dp")
    owner = lax.axis_index("owner")
    return me, lambda j: (j, owner)


def core_group():
    replica = lax.axis_index("dp")
    owner = lax.axis_index("owner")
    me = lax.rem(owner, 2)
    return me, lambda j: (replica, owner - me + j)


def chip_group():
    replica = lax.axis_index("dp")
    owner = lax.axis_index("owner")
    core = lax.rem(owner, 2)
    return lax.div(owner, 2), lambda j: (replica, j * 2 + core)


def enter(groups):
    barrier = pltpu.get_barrier_semaphore()
    total = 0
    for n, me, peer in groups:
        for k in range(1, n):
            pl.semaphore_signal(barrier, inc=1, device_id=peer(lax.rem(me + k, n)), device_id_type=MESH)
        total += n - 1
    pl.semaphore_wait(barrier, total)


def phase(group, source, dest, send, recv):
    n, me, peer = group
    copies = []
    for k in range(1, n):
        other = lax.rem(me + k, n)
        copy = pltpu.make_async_remote_copy(
            src_ref=source(other),
            dst_ref=dest(me),
            send_sem=send.at[k],
            recv_sem=recv.at[k],
            device_id=peer(other),
            device_id_type=MESH,
        )
        copy.start()
        copies.append(copy)
    return copies


def finish(copies):
    for copy in copies:
        copy.wait()


def sum_slots(buf, out, n, rows, start):
    step = 128 if rows % 128 == 0 else rows

    def one(i, carry):
        at = pl.multiple_of(i * step, step)
        total = buf[0, pl.ds(at, step), :].astype(jnp.float32)
        for j in range(1, n):
            total = total + buf[j, pl.ds(at, step), :].astype(jnp.float32)
        out[pl.ds(start + at, step), :] = total.astype(out.dtype)
        return carry

    lax.fori_loop(0, rows // step, one, 0)


def spread_phases(o_ref, core, dp, chip, piece, send, recv, first):
    n_dp, n_chip = dp[0], chip[0]
    c, r, m = core[1], dp[1], chip[1]
    chunk = n_chip * piece
    half = n_dp * chunk
    base = c * half + r * chunk
    finish(phase(chip, lambda j: o_ref.at[pl.ds(base + m * piece, piece)],
                 lambda me: o_ref.at[pl.ds(base + me * piece, piece)], send.at[first], recv.at[first]))
    copies = phase(dp, lambda j: o_ref.at[pl.ds(c * half + r * chunk, chunk)],
                   lambda me: o_ref.at[pl.ds(c * half + me * chunk, chunk)], send.at[first + 1], recv.at[first + 1])
    partner = core[2](1 - c)
    onward = []
    for k in range(n_dp):
        if k > 0:
            copies[k - 1].wait_recv()
        rows = o_ref.at[pl.ds(c * half + lax.rem(r - k + n_dp, n_dp) * chunk, chunk)]
        copy = pltpu.make_async_remote_copy(
            src_ref=rows,
            dst_ref=rows,
            send_sem=send.at[first + 2, k],
            recv_sem=recv.at[first + 2, k],
            device_id=partner,
            device_id_type=MESH,
        )
        copy.start()
        onward.append(copy)
    for copy in copies:
        copy.wait_send()
    finish(onward)


def groups_of(n_dp, n_chip):
    core_me, core_peer = core_group()
    dp_me, dp_peer = dp_group()
    chip_me, chip_peer = chip_group()
    return (2, core_me, core_peer), (n_dp, dp_me, dp_peer), (n_chip, chip_me, chip_peer)


def grad_kernel(n_dp, n_chip, sel, p_ref, o_ref, buf1, hbuf, buf2, mbuf, buf3, pair, cube, pay, buf5, send, recv):
    core, dp, chip = groups_of(n_dp, n_chip)
    enter((core, dp, chip))
    half = p_ref.shape[0] // 2
    chunk = half // n_dp
    piece = chunk // n_chip
    rows = cube.shape[1]
    slots = sel.shape[1]
    per = chunk // rows
    share = slots * rows // n_dp
    c, r, m = core[1], dp[1], chip[1]
    partner = core[2](1 - c)
    order = [lax.rem(r + k, n_dp) for k in range(n_dp)]
    halves = []
    for k in range(n_dp):
        copy = pltpu.make_async_remote_copy(
            src_ref=p_ref.at[pl.ds((1 - c) * half + order[k] * chunk, chunk)],
            dst_ref=buf1.at[pl.ds(order[k] * chunk, chunk)],
            send_sem=send.at[0, k],
            recv_sem=recv.at[0, k],
            device_id=partner,
            device_id_type=MESH,
        )
        copy.start()
        halves.append(copy)
    onward = []
    for k in range(n_dp):
        j = order[k]
        halves[k].wait_recv()
        out, start = (buf2.at[r], 0) if k == 0 else (hbuf, j * chunk)

        def add(i, carry, j=j, out=out, start=start):
            at = pl.multiple_of(i * 128, 128)
            own = p_ref[pl.ds(c * half + j * chunk + at, 128), :].astype(jnp.float32)
            got = buf1[pl.ds(j * chunk + at, 128), :].astype(jnp.float32)
            out[pl.ds(start + at, 128), :] = (own + got).astype(out.dtype)
            return carry

        lax.fori_loop(0, chunk // 128, add, 0)
        if k > 0:
            copy = pltpu.make_async_remote_copy(
                src_ref=hbuf.at[pl.ds(j * chunk, chunk)],
                dst_ref=buf2.at[r],
                send_sem=send.at[1, k],
                recv_sem=recv.at[1, k],
                device_id=dp[2](j),
                device_id_type=MESH,
            )
            copy.start()
            onward.append(copy)
    for copy in halves:
        copy.wait_send()
    finish(onward)
    sum_slots(buf2, mbuf, n_dp, chunk, 0)
    buf3[m] = mbuf[pl.ds(m * piece, piece), :]
    finish(phase(chip, lambda j: mbuf.at[pl.ds(j * piece, piece)], lambda me: buf3.at[me], send.at[2], recv.at[2]))
    mine = pair.at[c]
    sum_slots(buf3, mine, n_chip, piece, m * piece)
    finish(phase(chip, lambda j: mine.at[pl.ds(m * piece, piece)],
                 lambda me: mine.at[pl.ds(me * piece, piece)], send.at[3], recv.at[3]))
    finish(phase(core, lambda j: mine, lambda me: pair.at[me], send.at[4], recv.at[4]))
    for h in range(2):
        for i in range(per):
            cube[h * per + i] = pair[h, pl.ds(i * rows, rows), :]
    blocks = half // rows
    for k in range(slots):
        block = sel[0, k]
        side = block // blocks
        within = block - side * blocks
        inside = (within // per) == r
        value = cube[side * per + lax.rem(within, per)]
        pay[pl.ds(k * rows, rows), :] = jnp.where(inside, value, jnp.zeros_like(value))
    buf5[r] = pay[pl.ds(r * share, share), :]
    finish(phase(dp, lambda j: pay.at[pl.ds(j * share, share)], lambda me: buf5.at[me], send.at[5], recv.at[5]))
    sum_slots(buf5, o_ref, n_dp, share, r * share)
    finish(phase(dp, lambda j: o_ref.at[pl.ds(r * share, share)],
                 lambda me: o_ref.at[pl.ds(me * share, share)], send.at[6], recv.at[6]))


def weight_kernel(n_dp, n_chip, x_ref, o_ref, buf1, pbuf, buf3, send, recv):
    core, dp, chip = groups_of(n_dp, n_chip)
    enter((core, dp, chip))
    chunk = x_ref.shape[1]
    piece = chunk // n_chip
    half = n_dp * chunk
    c, r, m = core[1], dp[1], chip[1]
    finish(phase(core, lambda j: x_ref.at[j], lambda me: buf1.at[1], send.at[0], recv.at[0]))
    buf1[0] = x_ref[c]
    sum_slots(buf1, pbuf, 2, chunk, 0)
    buf3[m] = pbuf[pl.ds(m * piece, piece), :]
    finish(phase(chip, lambda j: pbuf.at[pl.ds(j * piece, piece)], lambda me: buf3.at[me], send.at[1], recv.at[1]))
    sum_slots(buf3, o_ref, n_chip, piece, c * half + r * chunk + m * piece)
    spread_phases(o_ref, core, dp, chip, piece, send, recv, 2)


def params(collective_id):
    return pltpu.CompilerParams(
        collective_id=collective_id, has_side_effects=True, vmem_limit_bytes=48 * 1024 * 1024
    )


def owned_gradient(blocks, sel, n_dp, n_chip):
    count, rows, cols = blocks.shape
    slots = sel.shape[1]
    flat = blocks.reshape(count * rows, cols)
    half = count * rows // 2
    chunk = half // n_dp
    piece = chunk // n_chip
    vmem = pl.BlockSpec(memory_space=pltpu.VMEM)
    out = pl.pallas_call(
        functools.partial(grad_kernel, n_dp, n_chip),
        out_shape=jax.ShapeDtypeStruct((slots * rows, cols), flat.dtype),
        in_specs=[pl.BlockSpec(memory_space=pltpu.SMEM), vmem],
        out_specs=vmem,
        scratch_shapes=[
            pltpu.VMEM((half, cols), flat.dtype),
            pltpu.VMEM((half, cols), flat.dtype),
            pltpu.VMEM((n_dp, chunk, cols), flat.dtype),
            pltpu.VMEM((chunk, cols), flat.dtype),
            pltpu.VMEM((n_chip, piece, cols), flat.dtype),
            pltpu.VMEM((2, chunk, cols), flat.dtype),
            pltpu.VMEM((2 * chunk // rows, rows, cols), flat.dtype),
            pltpu.VMEM((slots * rows, cols), flat.dtype),
            pltpu.VMEM((n_dp, slots * rows // n_dp, cols), flat.dtype),
            pltpu.SemaphoreType.DMA((7, n_chip)),
            pltpu.SemaphoreType.DMA((7, n_chip)),
        ],
        compiler_params=params(0),
    )(sel, flat)
    return out.reshape(slots, rows, cols)


def gather_blocks(chunks, n_dp, n_chip, count):
    _, chunk, cols = chunks.shape
    piece = chunk // n_chip
    vmem = pl.BlockSpec(memory_space=pltpu.VMEM)
    return pl.pallas_call(
        functools.partial(weight_kernel, n_dp, n_chip),
        out_shape=jax.ShapeDtypeStruct((2 * n_dp * chunk, cols), chunks.dtype),
        in_specs=[vmem],
        out_specs=vmem,
        scratch_shapes=[
            pltpu.VMEM((2, chunk, cols), chunks.dtype),
            pltpu.VMEM((chunk, cols), chunks.dtype),
            pltpu.VMEM((n_chip, piece, cols), chunks.dtype),
            pltpu.SemaphoreType.DMA((5, n_chip)),
            pltpu.SemaphoreType.DMA((5, n_chip)),
        ],
        compiler_params=params(1),
    )(chunks)


def split(a):
    hi = a.astype(jnp.bfloat16)
    lo = (a - hi.astype(jnp.float32)).astype(jnp.bfloat16)
    return hi, lo

def mm3(left, right):
    lh, ll = split(left)
    rh, rl = split(right)
    dot = functools.partial(jnp.dot, preferred_element_type=jnp.float32)
    return dot(lh, rh) + (dot(lh, rl) + dot(ll, rh))

def soap_kernel(scalars, pick, g_ref, m_ref, s_ref, sl_ref, sr_ref, bl_ref, br_ref, w_ref, d_out, l_out, r_out, c_out, u_buf):
    slots = g_ref.shape[0]
    correction = scalars[0]
    chains = []
    for i in range(slots):
        occupied = scalars[1 + i] > 0
        gradient = g_ref[i].astype(jnp.float32) * scalars[1 + i]
        basis_left = bl_ref[i]
        basis_right = br_ref[i]
        moment_new = 0.95 * m_ref[i] + 0.05 * gradient
        rotated = mm3(basis_left.T, mm3(gradient, basis_right))
        rot_moment = mm3(basis_left.T, mm3(moment_new, basis_right))
        second_new = 0.95 * s_ref[i] + 0.05 * rotated * rotated
        scaled = rot_moment / correction / (jnp.sqrt(second_new / correction) + 1e-08)
        direction = jnp.where(occupied, mm3(basis_left, mm3(scaled, basis_right.T)), 0.0)
        d_out[i] = direction
        master = w_ref[i]
        u_buf[i] = (master - 0.01 * (direction + 0.1 * master)).astype(u_buf.dtype)
        left_stat = 0.95 * sl_ref[i] + 0.05 * mm3(gradient, gradient.T)
        right_stat = 0.95 * sr_ref[i] + 0.05 * mm3(gradient.T, gradient)
        chains.append((left_stat, basis_left, l_out, i, occupied))
        chains.append((right_stat, basis_right, r_out, i, occupied))
    iterates = []
    for stat, basis, out, i, occupied in chains:
        power = mm3(stat, basis)
        magnitude = jnp.sqrt(jnp.sum(power * power, keepdims=True))
        iterates.append(power / (magnitude + 1e-06))
    for repeat_count in range(NS_ITERS):
        grams = [mm3(it.T, it) for it in iterates]
        iterates = [1.5 * it - 0.5 * mm3(it, gram) for it, gram in zip(iterates, grams)]
    for (stat, basis, out, i, occupied), it in zip(chains, iterates):
        out[i] = jnp.where(occupied, it, basis)
    halves, rows = c_out.shape[0], g_ref.shape[1]
    for h in range(halves):
        for k in range(c_out.shape[1] // rows):
            index = pick[h * (c_out.shape[1] // rows) + k]
            value = u_buf[jnp.maximum(index, 0)]
            c_out[h, pl.ds(k * rows, rows), :] = jnp.where(index >= 0, value, jnp.zeros_like(value))


def soap_slots(gradient, occupied, pick, moment, second, stat_left, stat_right, basis_left, basis_right, master, step_count):
    slots, rows, cols = gradient.shape
    elapsed = step_count[0].astype(jnp.float32)
    correction = 1.0 - jnp.power(jnp.float32(0.95), elapsed)
    scalars = jnp.concatenate([correction[None], (occupied > 0).astype(jnp.float32)])
    vmem = pl.BlockSpec(memory_space=pltpu.VMEM)
    smem = pl.BlockSpec(memory_space=pltpu.SMEM)
    f32 = jax.ShapeDtypeStruct(gradient.shape, jnp.float32)
    chunks = jax.ShapeDtypeStruct((2, pick.shape[0] // 2 * rows, cols), jnp.bfloat16)
    return pl.pallas_call(
        soap_kernel,
        out_shape=(f32, f32, f32, chunks),
        in_specs=[smem, smem] + [vmem] * 8,
        out_specs=(vmem, vmem, vmem, vmem),
        scratch_shapes=[pltpu.VMEM(gradient.shape, jnp.bfloat16)],
    )(scalars, pick, gradient, moment, second, stat_left, stat_right, basis_left, basis_right, master)


def body(
    partials,
    owners,
    step_count,
    master,
    moment,
    second,
    stat_left,
    stat_right,
    basis_left,
    basis_right,
):
    owner_count = lax.axis_size("owner")
    n_dp = lax.axis_size("dp")
    n_chip = owner_count // 2
    slot_count = master.shape[0]
    total_slot_count = slot_count * owner_count
    target, source, occupied = slot_layout(owners, slot_count, total_slot_count)
    first_slot = lax.axis_index("owner") * slot_count
    occupied_mine = lax.dynamic_slice_in_dim(occupied, first_slot, slot_count, 0)
    source_mine = lax.dynamic_slice_in_dim(source, first_slot, slot_count, 0)
    sel = source_mine[None, :].astype(jnp.int32)
    gradient = owned_gradient(partials[0], sel, n_dp, n_chip)
    block_count = owners.shape[0]
    count, rows, cols = block_count, master.shape[1], master.shape[2]
    per = count // (2 * n_dp)
    replica = lax.axis_index("dp")
    mine = (jnp.arange(2)[:, None] * (count // 2) + replica * per + jnp.arange(per)[None, :]).reshape(-1)
    rank = jnp.take(target, mine) - first_slot
    pick = jnp.where((rank >= 0) & (rank < slot_count), rank, -1).astype(jnp.int32)
    direction, left_new, right_new, chunks = soap_slots(
        gradient, occupied_mine, pick, moment, second, stat_left, stat_right, basis_left, basis_right, master, step_count
    )
    weights_all = gather_blocks(chunks, n_dp, n_chip, count).reshape(count, rows, cols)
    return (weights_all, direction, left_new, right_new)


def solution(mesh):
    placed = (
        P(("dp", "owner"), None, None, None),
        P(),
        P(),
        P("owner", None, None),
        P("owner", None, None),
        P("owner", None, None),
        P("owner", None, None),
        P("owner", None, None),
        P("owner", None, None),
        P("owner", None, None),
    )
    return jax.shard_map(
        body,
        mesh=mesh,
        in_specs=placed,
        out_specs=(P(), P("owner", None, None), P("owner", None, None), P("owner", None, None)),
        check_vma=False,
    )
```

```python
import functools

import jax
import jax.numpy as jnp
from jax import lax
from jax.experimental import pallas as pl
from jax.experimental.pallas import tpu as pltpu
from jax.sharding import PartitionSpec as P

MESH = pl.DeviceIdType.MESH

NS_ITERS = 6


def product(left, right):
    return jnp.matmul(left, right, precision=lax.Precision.HIGHEST)


def transposed(array):
    return jnp.swapaxes(array, 1, 2)


def refresh(stat, basis):
    power = product(stat, basis)
    magnitude = jnp.sqrt(jnp.sum(power * power, axis=(1, 2), keepdims=True))
    iterate = power / (magnitude + 1e-06)
    for repeat_count in range(NS_ITERS):
        iterate = 1.5 * iterate - 0.5 * product(iterate, product(transposed(iterate), iterate))
    return iterate


def slot_layout(owners, slot_count, total_slot_count):
    block_count = owners.shape[0]
    slot_position = jnp.arange(block_count, dtype=jnp.int32)
    before = (owners[:, None] == owners[None, :]) & (
        slot_position[:, None] > slot_position[None, :]
    )
    rank_in = jnp.sum(before.astype(jnp.int32), axis=1)
    target = owners * slot_count + rank_in
    matches = (target[:, None] == jnp.arange(total_slot_count, dtype=jnp.int32)[None, :]).astype(
        jnp.int32
    )
    source = jnp.sum(matches * slot_position[:, None], axis=0)
    occupied = jnp.sum(matches, axis=0)
    return (target, source, occupied)


def soap_update(
    gradient, occupied, moment, second, stat_left, stat_right, basis_left, basis_right, step_count
):
    elapsed = step_count[0].astype(jnp.float32)
    moment_new = 0.95 * moment + 0.05 * gradient
    rotated = product(transposed(basis_left), product(gradient, basis_right))
    rot_moment = product(transposed(basis_left), product(moment_new, basis_right))
    second_new = 0.95 * second + 0.05 * rotated * rotated
    correction = 1.0 - jnp.power(jnp.float32(0.95), elapsed)
    scaled = rot_moment / correction / (jnp.sqrt(second_new / correction) + 1e-08)
    occupied_mask = (occupied > 0)[:, None, None]
    direction = jnp.where(
        occupied_mask, product(basis_left, product(scaled, transposed(basis_right))), 0.0
    )
    left_stat = 0.95 * stat_left + 0.05 * product(gradient, transposed(gradient))
    right_stat = 0.95 * stat_right + 0.05 * product(transposed(gradient), gradient)
    left_new = jnp.where(occupied_mask, refresh(left_stat, basis_left), basis_left)
    right_new = jnp.where(occupied_mask, refresh(right_stat, basis_right), basis_right)
    return (direction, left_new, right_new)


def dp_group():
    me = lax.axis_index("dp")
    owner = lax.axis_index("owner")
    return me, lambda j: (j, owner)


def core_group():
    replica = lax.axis_index("dp")
    owner = lax.axis_index("owner")
    me = lax.rem(owner, 2)
    return me, lambda j: (replica, owner - me + j)


def chip_group():
    replica = lax.axis_index("dp")
    owner = lax.axis_index("owner")
    core = lax.rem(owner, 2)
    return lax.div(owner, 2), lambda j: (replica, j * 2 + core)


def enter(groups):
    barrier = pltpu.get_barrier_semaphore()
    total = 0
    for n, me, peer in groups:
        for k in range(1, n):
            pl.semaphore_signal(barrier, inc=1, device_id=peer(lax.rem(me + k, n)), device_id_type=MESH)
        total += n - 1
    pl.semaphore_wait(barrier, total)


def phase(group, source, dest, send, recv):
    n, me, peer = group
    copies = []
    for k in range(1, n):
        other = lax.rem(me + k, n)
        copy = pltpu.make_async_remote_copy(
            src_ref=source(other),
            dst_ref=dest(me),
            send_sem=send.at[k],
            recv_sem=recv.at[k],
            device_id=peer(other),
            device_id_type=MESH,
        )
        copy.start()
        copies.append(copy)
    return copies


def finish(copies):
    for copy in copies:
        copy.wait()


def sum_slots(buf, out, n, rows, start):
    step = 128 if rows % 128 == 0 else rows

    def one(i, carry):
        at = pl.multiple_of(i * step, step)
        total = buf[0, pl.ds(at, step), :].astype(jnp.float32)
        for j in range(1, n):
            total = total + buf[j, pl.ds(at, step), :].astype(jnp.float32)
        out[pl.ds(start + at, step), :] = total.astype(out.dtype)
        return carry

    lax.fori_loop(0, rows // step, one, 0)


def spread_phases(o_ref, core, dp, chip, piece, send, recv, first):
    n_dp, n_chip = dp[0], chip[0]
    c, r, m = core[1], dp[1], chip[1]
    chunk = n_chip * piece
    half = n_dp * chunk
    base = c * half + r * chunk
    finish(phase(chip, lambda j: o_ref.at[pl.ds(base + m * piece, piece)],
                 lambda me: o_ref.at[pl.ds(base + me * piece, piece)], send.at[first], recv.at[first]))
    copies = phase(dp, lambda j: o_ref.at[pl.ds(c * half + r * chunk, chunk)],
                   lambda me: o_ref.at[pl.ds(c * half + me * chunk, chunk)], send.at[first + 1], recv.at[first + 1])
    partner = core[2](1 - c)
    onward = []
    for k in range(n_dp):
        if k > 0:
            copies[k - 1].wait_recv()
        rows = o_ref.at[pl.ds(c * half + lax.rem(r - k + n_dp, n_dp) * chunk, chunk)]
        copy = pltpu.make_async_remote_copy(
            src_ref=rows,
            dst_ref=rows,
            send_sem=send.at[first + 2, k],
            recv_sem=recv.at[first + 2, k],
            device_id=partner,
            device_id_type=MESH,
        )
        copy.start()
        onward.append(copy)
    for copy in copies:
        copy.wait_send()
    finish(onward)


def groups_of(n_dp, n_chip):
    core_me, core_peer = core_group()
    dp_me, dp_peer = dp_group()
    chip_me, chip_peer = chip_group()
    return (2, core_me, core_peer), (n_dp, dp_me, dp_peer), (n_chip, chip_me, chip_peer)


def grad_kernel(n_dp, n_chip, sel, p_ref, o_ref, buf1, hbuf, buf2, mbuf, buf3, pair, cube, pay, buf5, send, recv):
    core, dp, chip = groups_of(n_dp, n_chip)
    enter((core, dp, chip))
    half = p_ref.shape[0] // 2
    chunk = half // n_dp
    piece = chunk // n_chip
    rows = cube.shape[1]
    slots = sel.shape[1]
    per = chunk // rows
    share = slots * rows // n_dp
    c, r, m = core[1], dp[1], chip[1]
    partner = core[2](1 - c)
    order = [lax.rem(r + k, n_dp) for k in range(n_dp)]
    halves = []
    for k in range(n_dp):
        copy = pltpu.make_async_remote_copy(
            src_ref=p_ref.at[pl.ds((1 - c) * half + order[k] * chunk, chunk)],
            dst_ref=buf1.at[pl.ds(order[k] * chunk, chunk)],
            send_sem=send.at[0, k],
            recv_sem=recv.at[0, k],
            device_id=partner,
            device_id_type=MESH,
        )
        copy.start()
        halves.append(copy)
    onward = []
    for k in range(n_dp):
        j = order[k]
        halves[k].wait_recv()
        out, start = (buf2.at[r], 0) if k == 0 else (hbuf, j * chunk)

        def add(i, carry, j=j, out=out, start=start):
            at = pl.multiple_of(i * 128, 128)
            own = p_ref[pl.ds(c * half + j * chunk + at, 128), :].astype(jnp.float32)
            got = buf1[pl.ds(j * chunk + at, 128), :].astype(jnp.float32)
            out[pl.ds(start + at, 128), :] = (own + got).astype(out.dtype)
            return carry

        lax.fori_loop(0, chunk // 128, add, 0)
        if k > 0:
            copy = pltpu.make_async_remote_copy(
                src_ref=hbuf.at[pl.ds(j * chunk, chunk)],
                dst_ref=buf2.at[r],
                send_sem=send.at[1, k],
                recv_sem=recv.at[1, k],
                device_id=dp[2](j),
                device_id_type=MESH,
            )
            copy.start()
            onward.append(copy)
    for copy in halves:
        copy.wait_send()
    finish(onward)
    sum_slots(buf2, mbuf, n_dp, chunk, 0)
    buf3[m] = mbuf[pl.ds(m * piece, piece), :]
    finish(phase(chip, lambda j: mbuf.at[pl.ds(j * piece, piece)], lambda me: buf3.at[me], send.at[2], recv.at[2]))
    mine = pair.at[c]
    sum_slots(buf3, mine, n_chip, piece, m * piece)
    finish(phase(chip, lambda j: mine.at[pl.ds(m * piece, piece)],
                 lambda me: mine.at[pl.ds(me * piece, piece)], send.at[3], recv.at[3]))
    finish(phase(core, lambda j: mine, lambda me: pair.at[me], send.at[4], recv.at[4]))
    for h in range(2):
        for i in range(per):
            cube[h * per + i] = pair[h, pl.ds(i * rows, rows), :]
    blocks = half // rows
    for k in range(slots):
        block = sel[0, k]
        side = block // blocks
        within = block - side * blocks
        inside = (within // per) == r
        value = cube[side * per + lax.rem(within, per)]
        pay[pl.ds(k * rows, rows), :] = jnp.where(inside, value, jnp.zeros_like(value))
    buf5[r] = pay[pl.ds(r * share, share), :]
    finish(phase(dp, lambda j: pay.at[pl.ds(j * share, share)], lambda me: buf5.at[me], send.at[5], recv.at[5]))
    sum_slots(buf5, o_ref, n_dp, share, r * share)
    finish(phase(dp, lambda j: o_ref.at[pl.ds(r * share, share)],
                 lambda me: o_ref.at[pl.ds(me * share, share)], send.at[6], recv.at[6]))


def weight_kernel(n_dp, n_chip, x_ref, o_ref, buf1, pbuf, buf3, send, recv):
    core, dp, chip = groups_of(n_dp, n_chip)
    enter((core, dp, chip))
    chunk = x_ref.shape[1]
    piece = chunk // n_chip
    half = n_dp * chunk
    c, r, m = core[1], dp[1], chip[1]
    partner = core[2](1 - c)
    order = [lax.rem(m + k, n_chip) for k in range(n_chip)]
    halves = []
    for k in range(n_chip):
        copy = pltpu.make_async_remote_copy(
            src_ref=x_ref.at[1 - c, pl.ds(order[k] * piece, piece)],
            dst_ref=buf1.at[1, pl.ds(order[k] * piece, piece)],
            send_sem=send.at[0, k],
            recv_sem=recv.at[0, k],
            device_id=partner,
            device_id_type=MESH,
        )
        copy.start()
        halves.append(copy)
    onward = []
    for k in range(n_chip):
        j = order[k]
        halves[k].wait_recv()
        total = x_ref[c, pl.ds(j * piece, piece), :].astype(jnp.float32)
        total = total + buf1[1, pl.ds(j * piece, piece), :].astype(jnp.float32)
        if k == 0:
            buf3[m] = total.astype(buf3.dtype)
            continue
        pbuf[pl.ds(j * piece, piece), :] = total.astype(pbuf.dtype)
        copy = pltpu.make_async_remote_copy(
            src_ref=pbuf.at[pl.ds(j * piece, piece)],
            dst_ref=buf3.at[m],
            send_sem=send.at[1, k],
            recv_sem=recv.at[1, k],
            device_id=chip[2](j),
            device_id_type=MESH,
        )
        copy.start()
        onward.append(copy)
    for copy in halves:
        copy.wait_send()
    finish(onward)
    sum_slots(buf3, o_ref, n_chip, piece, c * half + r * chunk + m * piece)
    spread_phases(o_ref, core, dp, chip, piece, send, recv, 2)


def params(collective_id):
    return pltpu.CompilerParams(
        collective_id=collective_id, has_side_effects=True, vmem_limit_bytes=48 * 1024 * 1024
    )


def owned_gradient(blocks, sel, n_dp, n_chip):
    count, rows, cols = blocks.shape
    slots = sel.shape[1]
    flat = blocks.reshape(count * rows, cols)
    half = count * rows // 2
    chunk = half // n_dp
    piece = chunk // n_chip
    vmem = pl.BlockSpec(memory_space=pltpu.VMEM)
    out = pl.pallas_call(
        functools.partial(grad_kernel, n_dp, n_chip),
        out_shape=jax.ShapeDtypeStruct((slots * rows, cols), flat.dtype),
        in_specs=[pl.BlockSpec(memory_space=pltpu.SMEM), vmem],
        out_specs=vmem,
        scratch_shapes=[
            pltpu.VMEM((half, cols), flat.dtype),
            pltpu.VMEM((half, cols), flat.dtype),
            pltpu.VMEM((n_dp, chunk, cols), flat.dtype),
            pltpu.VMEM((chunk, cols), flat.dtype),
            pltpu.VMEM((n_chip, piece, cols), flat.dtype),
            pltpu.VMEM((2, chunk, cols), flat.dtype),
            pltpu.VMEM((2 * chunk // rows, rows, cols), flat.dtype),
            pltpu.VMEM((slots * rows, cols), flat.dtype),
            pltpu.VMEM((n_dp, slots * rows // n_dp, cols), flat.dtype),
            pltpu.SemaphoreType.DMA((7, n_chip)),
            pltpu.SemaphoreType.DMA((7, n_chip)),
        ],
        compiler_params=params(0),
    )(sel, flat)
    return out.reshape(slots, rows, cols)


def gather_blocks(chunks, n_dp, n_chip, count):
    _, chunk, cols = chunks.shape
    piece = chunk // n_chip
    vmem = pl.BlockSpec(memory_space=pltpu.VMEM)
    return pl.pallas_call(
        functools.partial(weight_kernel, n_dp, n_chip),
        out_shape=jax.ShapeDtypeStruct((2 * n_dp * chunk, cols), chunks.dtype),
        in_specs=[vmem],
        out_specs=vmem,
        scratch_shapes=[
            pltpu.VMEM((2, chunk, cols), chunks.dtype),
            pltpu.VMEM((chunk, cols), chunks.dtype),
            pltpu.VMEM((n_chip, piece, cols), chunks.dtype),
            pltpu.SemaphoreType.DMA((5, n_chip)),
            pltpu.SemaphoreType.DMA((5, n_chip)),
        ],
        compiler_params=params(1),
    )(chunks)


def split(a):
    hi = a.astype(jnp.bfloat16)
    lo = (a - hi.astype(jnp.float32)).astype(jnp.bfloat16)
    return hi, lo

def mm3(left, right):
    lh, ll = split(left)
    rh, rl = split(right)
    dot = functools.partial(jnp.dot, preferred_element_type=jnp.float32)
    return dot(lh, rh) + (dot(lh, rl) + dot(ll, rh))

def soap_kernel(scalars, pick, g_ref, m_ref, s_ref, sl_ref, sr_ref, bl_ref, br_ref, w_ref, d_out, l_out, r_out, c_out, u_buf):
    slots = g_ref.shape[0]
    correction = scalars[0]
    chains = []
    for i in range(slots):
        occupied = scalars[1 + i] > 0
        gradient = g_ref[i]
        basis_left = bl_ref[i]
        basis_right = br_ref[i]
        moment_new = 0.95 * m_ref[i] + 0.05 * gradient
        rotated = mm3(basis_left.T, mm3(gradient, basis_right))
        rot_moment = mm3(basis_left.T, mm3(moment_new, basis_right))
        second_new = 0.95 * s_ref[i] + 0.05 * rotated * rotated
        scaled = rot_moment / correction / (jnp.sqrt(second_new / correction) + 1e-08)
        direction = jnp.where(occupied, mm3(basis_left, mm3(scaled, basis_right.T)), 0.0)
        d_out[i] = direction
        master = w_ref[i]
        u_buf[i] = (master - 0.01 * (direction + 0.1 * master)).astype(u_buf.dtype)
        left_stat = 0.95 * sl_ref[i] + 0.05 * mm3(gradient, gradient.T)
        right_stat = 0.95 * sr_ref[i] + 0.05 * mm3(gradient.T, gradient)
        chains.append((left_stat, basis_left, l_out, i, occupied))
        chains.append((right_stat, basis_right, r_out, i, occupied))
    iterates = []
    for stat, basis, out, i, occupied in chains:
        power = mm3(stat, basis)
        magnitude = jnp.sqrt(jnp.sum(power * power, keepdims=True))
        iterates.append(power / (magnitude + 1e-06))
    for repeat_count in range(NS_ITERS):
        grams = [mm3(it.T, it) for it in iterates]
        iterates = [1.5 * it - 0.5 * mm3(it, gram) for it, gram in zip(iterates, grams)]
    for (stat, basis, out, i, occupied), it in zip(chains, iterates):
        out[i] = jnp.where(occupied, it, basis)
    halves, rows = c_out.shape[0], g_ref.shape[1]
    for h in range(halves):
        for k in range(c_out.shape[1] // rows):
            index = pick[h * (c_out.shape[1] // rows) + k]
            value = u_buf[jnp.maximum(index, 0)]
            c_out[h, pl.ds(k * rows, rows), :] = jnp.where(index >= 0, value, jnp.zeros_like(value))


def soap_slots(gradient, occupied, pick, moment, second, stat_left, stat_right, basis_left, basis_right, master, step_count):
    slots, rows, cols = gradient.shape
    elapsed = step_count[0].astype(jnp.float32)
    correction = 1.0 - jnp.power(jnp.float32(0.95), elapsed)
    scalars = jnp.concatenate([correction[None], occupied.astype(jnp.float32)])
    vmem = pl.BlockSpec(memory_space=pltpu.VMEM)
    smem = pl.BlockSpec(memory_space=pltpu.SMEM)
    f32 = jax.ShapeDtypeStruct(gradient.shape, jnp.float32)
    chunks = jax.ShapeDtypeStruct((2, pick.shape[0] // 2 * rows, cols), jnp.bfloat16)
    return pl.pallas_call(
        soap_kernel,
        out_shape=(f32, f32, f32, chunks),
        in_specs=[smem, smem] + [vmem] * 8,
        out_specs=(vmem, vmem, vmem, vmem),
        scratch_shapes=[pltpu.VMEM(gradient.shape, jnp.bfloat16)],
    )(scalars, pick, gradient, moment, second, stat_left, stat_right, basis_left, basis_right, master)


def body(
    partials,
    owners,
    step_count,
    master,
    moment,
    second,
    stat_left,
    stat_right,
    basis_left,
    basis_right,
):
    owner_count = lax.axis_size("owner")
    n_dp = lax.axis_size("dp")
    n_chip = owner_count // 2
    slot_count = master.shape[0]
    total_slot_count = slot_count * owner_count
    target, source, occupied = slot_layout(owners, slot_count, total_slot_count)
    first_slot = lax.axis_index("owner") * slot_count
    occupied_mine = lax.dynamic_slice_in_dim(occupied, first_slot, slot_count, 0)
    source_mine = lax.dynamic_slice_in_dim(source, first_slot, slot_count, 0)
    sel = source_mine[None, :].astype(jnp.int32)
    mask_mine = (occupied_mine > 0).astype(jnp.float32)[:, None, None]
    gradient = owned_gradient(partials[0], sel, n_dp, n_chip).astype(jnp.float32) * mask_mine
    block_count = owners.shape[0]
    count, rows, cols = block_count, master.shape[1], master.shape[2]
    per = count // (2 * n_dp)
    replica = lax.axis_index("dp")
    mine = (jnp.arange(2)[:, None] * (count // 2) + replica * per + jnp.arange(per)[None, :]).reshape(-1)
    rank = jnp.take(target, mine) - first_slot
    pick = jnp.where((rank >= 0) & (rank < slot_count), rank, -1).astype(jnp.int32)
    direction, left_new, right_new, chunks = soap_slots(
        gradient, occupied_mine, pick, moment, second, stat_left, stat_right, basis_left, basis_right, master, step_count
    )
    weights_all = gather_blocks(chunks, n_dp, n_chip, count).reshape(count, rows, cols)
    return (weights_all, direction, left_new, right_new)


def solution(mesh):
    placed = (
        P(("dp", "owner"), None, None, None),
        P(),
        P(),
        P("owner", None, None),
        P("owner", None, None),
        P("owner", None, None),
        P("owner", None, None),
        P("owner", None, None),
        P("owner", None, None),
        P("owner", None, None),
    )
    return jax.shard_map(
        body,
        mesh=mesh,
        in_specs=placed,
        out_specs=(P(), P("owner", None, None), P("owner", None, None), P("owner", None, None)),
        check_vma=False,
    )
```

```python
import functools

import jax
import jax.numpy as jnp
from jax import lax
from jax.experimental import pallas as pl
from jax.experimental.pallas import tpu as pltpu
from jax.sharding import PartitionSpec as P

MESH = pl.DeviceIdType.MESH

NS_ITERS = 6


def product(left, right):
    return jnp.matmul(left, right, precision=lax.Precision.HIGHEST)


def transposed(array):
    return jnp.swapaxes(array, 1, 2)


def refresh(stat, basis):
    power = product(stat, basis)
    magnitude = jnp.sqrt(jnp.sum(power * power, axis=(1, 2), keepdims=True))
    iterate = power / (magnitude + 1e-06)
    for repeat_count in range(NS_ITERS):
        iterate = 1.5 * iterate - 0.5 * product(iterate, product(transposed(iterate), iterate))
    return iterate


def slot_layout(owners, slot_count, total_slot_count):
    block_count = owners.shape[0]
    slot_position = jnp.arange(block_count, dtype=jnp.int32)
    before = (owners[:, None] == owners[None, :]) & (
        slot_position[:, None] > slot_position[None, :]
    )
    rank_in = jnp.sum(before.astype(jnp.int32), axis=1)
    target = owners * slot_count + rank_in
    matches = (target[:, None] == jnp.arange(total_slot_count, dtype=jnp.int32)[None, :]).astype(
        jnp.int32
    )
    source = jnp.sum(matches * slot_position[:, None], axis=0)
    occupied = jnp.sum(matches, axis=0)
    return (target, source, occupied)


def soap_update(
    gradient, occupied, moment, second, stat_left, stat_right, basis_left, basis_right, step_count
):
    elapsed = step_count[0].astype(jnp.float32)
    moment_new = 0.95 * moment + 0.05 * gradient
    rotated = product(transposed(basis_left), product(gradient, basis_right))
    rot_moment = product(transposed(basis_left), product(moment_new, basis_right))
    second_new = 0.95 * second + 0.05 * rotated * rotated
    correction = 1.0 - jnp.power(jnp.float32(0.95), elapsed)
    scaled = rot_moment / correction / (jnp.sqrt(second_new / correction) + 1e-08)
    occupied_mask = (occupied > 0)[:, None, None]
    direction = jnp.where(
        occupied_mask, product(basis_left, product(scaled, transposed(basis_right))), 0.0
    )
    left_stat = 0.95 * stat_left + 0.05 * product(gradient, transposed(gradient))
    right_stat = 0.95 * stat_right + 0.05 * product(transposed(gradient), gradient)
    left_new = jnp.where(occupied_mask, refresh(left_stat, basis_left), basis_left)
    right_new = jnp.where(occupied_mask, refresh(right_stat, basis_right), basis_right)
    return (direction, left_new, right_new)


def dp_group():
    me = lax.axis_index("dp")
    owner = lax.axis_index("owner")
    return me, lambda j: (j, owner)


def core_group():
    replica = lax.axis_index("dp")
    owner = lax.axis_index("owner")
    me = lax.rem(owner, 2)
    return me, lambda j: (replica, owner - me + j)


def chip_group():
    replica = lax.axis_index("dp")
    owner = lax.axis_index("owner")
    core = lax.rem(owner, 2)
    return lax.div(owner, 2), lambda j: (replica, j * 2 + core)


def enter(groups):
    barrier = pltpu.get_barrier_semaphore()
    total = 0
    for n, me, peer in groups:
        for k in range(1, n):
            pl.semaphore_signal(barrier, inc=1, device_id=peer(lax.rem(me + k, n)), device_id_type=MESH)
        total += n - 1
    pl.semaphore_wait(barrier, total)


def phase(group, source, dest, send, recv):
    n, me, peer = group
    copies = {}
    for k in range(n - 1, 0, -1):
        other = lax.rem(me + k, n)
        copy = pltpu.make_async_remote_copy(
            src_ref=source(other),
            dst_ref=dest(me),
            send_sem=send.at[k],
            recv_sem=recv.at[k],
            device_id=peer(other),
            device_id_type=MESH,
        )
        copy.start()
        copies[k] = copy
    return [copies[k] for k in range(1, n)]


def finish(copies):
    for copy in copies:
        copy.wait()


def sum_slots(buf, out, n, rows, start):
    step = 128 if rows % 128 == 0 else rows

    def one(i, carry):
        at = pl.multiple_of(i * step, step)
        total = buf[0, pl.ds(at, step), :].astype(jnp.float32)
        for j in range(1, n):
            total = total + buf[j, pl.ds(at, step), :].astype(jnp.float32)
        out[pl.ds(start + at, step), :] = total.astype(out.dtype)
        return carry

    lax.fori_loop(0, rows // step, one, 0)


def spread_phases(o_ref, core, dp, chip, piece, send, recv, first):
    n_dp, n_chip = dp[0], chip[0]
    c, r, m = core[1], dp[1], chip[1]
    chunk = n_chip * piece
    half = n_dp * chunk
    base = c * half + r * chunk
    finish(phase(chip, lambda j: o_ref.at[pl.ds(base + m * piece, piece)],
                 lambda me: o_ref.at[pl.ds(base + me * piece, piece)], send.at[first], recv.at[first]))
    copies = phase(dp, lambda j: o_ref.at[pl.ds(c * half + r * chunk, chunk)],
                   lambda me: o_ref.at[pl.ds(c * half + me * chunk, chunk)], send.at[first + 1], recv.at[first + 1])
    partner = core[2](1 - c)
    onward = []
    for k in range(n_dp):
        if k > 0:
            copies[k - 1].wait_recv()
        rows = o_ref.at[pl.ds(c * half + lax.rem(r - k + n_dp, n_dp) * chunk, chunk)]
        copy = pltpu.make_async_remote_copy(
            src_ref=rows,
            dst_ref=rows,
            send_sem=send.at[first + 2, k],
            recv_sem=recv.at[first + 2, k],
            device_id=partner,
            device_id_type=MESH,
        )
        copy.start()
        onward.append(copy)
    for copy in copies:
        copy.wait_send()
    finish(onward)


def groups_of(n_dp, n_chip):
    core_me, core_peer = core_group()
    dp_me, dp_peer = dp_group()
    chip_me, chip_peer = chip_group()
    return (2, core_me, core_peer), (n_dp, dp_me, dp_peer), (n_chip, chip_me, chip_peer)


def grad_kernel(n_dp, n_chip, sel, p_ref, o_ref, buf1, hbuf, buf2, mbuf, buf3, pair, cube, pay, buf5, send, recv):
    core, dp, chip = groups_of(n_dp, n_chip)
    enter((core, dp, chip))
    half = p_ref.shape[0] // 2
    chunk = half // n_dp
    piece = chunk // n_chip
    rows = cube.shape[1]
    slots = sel.shape[1]
    per = chunk // rows
    share = slots * rows // n_dp
    c, r, m = core[1], dp[1], chip[1]
    partner = core[2](1 - c)
    order = [lax.rem(r + k, n_dp) for k in range(n_dp)]
    halves = []
    for k in range(n_dp):
        copy = pltpu.make_async_remote_copy(
            src_ref=p_ref.at[pl.ds((1 - c) * half + order[k] * chunk, chunk)],
            dst_ref=buf1.at[pl.ds(order[k] * chunk, chunk)],
            send_sem=send.at[0, k],
            recv_sem=recv.at[0, k],
            device_id=partner,
            device_id_type=MESH,
        )
        copy.start()
        halves.append(copy)
    onward = []
    for k in range(n_dp):
        j = order[k]
        halves[k].wait_recv()
        out, start = (buf2.at[r], 0) if k == 0 else (hbuf, j * chunk)

        def add(i, carry, j=j, out=out, start=start):
            at = pl.multiple_of(i * 128, 128)
            own = p_ref[pl.ds(c * half + j * chunk + at, 128), :].astype(jnp.float32)
            got = buf1[pl.ds(j * chunk + at, 128), :].astype(jnp.float32)
            out[pl.ds(start + at, 128), :] = (own + got).astype(out.dtype)
            return carry

        lax.fori_loop(0, chunk // 128, add, 0)
        if k > 0:
            copy = pltpu.make_async_remote_copy(
                src_ref=hbuf.at[pl.ds(j * chunk, chunk)],
                dst_ref=buf2.at[r],
                send_sem=send.at[1, k],
                recv_sem=recv.at[1, k],
                device_id=dp[2](j),
                device_id_type=MESH,
            )
            copy.start()
            onward.append(copy)
    for copy in halves:
        copy.wait_send()
    finish(onward)
    sum_slots(buf2, mbuf, n_dp, chunk, 0)
    buf3[m] = mbuf[pl.ds(m * piece, piece), :]
    finish(phase(chip, lambda j: mbuf.at[pl.ds(j * piece, piece)], lambda me: buf3.at[me], send.at[2], recv.at[2]))
    mine = pair.at[c]
    sum_slots(buf3, mine, n_chip, piece, m * piece)
    finish(phase(chip, lambda j: mine.at[pl.ds(m * piece, piece)],
                 lambda me: mine.at[pl.ds(me * piece, piece)], send.at[3], recv.at[3]))
    finish(phase(core, lambda j: mine, lambda me: pair.at[me], send.at[4], recv.at[4]))
    for h in range(2):
        for i in range(per):
            cube[h * per + i] = pair[h, pl.ds(i * rows, rows), :]
    blocks = half // rows
    for k in range(slots):
        block = sel[0, k]
        side = block // blocks
        within = block - side * blocks
        inside = (within // per) == r
        value = cube[side * per + lax.rem(within, per)]
        pay[pl.ds(k * rows, rows), :] = jnp.where(inside, value, jnp.zeros_like(value))
    buf5[r] = pay[pl.ds(r * share, share), :]
    finish(phase(dp, lambda j: pay.at[pl.ds(j * share, share)], lambda me: buf5.at[me], send.at[5], recv.at[5]))
    sum_slots(buf5, o_ref, n_dp, share, r * share)
    finish(phase(dp, lambda j: o_ref.at[pl.ds(r * share, share)],
                 lambda me: o_ref.at[pl.ds(me * share, share)], send.at[6], recv.at[6]))


def weight_kernel(n_dp, n_chip, x_ref, o_ref, buf1, pbuf, buf3, send, recv):
    core, dp, chip = groups_of(n_dp, n_chip)
    enter((core, dp, chip))
    chunk = x_ref.shape[1]
    piece = chunk // n_chip
    half = n_dp * chunk
    c, r, m = core[1], dp[1], chip[1]
    finish(phase(core, lambda j: x_ref.at[j], lambda me: buf1.at[1], send.at[0], recv.at[0]))
    buf1[0] = x_ref[c]
    sum_slots(buf1, pbuf, 2, chunk, 0)
    buf3[m] = pbuf[pl.ds(m * piece, piece), :]
    finish(phase(chip, lambda j: pbuf.at[pl.ds(j * piece, piece)], lambda me: buf3.at[me], send.at[1], recv.at[1]))
    sum_slots(buf3, o_ref, n_chip, piece, c * half + r * chunk + m * piece)
    spread_phases(o_ref, core, dp, chip, piece, send, recv, 2)


def params(collective_id):
    return pltpu.CompilerParams(
        collective_id=collective_id, has_side_effects=True, vmem_limit_bytes=48 * 1024 * 1024
    )


def owned_gradient(blocks, sel, n_dp, n_chip):
    count, rows, cols = blocks.shape
    slots = sel.shape[1]
    flat = blocks.reshape(count * rows, cols)
    half = count * rows // 2
    chunk = half // n_dp
    piece = chunk // n_chip
    vmem = pl.BlockSpec(memory_space=pltpu.VMEM)
    out = pl.pallas_call(
        functools.partial(grad_kernel, n_dp, n_chip),
        out_shape=jax.ShapeDtypeStruct((slots * rows, cols), flat.dtype),
        in_specs=[pl.BlockSpec(memory_space=pltpu.SMEM), vmem],
        out_specs=vmem,
        scratch_shapes=[
            pltpu.VMEM((half, cols), flat.dtype),
            pltpu.VMEM((half, cols), flat.dtype),
            pltpu.VMEM((n_dp, chunk, cols), flat.dtype),
            pltpu.VMEM((chunk, cols), flat.dtype),
            pltpu.VMEM((n_chip, piece, cols), flat.dtype),
            pltpu.VMEM((2, chunk, cols), flat.dtype),
            pltpu.VMEM((2 * chunk // rows, rows, cols), flat.dtype),
            pltpu.VMEM((slots * rows, cols), flat.dtype),
            pltpu.VMEM((n_dp, slots * rows // n_dp, cols), flat.dtype),
            pltpu.SemaphoreType.DMA((7, n_chip)),
            pltpu.SemaphoreType.DMA((7, n_chip)),
        ],
        compiler_params=params(0),
    )(sel, flat)
    return out.reshape(slots, rows, cols)


def gather_blocks(chunks, n_dp, n_chip, count):
    _, chunk, cols = chunks.shape
    piece = chunk // n_chip
    vmem = pl.BlockSpec(memory_space=pltpu.VMEM)
    return pl.pallas_call(
        functools.partial(weight_kernel, n_dp, n_chip),
        out_shape=jax.ShapeDtypeStruct((2 * n_dp * chunk, cols), chunks.dtype),
        in_specs=[vmem],
        out_specs=vmem,
        scratch_shapes=[
            pltpu.VMEM((2, chunk, cols), chunks.dtype),
            pltpu.VMEM((chunk, cols), chunks.dtype),
            pltpu.VMEM((n_chip, piece, cols), chunks.dtype),
            pltpu.SemaphoreType.DMA((5, n_chip)),
            pltpu.SemaphoreType.DMA((5, n_chip)),
        ],
        compiler_params=params(1),
    )(chunks)


def split(a):
    hi = a.astype(jnp.bfloat16)
    lo = (a - hi.astype(jnp.float32)).astype(jnp.bfloat16)
    return hi, lo

def mm3(left, right):
    lh, ll = split(left)
    rh, rl = split(right)
    dot = functools.partial(jnp.dot, preferred_element_type=jnp.float32)
    return dot(lh, rh) + (dot(lh, rl) + dot(ll, rh))

def soap_kernel(scalars, pick, g_ref, m_ref, s_ref, sl_ref, sr_ref, bl_ref, br_ref, w_ref, d_out, l_out, r_out, c_out, u_buf):
    slots = g_ref.shape[0]
    correction = scalars[0]
    chains = []
    for i in range(slots):
        occupied = scalars[1 + i] > 0
        gradient = g_ref[i]
        basis_left = bl_ref[i]
        basis_right = br_ref[i]
        moment_new = 0.95 * m_ref[i] + 0.05 * gradient
        rotated = mm3(basis_left.T, mm3(gradient, basis_right))
        rot_moment = mm3(basis_left.T, mm3(moment_new, basis_right))
        second_new = 0.95 * s_ref[i] + 0.05 * rotated * rotated
        scaled = rot_moment / correction / (jnp.sqrt(second_new / correction) + 1e-08)
        direction = jnp.where(occupied, mm3(basis_left, mm3(scaled, basis_right.T)), 0.0)
        d_out[i] = direction
        master = w_ref[i]
        u_buf[i] = (master - 0.01 * (direction + 0.1 * master)).astype(u_buf.dtype)
        left_stat = 0.95 * sl_ref[i] + 0.05 * mm3(gradient, gradient.T)
        right_stat = 0.95 * sr_ref[i] + 0.05 * mm3(gradient.T, gradient)
        chains.append((left_stat, basis_left, l_out, i, occupied))
        chains.append((right_stat, basis_right, r_out, i, occupied))
    iterates = []
    for stat, basis, out, i, occupied in chains:
        power = mm3(stat, basis)
        magnitude = jnp.sqrt(jnp.sum(power * power, keepdims=True))
        iterates.append(power / (magnitude + 1e-06))
    for repeat_count in range(NS_ITERS):
        grams = [mm3(it.T, it) for it in iterates]
        iterates = [1.5 * it - 0.5 * mm3(it, gram) for it, gram in zip(iterates, grams)]
    for (stat, basis, out, i, occupied), it in zip(chains, iterates):
        out[i] = jnp.where(occupied, it, basis)
    halves, rows = c_out.shape[0], g_ref.shape[1]
    for h in range(halves):
        for k in range(c_out.shape[1] // rows):
            index = pick[h * (c_out.shape[1] // rows) + k]
            value = u_buf[jnp.maximum(index, 0)]
            c_out[h, pl.ds(k * rows, rows), :] = jnp.where(index >= 0, value, jnp.zeros_like(value))


def soap_slots(gradient, occupied, pick, moment, second, stat_left, stat_right, basis_left, basis_right, master, step_count):
    slots, rows, cols = gradient.shape
    elapsed = step_count[0].astype(jnp.float32)
    correction = 1.0 - jnp.power(jnp.float32(0.95), elapsed)
    scalars = jnp.concatenate([correction[None], occupied.astype(jnp.float32)])
    vmem = pl.BlockSpec(memory_space=pltpu.VMEM)
    smem = pl.BlockSpec(memory_space=pltpu.SMEM)
    f32 = jax.ShapeDtypeStruct(gradient.shape, jnp.float32)
    chunks = jax.ShapeDtypeStruct((2, pick.shape[0] // 2 * rows, cols), jnp.bfloat16)
    return pl.pallas_call(
        soap_kernel,
        out_shape=(f32, f32, f32, chunks),
        in_specs=[smem, smem] + [vmem] * 8,
        out_specs=(vmem, vmem, vmem, vmem),
        scratch_shapes=[pltpu.VMEM(gradient.shape, jnp.bfloat16)],
    )(scalars, pick, gradient, moment, second, stat_left, stat_right, basis_left, basis_right, master)


def body(
    partials,
    owners,
    step_count,
    master,
    moment,
    second,
    stat_left,
    stat_right,
    basis_left,
    basis_right,
):
    owner_count = lax.axis_size("owner")
    n_dp = lax.axis_size("dp")
    n_chip = owner_count // 2
    slot_count = master.shape[0]
    total_slot_count = slot_count * owner_count
    target, source, occupied = slot_layout(owners, slot_count, total_slot_count)
    first_slot = lax.axis_index("owner") * slot_count
    occupied_mine = lax.dynamic_slice_in_dim(occupied, first_slot, slot_count, 0)
    source_mine = lax.dynamic_slice_in_dim(source, first_slot, slot_count, 0)
    sel = source_mine[None, :].astype(jnp.int32)
    mask_mine = (occupied_mine > 0).astype(jnp.float32)[:, None, None]
    gradient = owned_gradient(partials[0], sel, n_dp, n_chip).astype(jnp.float32) * mask_mine
    block_count = owners.shape[0]
    count, rows, cols = block_count, master.shape[1], master.shape[2]
    per = count // (2 * n_dp)
    replica = lax.axis_index("dp")
    mine = (jnp.arange(2)[:, None] * (count // 2) + replica * per + jnp.arange(per)[None, :]).reshape(-1)
    rank = jnp.take(target, mine) - first_slot
    pick = jnp.where((rank >= 0) & (rank < slot_count), rank, -1).astype(jnp.int32)
    direction, left_new, right_new, chunks = soap_slots(
        gradient, occupied_mine, pick, moment, second, stat_left, stat_right, basis_left, basis_right, master, step_count
    )
    weights_all = gather_blocks(chunks, n_dp, n_chip, count).reshape(count, rows, cols)
    return (weights_all, direction, left_new, right_new)


def solution(mesh):
    placed = (
        P(("dp", "owner"), None, None, None),
        P(),
        P(),
        P("owner", None, None),
        P("owner", None, None),
        P("owner", None, None),
        P("owner", None, None),
        P("owner", None, None),
        P("owner", None, None),
        P("owner", None, None),
    )
    return jax.shard_map(
        body,
        mesh=mesh,
        in_specs=placed,
        out_specs=(P(), P("owner", None, None), P("owner", None, None), P("owner", None, None)),
        check_vma=False,
    )
```

```python
import functools

import jax
import jax.numpy as jnp
from jax import lax
from jax.experimental import pallas as pl
from jax.experimental.pallas import tpu as pltpu
from jax.sharding import PartitionSpec as P

MESH = pl.DeviceIdType.MESH

NS_ITERS = 6


def product(left, right):
    return jnp.matmul(left, right, precision=lax.Precision.HIGHEST)


def transposed(array):
    return jnp.swapaxes(array, 1, 2)


def refresh(stat, basis):
    power = product(stat, basis)
    magnitude = jnp.sqrt(jnp.sum(power * power, axis=(1, 2), keepdims=True))
    iterate = power / (magnitude + 1e-06)
    for repeat_count in range(NS_ITERS):
        iterate = 1.5 * iterate - 0.5 * product(iterate, product(transposed(iterate), iterate))
    return iterate


def slot_layout(owners, slot_count, total_slot_count):
    block_count = owners.shape[0]
    slot_position = jnp.arange(block_count, dtype=jnp.int32)
    before = (owners[:, None] == owners[None, :]) & (
        slot_position[:, None] > slot_position[None, :]
    )
    rank_in = jnp.sum(before.astype(jnp.int32), axis=1)
    target = owners * slot_count + rank_in
    matches = (target[:, None] == jnp.arange(total_slot_count, dtype=jnp.int32)[None, :]).astype(
        jnp.int32
    )
    source = jnp.sum(matches * slot_position[:, None], axis=0)
    occupied = jnp.sum(matches, axis=0)
    return (target, source, occupied)


def soap_update(
    gradient, occupied, moment, second, stat_left, stat_right, basis_left, basis_right, step_count
):
    elapsed = step_count[0].astype(jnp.float32)
    moment_new = 0.95 * moment + 0.05 * gradient
    rotated = product(transposed(basis_left), product(gradient, basis_right))
    rot_moment = product(transposed(basis_left), product(moment_new, basis_right))
    second_new = 0.95 * second + 0.05 * rotated * rotated
    correction = 1.0 - jnp.power(jnp.float32(0.95), elapsed)
    scaled = rot_moment / correction / (jnp.sqrt(second_new / correction) + 1e-08)
    occupied_mask = (occupied > 0)[:, None, None]
    direction = jnp.where(
        occupied_mask, product(basis_left, product(scaled, transposed(basis_right))), 0.0
    )
    left_stat = 0.95 * stat_left + 0.05 * product(gradient, transposed(gradient))
    right_stat = 0.95 * stat_right + 0.05 * product(transposed(gradient), gradient)
    left_new = jnp.where(occupied_mask, refresh(left_stat, basis_left), basis_left)
    right_new = jnp.where(occupied_mask, refresh(right_stat, basis_right), basis_right)
    return (direction, left_new, right_new)


def dp_group():
    me = lax.axis_index("dp")
    owner = lax.axis_index("owner")
    return me, lambda j: (j, owner)


def core_group():
    replica = lax.axis_index("dp")
    owner = lax.axis_index("owner")
    me = lax.rem(owner, 2)
    return me, lambda j: (replica, owner - me + j)


def chip_group():
    replica = lax.axis_index("dp")
    owner = lax.axis_index("owner")
    core = lax.rem(owner, 2)
    return lax.div(owner, 2), lambda j: (replica, j * 2 + core)


def enter(groups):
    barrier = pltpu.get_barrier_semaphore()
    total = 0
    for n, me, peer in groups:
        for k in range(1, n):
            pl.semaphore_signal(barrier, inc=1, device_id=peer(lax.rem(me + k, n)), device_id_type=MESH)
        total += n - 1
    pl.semaphore_wait(barrier, total)


def phase(group, source, dest, send, recv):
    n, me, peer = group
    copies = {}
    near = [k for pair in zip(range(1, n), range(n - 1, 0, -1)) for k in pair]
    for k in list(dict.fromkeys(near))[: n - 1]:
        other = lax.rem(me + k, n)
        copy = pltpu.make_async_remote_copy(
            src_ref=source(other),
            dst_ref=dest(me),
            send_sem=send.at[k],
            recv_sem=recv.at[k],
            device_id=peer(other),
            device_id_type=MESH,
        )
        copy.start()
        copies[k] = copy
    return [copies[k] for k in range(1, n)]


def finish(copies):
    for copy in copies:
        copy.wait()


def sum_slots(buf, out, n, rows, start):
    step = 128 if rows % 128 == 0 else rows

    def one(i, carry):
        at = pl.multiple_of(i * step, step)
        total = buf[0, pl.ds(at, step), :].astype(jnp.float32)
        for j in range(1, n):
            total = total + buf[j, pl.ds(at, step), :].astype(jnp.float32)
        out[pl.ds(start + at, step), :] = total.astype(out.dtype)
        return carry

    lax.fori_loop(0, rows // step, one, 0)


def spread_phases(o_ref, core, dp, chip, piece, send, recv, first):
    n_dp, n_chip = dp[0], chip[0]
    c, r, m = core[1], dp[1], chip[1]
    chunk = n_chip * piece
    half = n_dp * chunk
    base = c * half + r * chunk
    finish(phase(chip, lambda j: o_ref.at[pl.ds(base + m * piece, piece)],
                 lambda me: o_ref.at[pl.ds(base + me * piece, piece)], send.at[first], recv.at[first]))
    copies = phase(dp, lambda j: o_ref.at[pl.ds(c * half + r * chunk, chunk)],
                   lambda me: o_ref.at[pl.ds(c * half + me * chunk, chunk)], send.at[first + 1], recv.at[first + 1])
    partner = core[2](1 - c)
    onward = []
    for k in range(n_dp):
        if k > 0:
            copies[k - 1].wait_recv()
        rows = o_ref.at[pl.ds(c * half + lax.rem(r - k + n_dp, n_dp) * chunk, chunk)]
        copy = pltpu.make_async_remote_copy(
            src_ref=rows,
            dst_ref=rows,
            send_sem=send.at[first + 2, k],
            recv_sem=recv.at[first + 2, k],
            device_id=partner,
            device_id_type=MESH,
        )
        copy.start()
        onward.append(copy)
    for copy in copies:
        copy.wait_send()
    finish(onward)


def groups_of(n_dp, n_chip):
    core_me, core_peer = core_group()
    dp_me, dp_peer = dp_group()
    chip_me, chip_peer = chip_group()
    return (2, core_me, core_peer), (n_dp, dp_me, dp_peer), (n_chip, chip_me, chip_peer)


def grad_kernel(n_dp, n_chip, sel, p_ref, o_ref, buf1, hbuf, buf2, mbuf, buf3, pair, cube, pay, buf5, send, recv):
    core, dp, chip = groups_of(n_dp, n_chip)
    enter((core, dp, chip))
    half = p_ref.shape[0] // 2
    chunk = half // n_dp
    piece = chunk // n_chip
    rows = cube.shape[1]
    slots = sel.shape[1]
    per = chunk // rows
    share = slots * rows // n_dp
    c, r, m = core[1], dp[1], chip[1]
    partner = core[2](1 - c)
    order = [lax.rem(r + k, n_dp) for k in range(n_dp)]
    halves = []
    for k in range(n_dp):
        copy = pltpu.make_async_remote_copy(
            src_ref=p_ref.at[pl.ds((1 - c) * half + order[k] * chunk, chunk)],
            dst_ref=buf1.at[pl.ds(order[k] * chunk, chunk)],
            send_sem=send.at[0, k],
            recv_sem=recv.at[0, k],
            device_id=partner,
            device_id_type=MESH,
        )
        copy.start()
        halves.append(copy)
    onward = []
    for k in range(n_dp):
        j = order[k]
        halves[k].wait_recv()
        out, start = (buf2.at[r], 0) if k == 0 else (hbuf, j * chunk)

        def add(i, carry, j=j, out=out, start=start):
            at = pl.multiple_of(i * 128, 128)
            own = p_ref[pl.ds(c * half + j * chunk + at, 128), :].astype(jnp.float32)
            got = buf1[pl.ds(j * chunk + at, 128), :].astype(jnp.float32)
            out[pl.ds(start + at, 128), :] = (own + got).astype(out.dtype)
            return carry

        lax.fori_loop(0, chunk // 128, add, 0)
        if k > 0:
            copy = pltpu.make_async_remote_copy(
                src_ref=hbuf.at[pl.ds(j * chunk, chunk)],
                dst_ref=buf2.at[r],
                send_sem=send.at[1, k],
                recv_sem=recv.at[1, k],
                device_id=dp[2](j),
                device_id_type=MESH,
            )
            copy.start()
            onward.append(copy)
    for copy in halves:
        copy.wait_send()
    finish(onward)
    sum_slots(buf2, mbuf, n_dp, chunk, 0)
    buf3[m] = mbuf[pl.ds(m * piece, piece), :]
    finish(phase(chip, lambda j: mbuf.at[pl.ds(j * piece, piece)], lambda me: buf3.at[me], send.at[2], recv.at[2]))
    mine = pair.at[c]
    sum_slots(buf3, mine, n_chip, piece, m * piece)
    finish(phase(chip, lambda j: mine.at[pl.ds(m * piece, piece)],
                 lambda me: mine.at[pl.ds(me * piece, piece)], send.at[3], recv.at[3]))
    finish(phase(core, lambda j: mine, lambda me: pair.at[me], send.at[4], recv.at[4]))
    for h in range(2):
        for i in range(per):
            cube[h * per + i] = pair[h, pl.ds(i * rows, rows), :]
    blocks = half // rows
    for k in range(slots):
        block = sel[0, k]
        side = block // blocks
        within = block - side * blocks
        inside = (within // per) == r
        value = cube[side * per + lax.rem(within, per)]
        pay[pl.ds(k * rows, rows), :] = jnp.where(inside, value, jnp.zeros_like(value))
    buf5[r] = pay[pl.ds(r * share, share), :]
    finish(phase(dp, lambda j: pay.at[pl.ds(j * share, share)], lambda me: buf5.at[me], send.at[5], recv.at[5]))
    sum_slots(buf5, o_ref, n_dp, share, r * share)
    finish(phase(dp, lambda j: o_ref.at[pl.ds(r * share, share)],
                 lambda me: o_ref.at[pl.ds(me * share, share)], send.at[6], recv.at[6]))


def weight_kernel(n_dp, n_chip, x_ref, o_ref, buf1, pbuf, buf3, send, recv):
    core, dp, chip = groups_of(n_dp, n_chip)
    enter((core, dp, chip))
    chunk = x_ref.shape[1]
    piece = chunk // n_chip
    half = n_dp * chunk
    c, r, m = core[1], dp[1], chip[1]
    finish(phase(core, lambda j: x_ref.at[j], lambda me: buf1.at[1], send.at[0], recv.at[0]))
    buf1[0] = x_ref[c]
    sum_slots(buf1, pbuf, 2, chunk, 0)
    buf3[m] = pbuf[pl.ds(m * piece, piece), :]
    finish(phase(chip, lambda j: pbuf.at[pl.ds(j * piece, piece)], lambda me: buf3.at[me], send.at[1], recv.at[1]))
    sum_slots(buf3, o_ref, n_chip, piece, c * half + r * chunk + m * piece)
    spread_phases(o_ref, core, dp, chip, piece, send, recv, 2)


def params(collective_id):
    return pltpu.CompilerParams(
        collective_id=collective_id, has_side_effects=True, vmem_limit_bytes=48 * 1024 * 1024
    )


def owned_gradient(blocks, sel, n_dp, n_chip):
    count, rows, cols = blocks.shape
    slots = sel.shape[1]
    flat = blocks.reshape(count * rows, cols)
    half = count * rows // 2
    chunk = half // n_dp
    piece = chunk // n_chip
    vmem = pl.BlockSpec(memory_space=pltpu.VMEM)
    out = pl.pallas_call(
        functools.partial(grad_kernel, n_dp, n_chip),
        out_shape=jax.ShapeDtypeStruct((slots * rows, cols), flat.dtype),
        in_specs=[pl.BlockSpec(memory_space=pltpu.SMEM), vmem],
        out_specs=vmem,
        scratch_shapes=[
            pltpu.VMEM((half, cols), flat.dtype),
            pltpu.VMEM((half, cols), flat.dtype),
            pltpu.VMEM((n_dp, chunk, cols), flat.dtype),
            pltpu.VMEM((chunk, cols), flat.dtype),
            pltpu.VMEM((n_chip, piece, cols), flat.dtype),
            pltpu.VMEM((2, chunk, cols), flat.dtype),
            pltpu.VMEM((2 * chunk // rows, rows, cols), flat.dtype),
            pltpu.VMEM((slots * rows, cols), flat.dtype),
            pltpu.VMEM((n_dp, slots * rows // n_dp, cols), flat.dtype),
            pltpu.SemaphoreType.DMA((7, n_chip)),
            pltpu.SemaphoreType.DMA((7, n_chip)),
        ],
        compiler_params=params(0),
    )(sel, flat)
    return out.reshape(slots, rows, cols)


def gather_blocks(chunks, n_dp, n_chip, count):
    _, chunk, cols = chunks.shape
    piece = chunk // n_chip
    vmem = pl.BlockSpec(memory_space=pltpu.VMEM)
    return pl.pallas_call(
        functools.partial(weight_kernel, n_dp, n_chip),
        out_shape=jax.ShapeDtypeStruct((2 * n_dp * chunk, cols), chunks.dtype),
        in_specs=[vmem],
        out_specs=vmem,
        scratch_shapes=[
            pltpu.VMEM((2, chunk, cols), chunks.dtype),
            pltpu.VMEM((chunk, cols), chunks.dtype),
            pltpu.VMEM((n_chip, piece, cols), chunks.dtype),
            pltpu.SemaphoreType.DMA((5, n_chip)),
            pltpu.SemaphoreType.DMA((5, n_chip)),
        ],
        compiler_params=params(1),
    )(chunks)


def split(a):
    hi = a.astype(jnp.bfloat16)
    lo = (a - hi.astype(jnp.float32)).astype(jnp.bfloat16)
    return hi, lo

def mm3(left, right):
    lh, ll = split(left)
    rh, rl = split(right)
    dot = functools.partial(jnp.dot, preferred_element_type=jnp.float32)
    return dot(lh, rh) + (dot(lh, rl) + dot(ll, rh))

def soap_kernel(scalars, pick, g_ref, m_ref, s_ref, sl_ref, sr_ref, bl_ref, br_ref, w_ref, d_out, l_out, r_out, c_out, u_buf):
    slots = g_ref.shape[0]
    correction = scalars[0]
    chains = []
    for i in range(slots):
        occupied = scalars[1 + i] > 0
        gradient = g_ref[i]
        basis_left = bl_ref[i]
        basis_right = br_ref[i]
        moment_new = 0.95 * m_ref[i] + 0.05 * gradient
        rotated = mm3(basis_left.T, mm3(gradient, basis_right))
        rot_moment = mm3(basis_left.T, mm3(moment_new, basis_right))
        second_new = 0.95 * s_ref[i] + 0.05 * rotated * rotated
        scaled = rot_moment / correction / (jnp.sqrt(second_new / correction) + 1e-08)
        direction = jnp.where(occupied, mm3(basis_left, mm3(scaled, basis_right.T)), 0.0)
        d_out[i] = direction
        master = w_ref[i]
        u_buf[i] = (master - 0.01 * (direction + 0.1 * master)).astype(u_buf.dtype)
        left_stat = 0.95 * sl_ref[i] + 0.05 * mm3(gradient, gradient.T)
        right_stat = 0.95 * sr_ref[i] + 0.05 * mm3(gradient.T, gradient)
        chains.append((left_stat, basis_left, l_out, i, occupied))
        chains.append((right_stat, basis_right, r_out, i, occupied))
    iterates = []
    for stat, basis, out, i, occupied in chains:
        power = mm3(stat, basis)
        magnitude = jnp.sqrt(jnp.sum(power * power, keepdims=True))
        iterates.append(power / (magnitude + 1e-06))
    for repeat_count in range(NS_ITERS):
        grams = [mm3(it.T, it) for it in iterates]
        iterates = [1.5 * it - 0.5 * mm3(it, gram) for it, gram in zip(iterates, grams)]
    for (stat, basis, out, i, occupied), it in zip(chains, iterates):
        out[i] = jnp.where(occupied, it, basis)
    halves, rows = c_out.shape[0], g_ref.shape[1]
    for h in range(halves):
        for k in range(c_out.shape[1] // rows):
            index = pick[h * (c_out.shape[1] // rows) + k]
            value = u_buf[jnp.maximum(index, 0)]
            c_out[h, pl.ds(k * rows, rows), :] = jnp.where(index >= 0, value, jnp.zeros_like(value))


def soap_slots(gradient, occupied, pick, moment, second, stat_left, stat_right, basis_left, basis_right, master, step_count):
    slots, rows, cols = gradient.shape
    elapsed = step_count[0].astype(jnp.float32)
    correction = 1.0 - jnp.power(jnp.float32(0.95), elapsed)
    scalars = jnp.concatenate([correction[None], occupied.astype(jnp.float32)])
    vmem = pl.BlockSpec(memory_space=pltpu.VMEM)
    smem = pl.BlockSpec(memory_space=pltpu.SMEM)
    f32 = jax.ShapeDtypeStruct(gradient.shape, jnp.float32)
    chunks = jax.ShapeDtypeStruct((2, pick.shape[0] // 2 * rows, cols), jnp.bfloat16)
    return pl.pallas_call(
        soap_kernel,
        out_shape=(f32, f32, f32, chunks),
        in_specs=[smem, smem] + [vmem] * 8,
        out_specs=(vmem, vmem, vmem, vmem),
        scratch_shapes=[pltpu.VMEM(gradient.shape, jnp.bfloat16)],
    )(scalars, pick, gradient, moment, second, stat_left, stat_right, basis_left, basis_right, master)


def body(
    partials,
    owners,
    step_count,
    master,
    moment,
    second,
    stat_left,
    stat_right,
    basis_left,
    basis_right,
):
    owner_count = lax.axis_size("owner")
    n_dp = lax.axis_size("dp")
    n_chip = owner_count // 2
    slot_count = master.shape[0]
    total_slot_count = slot_count * owner_count
    target, source, occupied = slot_layout(owners, slot_count, total_slot_count)
    first_slot = lax.axis_index("owner") * slot_count
    occupied_mine = lax.dynamic_slice_in_dim(occupied, first_slot, slot_count, 0)
    source_mine = lax.dynamic_slice_in_dim(source, first_slot, slot_count, 0)
    sel = source_mine[None, :].astype(jnp.int32)
    mask_mine = (occupied_mine > 0).astype(jnp.float32)[:, None, None]
    gradient = owned_gradient(partials[0], sel, n_dp, n_chip).astype(jnp.float32) * mask_mine
    block_count = owners.shape[0]
    count, rows, cols = block_count, master.shape[1], master.shape[2]
    per = count // (2 * n_dp)
    replica = lax.axis_index("dp")
    mine = (jnp.arange(2)[:, None] * (count // 2) + replica * per + jnp.arange(per)[None, :]).reshape(-1)
    rank = jnp.take(target, mine) - first_slot
    pick = jnp.where((rank >= 0) & (rank < slot_count), rank, -1).astype(jnp.int32)
    direction, left_new, right_new, chunks = soap_slots(
        gradient, occupied_mine, pick, moment, second, stat_left, stat_right, basis_left, basis_right, master, step_count
    )
    weights_all = gather_blocks(chunks, n_dp, n_chip, count).reshape(count, rows, cols)
    return (weights_all, direction, left_new, right_new)


def solution(mesh):
    placed = (
        P(("dp", "owner"), None, None, None),
        P(),
        P(),
        P("owner", None, None),
        P("owner", None, None),
        P("owner", None, None),
        P("owner", None, None),
        P("owner", None, None),
        P("owner", None, None),
        P("owner", None, None),
    )
    return jax.shard_map(
        body,
        mesh=mesh,
        in_specs=placed,
        out_specs=(P(), P("owner", None, None), P("owner", None, None), P("owner", None, None)),
        check_vma=False,
    )
```
